512 devices in a mesh: dp: 64 (over z, y_hi, x), ctx: 8 (over y_lo, core).
Axes of the slice: x: 4, y: 8 (y_hi: 2, y_lo: 4; y = y_hi * 4 + y_lo), z: 8, core: 2. Of those that a mesh axis runs over, the one named last changes fastest.
Arguments:
- inputs: bfloat16 [64, 16, 16, 16, 128], P('dp', 'ctx'), may hold values from -90 to 90
- cotangent: bfloat16 [64, 16, 16, 16, 128], P('dp', 'ctx'), may hold values from -18 to 18
- conv_weight: bfloat16 [3, 3, 3, 128, 128], replicated, may hold values from -0.109375 to 0.109375
- norm_gain: float32 [128], replicated, may hold values from 0.1 to 1.9
- norm_bias: float32 [128], replicated, may hold values from -3 to 3
Outputs:
- input_grad: bfloat16 [64, 16, 16, 16, 128], P('dp', 'ctx')
- weight_grad: float32 [3, 3, 3, 128, 128], replicated
- gain_grad: float32 [128], replicated
- bias_grad: float32 [128], replicated
The draws below stay inside these ranges and needn't reach their ends.
All inputs are finite; a program needn't handle non-finite values.
Results may differ from the reference program's by a relative error of at most 0.0027.
Values may be sent and summed in bfloat16 or wider, within the bound.
No kernel may reach another device: no remote copies, remote signals or barrier semaphores. Data moves between devices by JAX's collectives and lax.ppermute only.
A program may use at most 64 MiB of HBM per device.

```python
import math
import jax
import jax.numpy as jnp
from jax import lax

C = 128
GROUPS = 32
SIDE = 16
CLIPS = 64
FRAMES = 16
CELLS = 262144


def frame_rise(key_frames):
    position = jnp.arange(FRAMES, dtype=jnp.float32) / (FRAMES - 1)
    rough = jnp.exp(jax.random.uniform(key_frames, (CLIPS, FRAMES), jnp.float32, -0.35, 0.35))
    return (3.0 ** position)[None, :] * rough


def draw_inputs(key, part):
    keys = jax.random.split(jax.random.fold_in(key, 11), 4)
    shape_all = (CLIPS, FRAMES, SIDE, SIDE, C)
    rising = frame_rise(keys[0])
    channel_scale = jnp.exp(jax.random.uniform(keys[1], (C,), jnp.float32, math.log(0.4), math.log(4.0)))
    offset = jax.random.uniform(keys[2], (C,), jnp.float32, -1.0, 1.0)
    noise = jnp.clip(jax.random.normal(keys[3], shape_all, jnp.float32), -4.0, 4.0)
    values = offset + rising[:, :, None, None, None] * channel_scale * noise
    return values.astype(jnp.bfloat16)


def draw_cotangent(key, part):
    keys = jax.random.split(jax.random.fold_in(key, 23), 3)
    shape_all = (CLIPS, FRAMES, SIDE, SIDE, C)
    rising = frame_rise(keys[0])
    noise = jnp.clip(jax.random.normal(keys[2], shape_all, jnp.float32), -4.0, 4.0)
    values = rising[:, :, None, None, None] * noise
    return values.astype(jnp.bfloat16)


def normal_values(own_key, extent, deviation, bound, kind=jnp.bfloat16):
    drawn = deviation * jax.random.normal(own_key, extent, jnp.float32)
    return jnp.clip(drawn, min=-bound, max=bound).astype(kind)


def setup_inputs(seed: int = 0) -> dict:
    key_list = jax.random.split(jax.random.key(seed), 6)
    return {
        "inputs": draw_inputs(jax.random.fold_in(key_list[5], 71), 0),
        "cotangent": draw_cotangent(jax.random.fold_in(key_list[5], 71), 0),
        "conv_weight": normal_values(key_list[2], (3, 3, 3, C, C), (27 * C) ** -0.5, 0.109375),
        "norm_gain": jnp.clip(1.0 + 0.18 * jax.random.normal(key_list[3], (C,), jnp.float32), 0.1, 1.9),
        "norm_bias": normal_values(key_list[4], (C,), 0.5, 3.0, jnp.float32),
    }


epsilon = 1e-06

def group_average(per_channel, members):
    grouped = per_channel.reshape(GROUPS, -1).sum(axis=1, keepdims=True) / members
    return jnp.broadcast_to(grouped, (GROUPS, per_channel.shape[0] // GROUPS)).reshape(-1)

def kernel_terms(padded_act, grad_flat, frames_n, side_len, channels):
    pieces = []
    for tap_time in range(3):
        for tap_row in range(3):
            columns = jnp.concatenate([padded_act[tap_time:tap_time + frames_n, tap_row:tap_row + side_len, tap_col:tap_col + side_len] for tap_col in range(3)], axis=-1).reshape(-1, 3 * channels)
            pieces.append(lax.dot_general(columns, grad_flat, (((0,), (0,)), ((), ())), preferred_element_type=jnp.float32))
    return jnp.stack(pieces).reshape(3, 3, 3, channels, channels)

def spread_back(grad_ext, weight_turned, frames_out, side_len, channels):
    total_grad = jnp.zeros((frames_out * side_len * side_len, channels), jnp.float32)
    for tap_time in range(3):
        for tap_row in range(3):
            columns = jnp.concatenate([grad_ext[2 - tap_time:2 - tap_time + frames_out, 2 - tap_row:2 - tap_row + side_len, 2 - tap_col:2 - tap_col + side_len] for tap_col in range(3)], axis=-1).reshape(-1, 3 * channels)
            total_grad = total_grad + jnp.dot(columns, weight_turned[tap_time, tap_row].reshape(3 * channels, channels), preferred_element_type=jnp.float32)
    return total_grad.reshape(frames_out, side_len, side_len, channels)

def clip_backward(clip_inputs, clip_grad, conv_weight, norm_gain, norm_bias):
    frames_n, side_len, channels = (clip_inputs.shape[0], clip_inputs.shape[1], clip_inputs.shape[3])
    values = clip_inputs.astype(jnp.float32)
    flat_values = values.reshape(-1, channels)
    members = flat_values.shape[0] * (channels // GROUPS)
    average = group_average(flat_values.sum(axis=0), members)
    centered = flat_values - average
    spread = group_average((centered * centered).sum(axis=0), members)
    inverse_std = lax.rsqrt(spread + epsilon)
    normed = (values - average) * inverse_std
    shifted = normed * norm_gain + norm_bias
    activation = jax.nn.silu(shifted).astype(jnp.bfloat16)
    padded_act = jnp.concatenate([activation[:1], activation[:1], activation], axis=0)
    padded_act = jnp.pad(padded_act, ((0, 0), (1, 1), (1, 1), (0, 0)))
    grad_flat = clip_grad.reshape(-1, channels)
    kernel_sum = kernel_terms(padded_act, grad_flat, frames_n, side_len, channels)
    blank = jnp.zeros((2, side_len, side_len, channels), jnp.bfloat16)
    grad_ext = jnp.concatenate([blank, clip_grad, blank], axis=0)
    grad_ext = jnp.pad(grad_ext, ((0, 0), (1, 1), (1, 1), (0, 0)))
    weight_turned = jnp.transpose(conv_weight, (0, 1, 2, 4, 3))
    pad_grad = spread_back(grad_ext, weight_turned, frames_n + 2, side_len, channels)
    act_grad = pad_grad[2:].at[0].add(pad_grad[0] + pad_grad[1])
    sigmoid_val = jax.nn.sigmoid(shifted)
    pre_grad = act_grad * sigmoid_val * (1.0 + shifted * (1.0 - sigmoid_val))
    normed_grad = pre_grad * norm_gain
    first_mean = group_average(normed_grad.reshape(-1, channels).sum(axis=0), members)
    second_mean = group_average((normed_grad * normed).reshape(-1, channels).sum(axis=0), members)
    input_grad = (inverse_std * (normed_grad - first_mean - normed * second_mean)).astype(jnp.bfloat16)
    gain_part = (pre_grad * normed).reshape(-1, channels).sum(axis=0)
    bias_part = pre_grad.reshape(-1, channels).sum(axis=0)
    return (input_grad, kernel_sum, gain_part, bias_part)

def reference(inputs, cotangent, conv_weight, norm_gain, norm_bias):
    channels = inputs.shape[4]

    def step_clip(carry, pair):
        result = clip_backward(pair[0], pair[1], conv_weight, norm_gain, norm_bias)
        return ((carry[0] + result[1], carry[1] + result[2], carry[2] + result[3]), result[0])
    start = (jnp.zeros((3, 3, 3, channels, channels), jnp.float32), jnp.zeros((channels,), jnp.float32), jnp.zeros((channels,), jnp.float32))
    totals, input_grad = lax.scan(step_clip, start, (inputs, cotangent))
    scale_val = 1.0 / jnp.sqrt(jnp.float32(CELLS))
    return (input_grad, totals[0] * scale_val, totals[1] * scale_val, totals[2] * scale_val)
```

```python
import jax
import jax.numpy as jnp
from jax import lax
from jax.sharding import PartitionSpec as P

GROUPS = 32


epsilon = 1e-06


def from_behind(x, axis, by):
    count = lax.axis_size(axis)
    pairs = [(i, i + by) for i in range(count) if 0 <= i + by < count]
    return lax.ppermute(x, axis, pairs)


def copy_for_each(x, axis):
    count = lax.axis_size(axis)
    return lax.all_to_all(jnp.broadcast_to(x[None], (count, *x.shape)), axis, 0, 0, tiled=True)


def over_copies(x, axis):
    return copy_for_each(x, axis).sum(axis=0)


def packed_total(arrays, axis):
    ends = [0]
    for a in arrays:
        ends.append(ends[-1] + a.size)
    total = over_copies(jnp.concatenate([a.ravel() for a in arrays]), axis)
    return tuple((total[b:e].reshape(a.shape) for a, b, e in zip(arrays, ends, ends[1:])))


CHUNK = 56
PARTS = 32
PLANE = ("z", "x")
COLUMN = ("y_hi", "y_lo")
CTX = ("y_lo", "core")


def high_and_low(x):
    high = lax.reduce_precision(x, 8, 7)
    return jnp.concatenate([high, x - high], axis=0)


def total_over_all(kernel_sum, small):
    core = lax.axis_index("core")
    first, second = kernel_sum[: kernel_sum.shape[0] // 2], kernel_sum[kernel_sum.shape[0] // 2 :]
    swap = [(0, 1), (1, 0)]
    got = lax.ppermute(jnp.where(core == 0, second, first), "core", swap)
    half = jnp.where(core == 0, first, second) + got
    rows = half.shape[0]
    spare = PARTS * CHUNK - rows - 4
    buffer = jnp.concatenate(
        [half, jnp.zeros((spare, 128), jnp.float32), high_and_low(small)], axis=0
    ).astype(jnp.bfloat16)
    mine = lax.all_to_all(buffer.reshape(PARTS, CHUNK, 128), PLANE, 0, 0, tiled=True)
    mine = mine.astype(jnp.float32).sum(axis=0)
    mine = copy_for_each(mine, COLUMN).sum(axis=0)
    last = (lax.axis_index("z") == lax.axis_size("z") - 1) & (
        lax.axis_index("x") == lax.axis_size("x") - 1
    )
    end = high_and_low(mine[CHUNK - 4 : CHUNK - 2] + mine[CHUNK - 2 :])
    mine = jnp.concatenate(
        [mine[: CHUNK - 4], jnp.where(last, end, mine[CHUNK - 4 :])], axis=0
    ).astype(jnp.bfloat16)
    own = copy_for_each(mine, PLANE).reshape(PARTS * CHUNK, 128)
    other = lax.ppermute(own, "core", swap)
    tail = own[-4:].astype(jnp.float32) + other[-4:].astype(jnp.float32)
    tail = tail[:2] + tail[2:]
    whole = jnp.where(
        core == 0,
        jnp.stack([own[:rows], other[:rows]]),
        jnp.stack([other[:rows], own[:rows]]),
    ).astype(jnp.float32)
    return whole, tail[0], tail[1]


def group_average(per_channel, members):
    grouped = per_channel.reshape(GROUPS, -1).sum(axis=1, keepdims=True) / members
    return jnp.broadcast_to(grouped, (GROUPS, per_channel.shape[0] // GROUPS)).reshape(-1)


def kernel_terms(padded_act, grad_flat, frames_n, side_len, channels):
    pieces = []
    for tap_time in range(3):
        for tap_row in range(3):
            columns = jnp.concatenate(
                [
                    padded_act[
                        tap_time : tap_time + frames_n,
                        tap_row : tap_row + side_len,
                        tap_col : tap_col + side_len,
                    ]
                    for tap_col in range(3)
                ],
                axis=-1,
            ).reshape(-1, 3 * channels)
            pieces.append(
                lax.dot_general(
                    columns, grad_flat, (((0,), (0,)), ((), ())), preferred_element_type=jnp.float32
                )
            )
    return jnp.stack(pieces).reshape(3, 3, 3, channels, channels)


def spread_back(grad_ext, weight_turned, frames_out, side_len, channels):
    total_grad = jnp.zeros((frames_out * side_len * side_len, channels), jnp.float32)
    for tap_time in range(3):
        for tap_row in range(3):
            columns = jnp.concatenate(
                [
                    grad_ext[
                        2 - tap_time : 2 - tap_time + frames_out,
                        2 - tap_row : 2 - tap_row + side_len,
                        2 - tap_col : 2 - tap_col + side_len,
                    ]
                    for tap_col in range(3)
                ],
                axis=-1,
            ).reshape(-1, 3 * channels)
            total_grad = total_grad + jnp.dot(
                columns,
                weight_turned[tap_time, tap_row].reshape(3 * channels, channels),
                preferred_element_type=jnp.float32,
            )
    return total_grad.reshape(frames_out, side_len, side_len, channels)


def plane_back(plane, weight_plane, side_len, channels):
    padded = jnp.pad(plane, ((1, 1), (1, 1), (0, 0)))
    total_grad = jnp.zeros((side_len * side_len, channels), jnp.float32)
    for tap_row in range(3):
        columns = jnp.concatenate(
            [
                padded[2 - tap_row : 2 - tap_row + side_len, 2 - tap_col : 2 - tap_col + side_len]
                for tap_col in range(3)
            ],
            axis=-1,
        ).reshape(-1, 3 * channels)
        total_grad = total_grad + jnp.dot(
            columns,
            weight_plane[tap_row].reshape(3 * channels, channels),
            preferred_element_type=jnp.float32,
        )
    return total_grad.reshape(side_len, side_len, channels)


def body(inputs, cotangent, conv_weight, norm_gain, norm_bias):
    frames_n, side_len, channels = (inputs.shape[1], inputs.shape[2], inputs.shape[4])
    ctx_count = lax.axis_size(CTX)
    leading = lax.axis_index(CTX) == 0
    members = frames_n * side_len * side_len * ctx_count * (channels // GROUPS)
    values = inputs[0].astype(jnp.float32)
    flat_values = values.reshape(-1, channels)
    early_frames = from_behind(inputs[0, frames_n - 2 :], CTX, 1)
    totals, squares = packed_total(
        (flat_values.sum(axis=0), (flat_values * flat_values).sum(axis=0)), CTX
    )
    average = group_average(totals, members)
    spread = group_average(squares, members) - average * average
    inverse_std = lax.rsqrt(spread + epsilon)

    def normalize(frames_in):
        normed_val = (frames_in - average) * inverse_std
        shifted_val = normed_val * norm_gain + norm_bias
        return (normed_val, shifted_val, jax.nn.silu(shifted_val).astype(jnp.bfloat16))

    normed, shifted, activation = normalize(values)
    prior = normalize(early_frames.astype(jnp.float32))[2]
    prior = jnp.where(leading, jnp.broadcast_to(activation[:1], prior.shape), prior)
    padded_act = jnp.concatenate([prior, activation], axis=0)
    padded_act = jnp.pad(padded_act, ((0, 0), (1, 1), (1, 1), (0, 0)))
    grad_local = cotangent[0]
    after_frames = from_behind(grad_local, CTX, -1)
    kernel_sum = kernel_terms(
        padded_act, grad_local.reshape(-1, channels), frames_n, side_len, channels
    )
    grad_ext = jnp.concatenate([grad_local, after_frames], axis=0)
    grad_ext = jnp.pad(grad_ext, ((0, 0), (1, 1), (1, 1), (0, 0)))
    weight_turned = jnp.transpose(conv_weight, (0, 1, 2, 4, 3))
    pad_grad = spread_back(grad_ext, weight_turned, frames_n, side_len, channels)

    def fold_terms():
        first_part = plane_back(grad_local[0], weight_turned[0], side_len, channels)
        second_part = plane_back(grad_local[1], weight_turned[0], side_len, channels)
        third_part = plane_back(grad_local[0], weight_turned[1], side_len, channels)
        return first_part + (second_part + third_part)

    def fold_empty():
        return jnp.zeros((side_len, side_len, channels), jnp.float32)

    folded = lax.cond(leading, fold_terms, fold_empty)
    act_grad = pad_grad.at[0].add(folded)
    sigmoid_val = jax.nn.sigmoid(shifted)
    pre_grad = act_grad * sigmoid_val * (1.0 + shifted * (1.0 - sigmoid_val))
    normed_grad = pre_grad * norm_gain
    gain_part = (pre_grad * normed).reshape(-1, channels).sum(axis=0)
    bias_part = pre_grad.reshape(-1, channels).sum(axis=0)
    bias_clip, gain_clip = packed_total((bias_part, gain_part), CTX)
    first_mean = group_average(bias_clip * norm_gain, members)
    second_mean = group_average(gain_clip * norm_gain, members)
    input_grad = (inverse_std * (normed_grad - first_mean - normed * second_mean)).astype(
        jnp.bfloat16
    )[None]
    kernel_all, gain_all, bias_all = total_over_all(
        kernel_sum.reshape(-1, channels), jnp.stack([gain_part, bias_part])
    )
    kernel_all = kernel_all.reshape(kernel_sum.shape)
    cell_total = 64 * ctx_count * frames_n * side_len * side_len
    scale_val = 1.0 / jnp.sqrt(jnp.float32(cell_total))
    return (input_grad, kernel_all * scale_val, gain_all * scale_val, bias_all * scale_val)


def solution(mesh):
    fine = jax.sharding.Mesh(
        mesh.devices.reshape(8, 2, 4, 4, 2), ("z", "y_hi", "x", "y_lo", "core")
    )
    whole = P(("z", "y_hi", "x"), CTX, None, None, None)
    return jax.shard_map(
        body,
        mesh=fine,
        in_specs=(whole, whole, P(), P(), P()),
        out_specs=(whole, P(), P(), P()),
        check_vma=False,
    )
```

```python
import functools

import jax
import jax.numpy as jnp
from jax import lax
from jax.experimental import pallas as pl
from jax.experimental.pallas import tpu as pltpu
from jax.sharding import PartitionSpec as P

GROUPS = 32
CHANNELS = 128
SIDE = 16
FRAMES = 2
ROWS = FRAMES * SIDE * SIDE
EPSILON = 1e-06
PAIRS = 5
OWNED = PAIRS * 3 * CHANNELS
CHUNK = 32
PARTS = 64
SMALL_PART = OWNED // CHUNK

DP = ("z", "y_hi", "x")
CTX = ("y_lo", "core")
CELLS = 64 * 8 * ROWS
MEMBERS = 8 * ROWS * (CHANNELS // GROUPS)
SCALE = CELLS**-0.5

f32 = jnp.float32
bf16 = jnp.bfloat16


def call(kernel, outs, scratch=(), flops=0, bytes_accessed=0, transcendentals=0):
    return pl.pallas_call(
        kernel,
        out_shape=[jax.ShapeDtypeStruct(s, d) for s, d in outs],
        out_specs=[pl.BlockSpec(memory_space=pltpu.VMEM) for _ in outs],
        scratch_shapes=list(scratch),
        compiler_params=pltpu.CompilerParams(vmem_limit_bytes=32 << 20),
        cost_estimate=pl.CostEstimate(
            flops=flops, bytes_accessed=bytes_accessed, transcendentals=transcendentals
        ),
    )


def column(rows):
    return lax.broadcasted_iota(jnp.int32, (rows, CHANNELS), 0) % SIDE


def next_column(x):
    return jnp.where(column(x.shape[0]) == SIDE - 1, 0.0, pltpu.roll(x, x.shape[0] - 1, 0))


def last_column(x):
    return jnp.where(column(x.shape[0]) == 0, 0.0, pltpu.roll(x, 1, 0))


def group_mean(x):
    place = lax.broadcasted_iota(jnp.int32, x.shape, 1) % (CHANNELS // GROUPS)
    total = x
    for d in range(1, CHANNELS // GROUPS):
        total = total + jnp.where(place >= d, pltpu.roll(x, d, 1), 0.0)
        total = total + jnp.where(
            place < CHANNELS // GROUPS - d, pltpu.roll(x, CHANNELS - d, 1), 0.0
        )
    return total / MEMBERS


def fill_padded(pad_ref, first, second):
    blank = jnp.zeros((2 * FRAMES, 1, SIDE, CHANNELS), bf16)
    pad_ref[:, 0:1] = blank
    pad_ref[:, SIDE + 1 : SIDE + 2] = blank
    pad_ref[0:FRAMES, 1 : SIDE + 1] = first
    pad_ref[FRAMES : 2 * FRAMES, 1 : SIDE + 1] = second


def data_grad_kernel(cot_ref, after_ref, weight_ref, out_ref, pad_ref, wide_ref):
    fill_padded(pad_ref, cot_ref[...], after_ref[...])

    def slab(frame, count):
        return jnp.concatenate(
            [
                pad_ref[frame : frame + count, 2 - b : 2 - b + SIDE].reshape(-1, CHANNELS)
                for b in range(3)
            ],
            axis=1,
        )

    def taps(a):
        return jnp.concatenate(
            [weight_ref[a, b].reshape(3 * CHANNELS, CHANNELS) for b in range(3)], axis=1
        )

    def product(x, w):
        return lax.dot_general(x, w, (((1,), (1,)), ((), ())), preferred_element_type=f32)

    wide_ref[...] = (
        product(slab(2, FRAMES), taps(0))
        + product(slab(1, FRAMES), taps(1))
        + product(slab(0, FRAMES), taps(2))
    )

    @pl.when((lax.axis_index("y_lo") == 0) & (lax.axis_index("core") == 0))
    def _():
        plane = SIDE * SIDE
        wide_ref[0:plane] = wide_ref[0:plane] + (
            product(slab(0, 1), taps(0)) + (product(slab(1, 1), taps(0)) + product(slab(0, 1), taps(1)))
        )

    out_ref[...] = (
        next_column(wide_ref[:, 0:CHANNELS])
        + wide_ref[:, CHANNELS : 2 * CHANNELS]
        + last_column(wide_ref[:, 2 * CHANNELS :])
    )


def pair_products(start, act_ref, cot_ref, out_ref):
    for j in range(PAIRS):
        q = jnp.minimum(start + j, 8)
        a, b = q // 3, q % 3
        x = act_ref[pl.ds(a, FRAMES), pl.ds(b, SIDE)].reshape(ROWS, CHANNELS)
        y = lax.dot_general(x, cot_ref[...], (((0,), (0,)), ((), ())), preferred_element_type=f32)
        for c in range(3):
            at = (j * 3 + c) * CHANNELS
            out_ref[at : at + CHANNELS] = y[:, c * CHANNELS : (c + 1) * CHANNELS]


def other_taps_kernel(
    x_ref, prior_ref, cot_ref, stats_ref, gain_ref, bias_ref, out_ref, act_ref, wide_ref, norm_ref
):
    sums = jnp.sum(stats_ref[...], axis=0)
    both = jnp.concatenate(
        [sums[:, 0:CHANNELS], sums[:, CHANNELS:], jnp.zeros((6, CHANNELS), f32)], axis=0
    )
    means = group_mean(both)
    average = means[0:1]
    spread = means[1:2] - average * average
    inverse_std = lax.rsqrt(spread + EPSILON)
    norm_ref[...] = jnp.concatenate([average, inverse_std, jnp.zeros((6, CHANNELS), f32)], axis=0)

    def activation(x):
        values = x.reshape(-1, CHANNELS).astype(f32)
        shifted = (values - average) * inverse_std * gain_ref[...] + bias_ref[...]
        return (shifted / (1.0 + jnp.exp(-shifted))).astype(bf16).reshape(x.shape)

    act = activation(x_ref[...])
    leading = (lax.axis_index("y_lo") == 0) & (lax.axis_index("core") == 0)
    fill_padded(act_ref, activation(prior_ref[...]), act)

    @pl.when(leading)
    def _():
        act_ref[0:1, 1 : SIDE + 1] = act[0:1]
        act_ref[1:2, 1 : SIDE + 1] = act[0:1]

    cot = cot_ref[...].reshape(ROWS, CHANNELS)
    cot32 = cot.astype(f32)
    wide_ref[:, 0:CHANNELS] = next_column(cot32).astype(bf16)
    wide_ref[:, CHANNELS : 2 * CHANNELS] = cot
    wide_ref[:, 2 * CHANNELS :] = last_column(cot32).astype(bf16)
    pair_products(
        jnp.where(lax.axis_index("core") == 0, PAIRS, 0), act_ref, wide_ref, out_ref
    )


def own_taps_kernel(
    x_ref, act_ref, wide_ref, norm_ref, grad_ref, gain_ref, bias_ref, out_ref, pre_ref, small_ref
):
    pair_products(
        jnp.where(lax.axis_index("core") == 0, 0, PAIRS), act_ref, wide_ref, out_ref
    )
    normed = (x_ref[...].reshape(ROWS, CHANNELS).astype(f32) - norm_ref[0:1]) * norm_ref[1:2]
    shifted = normed * gain_ref[...] + bias_ref[...]
    sig = 1.0 / (1.0 + jnp.exp(-shifted))
    pre = grad_ref[...] * sig * (1.0 + shifted * (1.0 - sig))
    pre_ref[...] = pre
    small_ref[...] = jnp.concatenate(
        [
            jnp.sum(pre * normed, axis=0, keepdims=True),
            jnp.sum(pre, axis=0, keepdims=True),
            jnp.zeros((6, CHANNELS), f32),
        ],
        axis=0,
    )


def high_and_low(x):
    high = x.astype(bf16).astype(f32)
    return jnp.concatenate([high, x - high], axis=0)


def fill_kernel(own_ref, got_ref, small_ref, out_ref):
    out_ref[0:OWNED] = (own_ref[...] + got_ref[...]).astype(bf16)
    out_ref[OWNED : OWNED + 16] = jnp.concatenate(
        [high_and_low(small_ref[0:2]), jnp.zeros((12, CHANNELS), f32)], axis=0
    ).astype(bf16)
    rest = PARTS * CHUNK - OWNED - 16
    out_ref[OWNED + 16 :] = jnp.zeros((rest, CHANNELS), bf16)


def sum_kernel(parts_ref, small_ref, other_ref, out_ref):
    total = parts_ref[0].astype(f32)
    for i in range(1, PARTS):
        total = total + parts_ref[i].astype(f32)
    out_ref[0:CHUNK] = total
    out_ref[CHUNK : CHUNK + 8] = small_ref[...] + other_ref[...]


def spread_kernel(one_ref, two_ref, out_ref, clip_ref):
    total = one_ref[...] + two_ref[...]
    clip_ref[...] = total[CHUNK:]
    place = (lax.axis_index("z") * 2 + lax.axis_index("y_hi")) * 4 + lax.axis_index("x")
    small = high_and_low(total[0:2] + total[2:4])
    with_small = jnp.concatenate([small, total[4:CHUNK]], axis=0)
    mine = jnp.where(place == SMALL_PART, with_small, total[0:CHUNK]).astype(bf16)
    out_ref[...] = jnp.broadcast_to(mine[None], (PARTS, CHUNK, CHANNELS))


def input_grad_kernel(x_ref, pre_ref, norm_ref, clip_ref, gain_ref, out_ref):
    means = group_mean(clip_ref[...] * gain_ref[...])
    normed = (x_ref[...].reshape(ROWS, CHANNELS).astype(f32) - norm_ref[0:1]) * norm_ref[1:2]
    grad = norm_ref[1:2] * (pre_ref[...] * gain_ref[...] - means[1:2] - normed * means[0:1])
    out_ref[...] = grad.astype(bf16).reshape(x_ref.shape)


def final_kernel(own_ref, other_ref, weight_ref, small_ref):
    core = lax.axis_index("core")

    def put(first_ref, second_ref):
        weight_ref[0:OWNED] = first_ref[0:OWNED].astype(f32) * SCALE
        rest = 27 * CHANNELS - OWNED
        weight_ref[OWNED:] = second_ref[0:rest].astype(f32) * SCALE

    @pl.when(core == 0)
    def _():
        put(own_ref, other_ref)

    @pl.when(core == 1)
    def _():
        put(other_ref, own_ref)

    both = own_ref[OWNED : OWNED + 16].astype(f32) + other_ref[OWNED : OWNED + 16].astype(f32)
    small_ref[...] = (both[0:8] + pltpu.roll(both[0:8], 6, 0)) * SCALE


def body(inputs, cotangent, conv_weight, norm_gain, norm_bias):
    x, cot = inputs[0], cotangent[0]
    gain, bias = norm_gain[None], norm_bias[None]
    swap = [(0, 1), (1, 0)]

    flat = x.astype(f32).reshape(-1, CHANNELS)
    sums = jnp.concatenate([flat.sum(axis=0), (flat * flat).sum(axis=0)])
    stats = lax.all_to_all(jnp.broadcast_to(sums, (8, 1, 2 * CHANNELS)), CTX, 0, 0, tiled=True)
    after = lax.ppermute(cot, CTX, [(i + 1, i) for i in range(7)])
    prior = lax.ppermute(x, CTX, [(i, i + 1) for i in range(7)])

    (act_grad,) = call(
        data_grad_kernel,
        [((ROWS, CHANNELS), f32)],
        [pltpu.VMEM((4, SIDE + 2, SIDE, CHANNELS), bf16), pltpu.VMEM((ROWS, 3 * CHANNELS), f32)],
        flops=2 * ROWS * 27 * CHANNELS * CHANNELS,
        bytes_accessed=2 << 20,
    )(cot, after, conv_weight)
    others, act, wide, norm = call(
        other_taps_kernel,
        [
            ((OWNED, CHANNELS), f32),
            ((4, SIDE + 2, SIDE, CHANNELS), bf16),
            ((ROWS, 3 * CHANNELS), bf16),
            ((8, CHANNELS), f32),
        ],
        flops=2 * ROWS * OWNED * CHANNELS,
        bytes_accessed=2 << 20,
    )(x, prior, cot, stats, gain, bias)
    got = lax.ppermute(others, "core", swap)
    owns, pre, small = call(
        own_taps_kernel,
        [((OWNED, CHANNELS), f32), ((ROWS, CHANNELS), f32), ((8, CHANNELS), f32)],
        flops=2 * ROWS * OWNED * CHANNELS,
        bytes_accessed=2 << 20,
    )(x, act, wide, norm, act_grad, gain, bias)
    (buffer,) = call(fill_kernel, [((PARTS * CHUNK, CHANNELS), bf16)], bytes_accessed=3 << 20)(
        owns, got, small
    )
    other_small = lax.ppermute(small, "core", swap)
    parts = lax.all_to_all(buffer.reshape(PARTS, CHUNK, CHANNELS), DP, 0, 0, tiled=True)
    (one,) = call(sum_kernel, [((CHUNK + 8, CHANNELS), f32)], bytes_accessed=1 << 19)(
        parts, small, other_small
    )
    one = one + lax.ppermute(one, "y_lo", [(i, i ^ 1) for i in range(4)])
    two = lax.ppermute(one, "y_lo", [(i, i ^ 2) for i in range(4)])
    spread, clip = call(
        spread_kernel,
        [((PARTS, CHUNK, CHANNELS), bf16), ((8, CHANNELS), f32)],
        bytes_accessed=1 << 19,
    )(one, two)
    own_total = lax.all_to_all(spread, DP, 0, 0, tiled=True).reshape(PARTS * CHUNK, CHANNELS)
    (input_grad,) = call(input_grad_kernel, [(x.shape, bf16)], bytes_accessed=1 << 19)(
        x, pre, norm, clip, gain
    )
    other_total = lax.ppermute(own_total, "core", swap)
    weight_grad, tail = call(
        final_kernel,
        [((27 * CHANNELS, CHANNELS), f32), ((8, CHANNELS), f32)],
        bytes_accessed=3 << 20,
    )(own_total, other_total)
    return (
        input_grad[None],
        weight_grad.reshape(3, 3, 3, CHANNELS, CHANNELS),
        tail[0],
        tail[1],
    )


def solution(mesh):
    fine = jax.sharding.Mesh(
        mesh.devices.reshape(8, 2, 4, 4, 2), ("z", "y_hi", "x", "y_lo", "core")
    )
    whole = P(DP, CTX, None, None, None)
    return jax.shard_map(
        body,
        mesh=fine,
        in_specs=(whole, whole, P(), P(), P()),
        out_specs=(whole, P(), P(), P()),
        check_vma=False,
    )
```

```python
import functools

import jax
import jax.numpy as jnp
from jax import lax
from jax.experimental import pallas as pl
from jax.experimental.pallas import tpu as pltpu
from jax.sharding import PartitionSpec as P

GROUPS = 32
CHANNELS = 128
SIDE = 16
FRAMES = 2
ROWS = FRAMES * SIDE * SIDE
EPSILON = 1e-06
TAPS = 14
OWNED = TAPS * CHANNELS
PARTS = 32
CHUNK = OWNED // PARTS

ALL = ("z", "y_hi", "x", "y_lo", "core")
DP = ("z", "y_hi", "x")
CTX = ("y_lo", "core")
CELLS = 64 * 8 * ROWS
MEMBERS = 8 * ROWS * (CHANNELS // GROUPS)
SCALE = CELLS**-0.5

f32 = jnp.float32
bf16 = jnp.bfloat16


def index(z, y, x, core):
    return ((z * 2 + y // 4) * 4 + x) * 8 + (y % 4) * 2 + core


EXCHANGE = [[index(z, y, x, 0) for z in range(8) for x in range(4)] for y in range(8)] + [
    [index(z, y, x, 1) for y in range(8) for x in range(4)] for z in range(8)
]


def across(bit):
    pairs = []
    for z in range(8):
        for y in range(8):
            for x in range(4):
                pairs.append((index(z, y, x, 0), index(z, y ^ bit, x, 0)))
                pairs.append((index(z, y, x, 1), index(z ^ bit, y, x, 1)))
    return pairs


def call(kernel, ins, outs, scratch=(), flops=0, bytes_accessed=0):
    return pl.pallas_call(
        kernel,
        out_shape=[jax.ShapeDtypeStruct(s, d) for s, d in outs],
        in_specs=[pl.BlockSpec(memory_space=pl.ANY if i else pltpu.VMEM) for i in ins],
        out_specs=[pl.BlockSpec(memory_space=pltpu.VMEM) for _ in outs],
        scratch_shapes=list(scratch),
        compiler_params=pltpu.CompilerParams(vmem_limit_bytes=32 << 20),
        cost_estimate=pl.CostEstimate(
            flops=flops, bytes_accessed=bytes_accessed, transcendentals=0
        ),
    )


def column(rows):
    return lax.broadcasted_iota(jnp.int32, (rows, CHANNELS), 0) % SIDE


def next_column(x):
    return jnp.where(column(x.shape[0]) == SIDE - 1, 0.0, pltpu.roll(x, x.shape[0] - 1, 0))


def last_column(x):
    return jnp.where(column(x.shape[0]) == 0, 0.0, pltpu.roll(x, 1, 0))


def group_mean(x):
    place = lax.broadcasted_iota(jnp.int32, x.shape, 1) % (CHANNELS // GROUPS)
    total = x
    for d in range(1, CHANNELS // GROUPS):
        total = total + jnp.where(place >= d, pltpu.roll(x, d, 1), 0.0)
        total = total + jnp.where(
            place < CHANNELS // GROUPS - d, pltpu.roll(x, CHANNELS - d, 1), 0.0
        )
    return total / MEMBERS


def first_chip():
    return lax.axis_index("y_lo") == 0


def load_kernel(
    x_hbm, cot_hbm, gain_hbm, bias_hbm, both_ref, mixed_ref, stats_ref, gain_ref, bias_ref, sems
):
    copies = [
        pltpu.make_async_copy(src, dst, sems.at[i])
        for i, (src, dst) in enumerate(
            [
                (x_hbm, both_ref.at[0:FRAMES]),
                (cot_hbm, both_ref.at[FRAMES:]),
                (gain_hbm, gain_ref),
                (bias_hbm, bias_ref),
            ]
        )
    ]
    for copy in copies:
        copy.start()
    copies[0].wait()
    values = both_ref[0:FRAMES].reshape(ROWS, CHANNELS).astype(f32)
    sums = jnp.concatenate(
        [
            jnp.sum(values, axis=0, keepdims=True),
            jnp.sum(values * values, axis=0, keepdims=True),
            jnp.zeros((6, CHANNELS), f32),
        ],
        axis=0,
    )
    stats_ref[...] = jnp.broadcast_to(sums[None], stats_ref.shape)
    for copy in copies[1:]:
        copy.wait()
    core = lax.axis_index("core")

    @pl.when(core == 0)
    def _():
        mixed_ref[...] = both_ref[FRAMES:]

    @pl.when(core == 1)
    def _():
        mixed_ref[...] = both_ref[0:FRAMES]


def blank_edges(pad_ref):
    blank = jnp.zeros((pad_ref.shape[0], 1, SIDE, CHANNELS), bf16)
    pad_ref[:, 0:1] = blank
    pad_ref[:, SIDE + 1 : SIDE + 2] = blank


def taps_kernel(
    both_ref, partner_ref, mixed_ref, far_ref, stats_ref, gain_ref, bias_ref,
    out_ref, norm_ref, act_ref, wide_ref,
):
    core = lax.axis_index("core")
    means = group_mean(jnp.sum(stats_ref[...], axis=0))
    average = means[0:1]
    spread = means[1:2] - average * average
    inverse_std = lax.rsqrt(spread + EPSILON)
    norm_ref[...] = jnp.concatenate([average, inverse_std, jnp.zeros((6, CHANNELS), f32)], axis=0)

    def activation(x):
        values = x.reshape(-1, CHANNELS).astype(f32)
        shifted = (values - average) * inverse_std * gain_ref[...] + bias_ref[...]
        return (shifted / (1.0 + jnp.exp(-shifted))).astype(bf16).reshape(x.shape)

    inside = slice(1, SIDE + 1)
    blank_edges(act_ref)
    act_ref[pl.ds(FRAMES + FRAMES * core, FRAMES), inside] = activation(both_ref[0:FRAMES])
    act_ref[pl.ds(2 * FRAMES - FRAMES * core, FRAMES), inside] = activation(
        partner_ref[0:FRAMES]
    )

    @pl.when(first_chip())
    def _():
        act_ref[0:1, inside] = act_ref[2:3, inside]
        act_ref[1:2, inside] = act_ref[2:3, inside]

    @pl.when(jnp.logical_not(first_chip()) & (core == 0))
    def _():
        act_ref[0:FRAMES, inside] = activation(mixed_ref[...])

    @pl.when(jnp.logical_not(first_chip()) & (core == 1))
    def _():
        act_ref[0:FRAMES, inside] = activation(far_ref[...])

    for source, at in ((both_ref, core), (partner_ref, 1 - core)):
        rows = pl.ds(pl.multiple_of(at * ROWS, ROWS), ROWS)
        cot = source[FRAMES:].reshape(ROWS, CHANNELS)
        cot32 = cot.astype(f32)
        wide_ref[rows, 0:CHANNELS] = next_column(cot32).astype(bf16)
        wide_ref[rows, CHANNELS : 2 * CHANNELS] = cot
        wide_ref[rows, 2 * CHANNELS :] = last_column(cot32).astype(bf16)

    for j in range(5):
        q = 4 * core + j
        a, b = q // 3, q % 3
        x = act_ref[pl.ds(a, 2 * FRAMES), pl.ds(b, SIDE)].reshape(2 * ROWS, CHANNELS)
        y = lax.dot_general(
            x, wide_ref[...], (((0,), (0,)), ((), ())), preferred_element_type=f32
        ).astype(bf16)
        for c in range(3):
            value = y[:, c * CHANNELS : (c + 1) * CHANNELS]
            at = j * 3 + c

            def put(value=value, at=at):
                rows = pl.ds(pl.multiple_of((at - 2 * core) * CHANNELS, CHANNELS), CHANNELS)
                out_ref[rows] = value

            if at < 2:
                pl.when(core == 0)(put)
            elif at >= TAPS:
                pl.when(core == 1)(put)
            else:
                put()

    @pl.when(core == 1)
    def _():
        out_ref[OWNED - CHANNELS :] = jnp.zeros((CHANNELS, CHANNELS), bf16)


def data_grad_kernel(
    both_ref, partner_ref, mixed_ref, norm_ref, gain_ref, bias_ref, weight_hbm,
    pre_ref, small_ref, pad_ref, wide_ref, weight_ref, sem,
):
    load = pltpu.make_async_copy(weight_hbm, weight_ref, sem)
    load.start()
    core = lax.axis_index("core")
    inside = slice(1, SIDE + 1)
    blank_edges(pad_ref)
    pad_ref[0:FRAMES, inside] = both_ref[FRAMES:]

    @pl.when(core == 0)
    def _():
        pad_ref[FRAMES:, inside] = partner_ref[FRAMES:]

    @pl.when(core == 1)
    def _():
        pad_ref[FRAMES:, inside] = mixed_ref[...]

    def slab(frame, count):
        return jnp.concatenate(
            [
                pad_ref[frame : frame + count, 2 - b : 2 - b + SIDE].reshape(-1, CHANNELS)
                for b in range(3)
            ],
            axis=1,
        )

    def taps(a):
        return jnp.concatenate(
            [weight_ref[a, b].reshape(3 * CHANNELS, CHANNELS) for b in range(3)], axis=1
        )

    def product(x, w):
        return lax.dot_general(x, w, (((1,), (1,)), ((), ())), preferred_element_type=f32)

    load.wait()
    wide_ref[...] = (
        product(slab(2, FRAMES), taps(0))
        + product(slab(1, FRAMES), taps(1))
        + product(slab(0, FRAMES), taps(2))
    )

    @pl.when(first_chip() & (core == 0))
    def _():
        plane = SIDE * SIDE
        wide_ref[0:plane] = wide_ref[0:plane] + (
            product(slab(0, 1), taps(0))
            + (product(slab(1, 1), taps(0)) + product(slab(0, 1), taps(1)))
        )

    act_grad = (
        next_column(wide_ref[:, 0:CHANNELS])
        + wide_ref[:, CHANNELS : 2 * CHANNELS]
        + last_column(wide_ref[:, 2 * CHANNELS :])
    )
    values = both_ref[0:FRAMES].reshape(ROWS, CHANNELS).astype(f32)
    normed = (values - norm_ref[0:1]) * norm_ref[1:2]
    shifted = normed * gain_ref[...] + bias_ref[...]
    sig = 1.0 / (1.0 + jnp.exp(-shifted))
    pre = act_grad * sig * (1.0 + shifted * (1.0 - sig))
    pre_ref[...] = pre
    small_ref[...] = jnp.concatenate(
        [
            jnp.sum(pre * normed, axis=0, keepdims=True),
            jnp.sum(pre, axis=0, keepdims=True),
            jnp.zeros((6, CHANNELS), f32),
        ],
        axis=0,
    )


def sum_kernel(parts_ref, small_ref, other_ref, out_ref):
    total = parts_ref[0].astype(f32)
    for i in range(1, PARTS):
        total = total + parts_ref[i].astype(f32)
    out_ref[0:CHUNK] = total
    out_ref[CHUNK:] = small_ref[...] + other_ref[...]


def spread_kernel(one_ref, two_ref, out_ref, clip_ref):
    total = one_ref[...] + two_ref[...]
    clip_ref[...] = one_ref[CHUNK:]
    small = total[CHUNK : CHUNK + 2]
    high = small.astype(bf16).astype(f32)
    mine = jnp.concatenate(
        [total[0:CHUNK], high, small - high, jnp.zeros((4, CHANNELS), f32)], axis=0
    ).astype(bf16)
    out_ref[...] = jnp.broadcast_to(mine[None], out_ref.shape)


def input_grad_kernel(both_ref, pre_ref, norm_ref, clip_ref, other_ref, gain_ref, out_ref):
    clip = jnp.where(lax.axis_index("core") == 0, clip_ref[...], other_ref[...])
    means = group_mean(clip * gain_ref[...])
    values = both_ref[0:FRAMES].reshape(ROWS, CHANNELS).astype(f32)
    normed = (values - norm_ref[0:1]) * norm_ref[1:2]
    grad = norm_ref[1:2] * (pre_ref[...] * gain_ref[...] - means[1:2] - normed * means[0:1])
    out_ref[...] = grad.astype(bf16).reshape(out_ref.shape)


def final_kernel(own_ref, other_ref, weight_ref, gain_ref, bias_ref):
    core = lax.axis_index("core")
    end = 27 * CHANNELS

    def put(first_ref, second_ref):
        for m in range(PARTS):
            weight_ref[m * CHUNK : (m + 1) * CHUNK] = first_ref[m, 0:CHUNK].astype(f32) * SCALE
            at = OWNED + m * CHUNK
            rows = min(CHUNK, end - at)
            if rows > 0:
                weight_ref[at : at + rows] = second_ref[m, 0:rows].astype(f32) * SCALE
        small = first_ref[0, CHUNK:].astype(f32)
        for m in range(1, PARTS):
            small = small + first_ref[m, CHUNK:].astype(f32)
        gain_ref[...] = (small[0:1] + small[2:3]) * SCALE
        bias_ref[...] = (small[1:2] + small[3:4]) * SCALE

    @pl.when(core == 0)
    def _():
        put(own_ref, other_ref)

    @pl.when(core == 1)
    def _():
        put(other_ref, own_ref)


def exchange(x):
    return lax.all_to_all(x, ALL, 0, 0, axis_index_groups=EXCHANGE, tiled=True)


def body(inputs, cotangent, conv_weight, norm_gain, norm_bias):
    x, cot = inputs[0], cotangent[0]
    swap = [(0, 1), (1, 0)]
    frames = (FRAMES, SIDE, SIDE, CHANNELS)
    one_row = ((1, CHANNELS), f32)

    both, mixed, stats, gain, bias = call(
        load_kernel,
        [1, 1, 1, 1],
        [((2 * FRAMES, SIDE, SIDE, CHANNELS), bf16), (frames, bf16), ((8, 8, CHANNELS), f32),
         one_row, one_row],
        [pltpu.SemaphoreType.DMA((4,))],
        bytes_accessed=1 << 18,
    )(x, cot, norm_gain[None], norm_bias[None])
    stats = lax.all_to_all(stats, CTX, 0, 0, tiled=True)
    partner = lax.ppermute(both, "core", swap)
    mixed = lax.ppermute(
        mixed, CTX, [(1, 2), (3, 4), (5, 6), (2, 1), (4, 3), (6, 5)]
    )
    far = lax.ppermute(both[0:FRAMES], CTX, [(1, 3), (3, 5), (5, 7)])

    buffer, norm = call(
        taps_kernel,
        [0] * 7,
        [((OWNED, CHANNELS), bf16), ((8, CHANNELS), f32)],
        [
            pltpu.VMEM((3 * FRAMES, SIDE + 2, SIDE, CHANNELS), bf16),
            pltpu.VMEM((2 * ROWS, 3 * CHANNELS), bf16),
        ],
        flops=4 * ROWS * 15 * CHANNELS * CHANNELS,
        bytes_accessed=1 << 20,
    )(both, partner, mixed, far, stats, gain, bias)
    parts = exchange(buffer.reshape(PARTS, CHUNK, CHANNELS))
    pre, small = call(
        data_grad_kernel,
        [0] * 6 + [1],
        [((ROWS, CHANNELS), f32), ((8, CHANNELS), f32)],
        [
            pltpu.VMEM((2 * FRAMES, SIDE + 2, SIDE, CHANNELS), bf16),
            pltpu.VMEM((ROWS, 3 * CHANNELS), f32),
            pltpu.VMEM((3, 3, 3, CHANNELS, CHANNELS), bf16),
            pltpu.SemaphoreType.DMA,
        ],
        flops=2 * ROWS * 27 * CHANNELS * CHANNELS,
        bytes_accessed=2 << 20,
    )(both, partner, mixed, norm, gain, bias, conv_weight)
    other_small = lax.ppermute(small, "core", swap)
    (one,) = call(sum_kernel, [0] * 3, [((CHUNK + 8, CHANNELS), f32)], bytes_accessed=1 << 19)(
        parts, small, other_small
    )
    one = one + lax.ppermute(one, ALL, across(1))
    one = one + lax.ppermute(one, ALL, across(2))
    two = lax.ppermute(one, ALL, across(4))
    spread, clip = call(
        spread_kernel,
        [0] * 2,
        [((PARTS, CHUNK + 8, CHANNELS), bf16), ((8, CHANNELS), f32)],
        bytes_accessed=1 << 19,
    )(one, two)
    own_total = exchange(spread)
    other_clip = lax.ppermute(clip, "core", [(0, 1)])
    (input_grad,) = call(input_grad_kernel, [0] * 6, [(frames, bf16)], bytes_accessed=1 << 19)(
        both, pre, norm, clip, other_clip, gain
    )
    other_total = lax.ppermute(own_total, "core", swap)
    weight_grad, gain_grad, bias_grad = call(
        final_kernel,
        [0] * 2,
        [((27 * CHANNELS, CHANNELS), f32), one_row, one_row],
        bytes_accessed=3 << 20,
    )(own_total, other_total)
    return (
        input_grad[None],
        weight_grad.reshape(3, 3, 3, CHANNELS, CHANNELS),
        gain_grad[0],
        bias_grad[0],
    )


def solution(mesh):
    fine = jax.sharding.Mesh(
        mesh.devices.reshape(8, 2, 4, 4, 2), ("z", "y_hi", "x", "y_lo", "core")
    )
    whole = P(DP, CTX, None, None, None)
    return jax.shard_map(
        body,
        mesh=fine,
        in_specs=(whole, whole, P(), P(), P()),
        out_specs=(whole, P(), P(), P()),
        check_vma=False,
    )
```

```python
import functools

import jax
import jax.numpy as jnp
from jax import lax
from jax.experimental import pallas as pl
from jax.experimental.pallas import tpu as pltpu
from jax.sharding import PartitionSpec as P

GROUPS = 32
CHANNELS = 128
SIDE = 16
FRAMES = 2
ROWS = FRAMES * SIDE * SIDE
EPSILON = 1e-06
TAPS = 14
OWNED = TAPS * CHANNELS
PARTS = 32
CHUNK = OWNED // PARTS

ALL = ("z", "y_hi", "x", "y_lo", "core")
DP = ("z", "y_hi", "x")
CTX = ("y_lo", "core")
CELLS = 64 * 8 * ROWS
MEMBERS = 8 * ROWS * (CHANNELS // GROUPS)
SCALE = CELLS**-0.5

f32 = jnp.float32
bf16 = jnp.bfloat16


def index(z, y, x, core):
    return ((z * 2 + y // 4) * 4 + x) * 8 + (y % 4) * 2 + core


EXCHANGE = [[index(z, y, x, 0) for z in range(8) for x in range(4)] for y in range(8)] + [
    [index(z, y, x, 1) for y in range(8) for x in range(4)] for z in range(8)
]


COLUMN = [[index(z, y, x, 0) for y in range(8)] for z in range(8) for x in range(4)] + [
    [index(z, y, x, 1) for z in range(8)] for y in range(8) for x in range(4)
]


def call(kernel, ins, outs, scratch=(), flops=0, bytes_accessed=0, vmem=32):
    return pl.pallas_call(
        kernel,
        out_shape=[jax.ShapeDtypeStruct(s, d) for s, d in outs],
        in_specs=[pl.BlockSpec(memory_space=pltpu.HBM if i else pltpu.VMEM) for i in ins],
        out_specs=[pl.BlockSpec(memory_space=pltpu.VMEM) for _ in outs],
        scratch_shapes=list(scratch),
        compiler_params=pltpu.CompilerParams(vmem_limit_bytes=vmem << 20),
        cost_estimate=pl.CostEstimate(
            flops=flops, bytes_accessed=bytes_accessed, transcendentals=0
        ),
    )


def column(rows):
    return lax.broadcasted_iota(jnp.int32, (rows, CHANNELS), 0) % SIDE


def next_column(x):
    return jnp.where(column(x.shape[0]) == SIDE - 1, 0.0, pltpu.roll(x, x.shape[0] - 1, 0))


def last_column(x):
    return jnp.where(column(x.shape[0]) == 0, 0.0, pltpu.roll(x, 1, 0))


def group_mean(x):
    place = lax.broadcasted_iota(jnp.int32, x.shape, 1) % (CHANNELS // GROUPS)
    total = x
    for d in range(1, CHANNELS // GROUPS):
        total = total + jnp.where(place >= d, pltpu.roll(x, d, 1), 0.0)
        total = total + jnp.where(
            place < CHANNELS // GROUPS - d, pltpu.roll(x, CHANNELS - d, 1), 0.0
        )
    return total / MEMBERS


def first_chip():
    return lax.axis_index("y_lo") == 0


def load_kernel(
    x_hbm, cot_hbm, both_ref, mixed_ref, far_ref, stats_ref, sems,
):
    copies = [
        pltpu.make_async_copy(src, dst, sems.at[i])
        for i, (src, dst) in enumerate(
            [
                (x_hbm, both_ref.at[0:FRAMES]),
                (cot_hbm, both_ref.at[FRAMES:]),
            ]
        )
    ]
    for copy in copies:
        copy.start()
    copies[0].wait()
    values = both_ref[0:FRAMES].reshape(ROWS, CHANNELS).astype(f32)
    sums = jnp.concatenate(
        [
            jnp.sum(values, axis=0, keepdims=True),
            jnp.sum(values * values, axis=0, keepdims=True),
            jnp.zeros((6, CHANNELS), f32),
        ],
        axis=0,
    )
    stats_ref[...] = jnp.broadcast_to(sums[None], stats_ref.shape)
    for copy in copies[1:]:
        copy.wait()
    far_ref[...] = both_ref[0:FRAMES]
    core = lax.axis_index("core")

    @pl.when(core == 0)
    def _():
        mixed_ref[...] = both_ref[FRAMES:]

    @pl.when(core == 1)
    def _():
        mixed_ref[...] = both_ref[0:FRAMES]


def gather_kernel(
    both_ref, partner_ref, mixed_ref, far_ref, gain_ref, bias_ref,
    frames_ref, wide_ref, gain_out, bias_out,
):
    core = lax.axis_index("core")
    for source, at in ((both_ref, core), (partner_ref, 1 - core)):
        frames_ref[pl.ds(FRAMES + FRAMES * at, FRAMES)] = source[0:FRAMES]
        rows = pl.ds(pl.multiple_of(at * ROWS, ROWS), ROWS)
        cot = source[FRAMES:].reshape(ROWS, CHANNELS)
        cot32 = cot.astype(f32)
        wide_ref[rows, 0:CHANNELS] = next_column(cot32).astype(bf16)
        wide_ref[rows, CHANNELS : 2 * CHANNELS] = cot
        wide_ref[rows, 2 * CHANNELS :] = last_column(cot32).astype(bf16)
    gain_out[...] = gain_ref[...]
    bias_out[...] = bias_ref[...]
    later = jnp.logical_not(first_chip())

    @pl.when(first_chip())
    def _():
        frames_ref[0] = frames_ref[FRAMES]
        frames_ref[1] = frames_ref[FRAMES]

    @pl.when(later & (core == 0))
    def _():
        frames_ref[0:FRAMES] = mixed_ref[...]

    @pl.when(later & (core == 1))
    def _():
        frames_ref[0:FRAMES] = far_ref[...]


def blank_edges(pad_ref):
    blank = jnp.zeros((pad_ref.shape[0], 1, SIDE, CHANNELS), bf16)
    pad_ref[:, 0:1] = blank
    pad_ref[:, SIDE + 1 : SIDE + 2] = blank


def taps_kernel(
    frames_ref, wide_ref, stats_ref, gain_ref, bias_ref, out_ref, norm_ref, act_ref
):
    core = lax.axis_index("core")
    means = group_mean(jnp.sum(stats_ref[...], axis=0))
    average = means[0:1]
    spread = means[1:2] - average * average
    inverse_std = lax.rsqrt(spread + EPSILON)
    norm_ref[...] = jnp.concatenate([average, inverse_std, jnp.zeros((6, CHANNELS), f32)], axis=0)

    blank_edges(act_ref)
    for at in range(0, 3 * FRAMES, FRAMES):
        values = frames_ref[at : at + FRAMES].reshape(ROWS, CHANNELS).astype(f32)
        shifted = (values - average) * inverse_std * gain_ref[...] + bias_ref[...]
        act = (shifted / (1.0 + jnp.exp(-shifted))).astype(bf16)
        act_ref[at : at + FRAMES, 1 : SIDE + 1] = act.reshape(FRAMES, SIDE, SIDE, CHANNELS)

    for j in range(5):
        q = 4 * core + j
        a, b = q // 3, q % 3
        x = act_ref[pl.ds(a, 2 * FRAMES), pl.ds(b, SIDE)].reshape(2 * ROWS, CHANNELS)
        y = lax.dot_general(
            x, wide_ref[...], (((0,), (0,)), ((), ())), preferred_element_type=f32
        ).astype(bf16)
        for c in range(3):
            value = y[:, c * CHANNELS : (c + 1) * CHANNELS]
            at = j * 3 + c

            def put(value=value, at=at):
                rows = pl.ds(pl.multiple_of((at - 2 * core) * CHANNELS, CHANNELS), CHANNELS)
                out_ref[rows] = value

            if at < 2:
                pl.when(core == 0)(put)
            elif at >= TAPS:
                pl.when(core == 1)(put)
            else:
                put()

    @pl.when(core == 1)
    def _():
        out_ref[OWNED - CHANNELS :] = jnp.zeros((CHANNELS, CHANNELS), bf16)


def data_grad_kernel(
    both_ref, partner_ref, mixed_ref, norm_ref, gain_ref, bias_ref, weight_hbm,
    pre_ref, small_ref, pad_ref, wide_ref, weight_ref, sem,
):
    load = pltpu.make_async_copy(weight_hbm, weight_ref, sem)
    load.start()
    core = lax.axis_index("core")
    inside = slice(1, SIDE + 1)
    blank_edges(pad_ref)
    pad_ref[0:FRAMES, inside] = both_ref[FRAMES:]

    @pl.when(core == 0)
    def _():
        pad_ref[FRAMES:, inside] = partner_ref[FRAMES:]

    @pl.when(core == 1)
    def _():
        pad_ref[FRAMES:, inside] = mixed_ref[...]

    def slab(frame, count):
        return jnp.concatenate(
            [
                pad_ref[frame : frame + count, 2 - b : 2 - b + SIDE].reshape(-1, CHANNELS)
                for b in range(3)
            ],
            axis=1,
        )

    def taps(a):
        return jnp.concatenate(
            [weight_ref[a, b].reshape(3 * CHANNELS, CHANNELS) for b in range(3)], axis=1
        )

    def product(x, w):
        return lax.dot_general(x, w, (((1,), (1,)), ((), ())), preferred_element_type=f32)

    load.wait()
    wide_ref[...] = (
        product(slab(2, FRAMES), taps(0))
        + product(slab(1, FRAMES), taps(1))
        + product(slab(0, FRAMES), taps(2))
    )

    @pl.when(first_chip() & (core == 0))
    def _():
        plane = SIDE * SIDE
        wide_ref[0:plane] = wide_ref[0:plane] + (
            product(slab(0, 1), taps(0))
            + (product(slab(1, 1), taps(0)) + product(slab(0, 1), taps(1)))
        )

    act_grad = (
        next_column(wide_ref[:, 0:CHANNELS])
        + wide_ref[:, CHANNELS : 2 * CHANNELS]
        + last_column(wide_ref[:, 2 * CHANNELS :])
    )
    values = both_ref[0:FRAMES].reshape(ROWS, CHANNELS).astype(f32)
    normed = (values - norm_ref[0:1]) * norm_ref[1:2]
    shifted = normed * gain_ref[...] + bias_ref[...]
    sig = 1.0 / (1.0 + jnp.exp(-shifted))
    pre = act_grad * sig * (1.0 + shifted * (1.0 - sig))
    pre_ref[...] = pre
    small_ref[...] = jnp.concatenate(
        [
            jnp.sum(pre * normed, axis=0, keepdims=True),
            jnp.sum(pre, axis=0, keepdims=True),
            jnp.zeros((6, CHANNELS), f32),
        ],
        axis=0,
    )


def sum_kernel(parts_ref, small_ref, other_ref, out_ref):
    total = parts_ref[0].astype(f32)
    for i in range(1, PARTS):
        total = total + parts_ref[i].astype(f32)
    total = jnp.concatenate([total, small_ref[...] + other_ref[...]], axis=0)
    out_ref[...] = jnp.broadcast_to(total[None], out_ref.shape)


def spread_kernel(parts_ref, out_ref, clip_ref):
    total = jnp.sum(parts_ref[...], axis=0)
    clip_ref[...] = jnp.sum(parts_ref[pl.ds(4 * lax.axis_index("y_hi"), 4), CHUNK:], axis=0)
    small = total[CHUNK : CHUNK + 2]
    high = small.astype(bf16).astype(f32)
    mine = jnp.concatenate(
        [total[0:CHUNK], high, small - high, jnp.zeros((4, CHANNELS), f32)], axis=0
    ).astype(bf16)
    out_ref[...] = jnp.broadcast_to(mine[None], out_ref.shape)


def input_grad_kernel(both_ref, pre_ref, norm_ref, clip_ref, other_ref, gain_ref, out_ref):
    clip = jnp.where(lax.axis_index("core") == 0, clip_ref[...], other_ref[...])
    means = group_mean(clip * gain_ref[...])
    values = both_ref[0:FRAMES].reshape(ROWS, CHANNELS).astype(f32)
    normed = (values - norm_ref[0:1]) * norm_ref[1:2]
    grad = norm_ref[1:2] * (pre_ref[...] * gain_ref[...] - means[1:2] - normed * means[0:1])
    out_ref[...] = grad.astype(bf16).reshape(out_ref.shape)


def final_kernel(own_ref, other_ref, weight_ref, gain_ref, bias_ref):
    core = lax.axis_index("core")
    end = 27 * CHANNELS

    def put(first_ref, second_ref):
        for m in range(PARTS):
            weight_ref[m * CHUNK : (m + 1) * CHUNK] = first_ref[m, 0:CHUNK].astype(f32) * SCALE
            at = OWNED + m * CHUNK
            rows = min(CHUNK, end - at)
            if rows > 0:
                weight_ref[at : at + rows] = second_ref[m, 0:rows].astype(f32) * SCALE
        small = first_ref[0, CHUNK:].astype(f32)
        for m in range(1, PARTS):
            small = small + first_ref[m, CHUNK:].astype(f32)
        gain_ref[...] = (small[0:1] + small[2:3]) * SCALE
        bias_ref[...] = (small[1:2] + small[3:4]) * SCALE

    @pl.when(core == 0)
    def _():
        put(own_ref, other_ref)

    @pl.when(core == 1)
    def _():
        put(other_ref, own_ref)


def exchange(x, groups):
    return lax.all_to_all(x, ALL, 0, 0, axis_index_groups=groups, tiled=True)


def body(inputs, cotangent, conv_weight, norm_gain, norm_bias):
    x, cot = inputs[0], cotangent[0]
    swap = [(0, 1), (1, 0)]
    frames = (FRAMES, SIDE, SIDE, CHANNELS)
    one_row = ((1, CHANNELS), f32)

    both, mixed, far, stats = call(
        load_kernel,
        [1, 1],
        [((2 * FRAMES, SIDE, SIDE, CHANNELS), bf16), (frames, bf16), (frames, bf16),
         ((8, 8, CHANNELS), f32)],
        [pltpu.SemaphoreType.DMA((2,))],
        bytes_accessed=1 << 18,
        vmem=60,
    )(x, cot)
    stats = lax.all_to_all(stats, CTX, 0, 0, tiled=True)
    partner = lax.ppermute(both, "core", swap)
    mixed = lax.ppermute(
        mixed, CTX, [(1, 2), (3, 4), (5, 6), (2, 1), (4, 3), (6, 5)]
    )
    far = lax.ppermute(far, CTX, [(1, 3), (3, 5), (5, 7)])

    six, wide, gain, bias = call(
        gather_kernel,
        [0] * 6,
        [((3 * FRAMES, SIDE, SIDE, CHANNELS), bf16), ((2 * ROWS, 3 * CHANNELS), bf16),
         one_row, one_row],
        bytes_accessed=2 << 20,
    )(both, partner, mixed, far, norm_gain[None], norm_bias[None])
    buffer, norm = call(
        taps_kernel,
        [0] * 5,
        [((OWNED, CHANNELS), bf16), ((8, CHANNELS), f32)],
        [pltpu.VMEM((3 * FRAMES, SIDE + 2, SIDE, CHANNELS), bf16)],
        flops=4 * ROWS * 15 * CHANNELS * CHANNELS,
        bytes_accessed=1 << 20,
    )(six, wide, stats, gain, bias)
    parts = exchange(buffer.reshape(PARTS, CHUNK, CHANNELS), EXCHANGE)
    pre, small = call(
        data_grad_kernel,
        [0] * 6 + [1],
        [((ROWS, CHANNELS), f32), ((8, CHANNELS), f32)],
        [
            pltpu.VMEM((2 * FRAMES, SIDE + 2, SIDE, CHANNELS), bf16),
            pltpu.VMEM((ROWS, 3 * CHANNELS), f32),
            pltpu.VMEM((3, 3, 3, CHANNELS, CHANNELS), bf16),
            pltpu.SemaphoreType.DMA,
        ],
        flops=2 * ROWS * 27 * CHANNELS * CHANNELS,
        bytes_accessed=2 << 20,
    )(both, partner, mixed, norm, gain, bias, conv_weight)
    other_small = lax.ppermute(small, "core", swap)
    (one,) = call(sum_kernel, [0] * 3, [((8, CHUNK + 8, CHANNELS), f32)], bytes_accessed=1 << 19)(
        parts, small, other_small
    )
    spread, clip = call(
        spread_kernel,
        [0],
        [((PARTS, CHUNK + 8, CHANNELS), bf16), ((8, CHANNELS), f32)],
        bytes_accessed=1 << 19,
    )(exchange(one, COLUMN))
    own_total = exchange(spread, EXCHANGE)
    other_clip = lax.ppermute(clip, "core", [(0, 1)])
    (input_grad,) = call(input_grad_kernel, [0] * 6, [(frames, bf16)], bytes_accessed=1 << 19)(
        both, pre, norm, clip, other_clip, gain
    )
    own_total, input_grad = lax.optimization_barrier((own_total, input_grad))
    other_total = lax.ppermute(own_total, "core", swap)
    weight_grad, gain_grad, bias_grad = call(
        final_kernel,
        [0] * 2,
        [((27 * CHANNELS, CHANNELS), f32), one_row, one_row],
        bytes_accessed=3 << 20,
    )(own_total, other_total)
    return (
        input_grad[None],
        weight_grad.reshape(3, 3, 3, CHANNELS, CHANNELS),
        gain_grad[0],
        bias_grad[0],
    )


def solution(mesh):
    fine = jax.sharding.Mesh(
        mesh.devices.reshape(8, 2, 4, 4, 2), ("z", "y_hi", "x", "y_lo", "core")
    )
    whole = P(DP, CTX, None, None, None)
    return jax.shard_map(
        body,
        mesh=fine,
        in_specs=(whole, whole, P(), P(), P()),
        out_specs=(whole, P(), P(), P()),
        check_vma=False,
    )
```

```python
import functools

import jax
import jax.numpy as jnp
from jax import lax
from jax.experimental import pallas as pl
from jax.experimental.pallas import tpu as pltpu
from jax.sharding import PartitionSpec as P

GROUPS = 32
CHANNELS = 128
SIDE = 16
FRAMES = 2
ROWS = FRAMES * SIDE * SIDE
EPSILON = 1e-06
TAPS = 14
OWNED = TAPS * CHANNELS
PARTS = 32
CHUNK = OWNED // PARTS

ALL = ("z", "y_hi", "x", "y_lo", "core")
DP = ("z", "y_hi", "x")
CTX = ("y_lo", "core")
CELLS = 64 * 8 * ROWS
MEMBERS = 8 * ROWS * (CHANNELS // GROUPS)
SCALE = CELLS**-0.5

f32 = jnp.float32
bf16 = jnp.bfloat16


def index(z, y, x, core):
    return ((z * 2 + y // 4) * 4 + x) * 8 + (y % 4) * 2 + core


EXCHANGE = [[index(z, y, x, 0) for z in range(8) for x in range(4)] for y in range(8)] + [
    [index(z, y, x, 1) for y in range(8) for x in range(4)] for z in range(8)
]


COLUMN = [[index(z, y, x, 0) for y in range(8)] for z in range(8) for x in range(4)] + [
    [index(z, y, x, 1) for z in range(8)] for y in range(8) for x in range(4)
]


def call(
    kernel, ins, outs, scratch=(), flops=0, bytes_accessed=0, vmem=32, far_outs=(), aliases=None
):
    return pl.pallas_call(
        kernel,
        out_shape=[jax.ShapeDtypeStruct(s, d) for s, d in outs],
        in_specs=[pl.BlockSpec(memory_space=pltpu.HBM if i else pltpu.VMEM) for i in ins],
        out_specs=[
            pl.BlockSpec(memory_space=pltpu.HBM if i in far_outs else pltpu.VMEM)
            for i in range(len(outs))
        ],
        input_output_aliases=aliases or {},
        scratch_shapes=list(scratch),
        compiler_params=pltpu.CompilerParams(vmem_limit_bytes=vmem << 20),
        cost_estimate=pl.CostEstimate(
            flops=flops, bytes_accessed=bytes_accessed, transcendentals=0
        ),
    )


def column(rows):
    return lax.broadcasted_iota(jnp.int32, (rows, CHANNELS), 0) % SIDE


def next_column(x):
    return jnp.where(column(x.shape[0]) == SIDE - 1, 0.0, pltpu.roll(x, x.shape[0] - 1, 0))


def last_column(x):
    return jnp.where(column(x.shape[0]) == 0, 0.0, pltpu.roll(x, 1, 0))


def group_mean(x):
    place = lax.broadcasted_iota(jnp.int32, x.shape, 1) % (CHANNELS // GROUPS)
    total = x
    for d in range(1, CHANNELS // GROUPS):
        total = total + jnp.where(place >= d, pltpu.roll(x, d, 1), 0.0)
        total = total + jnp.where(
            place < CHANNELS // GROUPS - d, pltpu.roll(x, CHANNELS - d, 1), 0.0
        )
    return total / MEMBERS


def first_chip():
    return lax.axis_index("y_lo") == 0


def load_kernel(
    x_hbm, cot_hbm, both_ref, mixed_ref, stats_ref, sems
):
    copies = [
        pltpu.make_async_copy(src, dst, sems.at[i])
        for i, (src, dst) in enumerate(
            [
                (x_hbm, both_ref.at[0:FRAMES]),
                (cot_hbm, both_ref.at[FRAMES:]),
            ]
        )
    ]
    for copy in copies:
        copy.start()
    copies[0].wait()
    values = both_ref[0:FRAMES].reshape(ROWS, CHANNELS).astype(f32)
    sums = jnp.concatenate(
        [
            jnp.sum(values, axis=0, keepdims=True),
            jnp.sum(values * values, axis=0, keepdims=True),
            jnp.zeros((6, CHANNELS), f32),
        ],
        axis=0,
    )
    stats_ref[...] = jnp.broadcast_to(sums[None], stats_ref.shape)
    for copy in copies[1:]:
        copy.wait()
    core = lax.axis_index("core")

    @pl.when(core == 0)
    def _():
        mixed_ref[...] = both_ref[FRAMES:]

    @pl.when(core == 1)
    def _():
        mixed_ref[...] = both_ref[0:FRAMES]


def gather_kernel(
    both_ref, partner_ref, mixed_ref, gain_ref, bias_ref,
    frames_ref, wide_ref, gain_out, bias_out,
):
    core = lax.axis_index("core")

    def put_columns(cot, start):
        cot = cot.reshape(-1, CHANNELS)
        rows = pl.ds(pl.multiple_of(start, SIDE * SIDE), cot.shape[0])
        cot32 = cot.astype(f32)
        wide_ref[rows, 0:CHANNELS] = next_column(cot32).astype(bf16)
        wide_ref[rows, CHANNELS : 2 * CHANNELS] = cot
        wide_ref[rows, 2 * CHANNELS :] = last_column(cot32).astype(bf16)

    for source, at in ((both_ref, core), (partner_ref, 1 - core)):
        frames_ref[pl.ds(FRAMES + FRAMES * at, FRAMES)] = source[0:FRAMES]
        put_columns(source[FRAMES:], at * ROWS)
    gain_out[...] = gain_ref[...]
    bias_out[...] = bias_ref[...]

    @pl.when(core == 0)
    def _():
        wide_ref[2 * ROWS :] = jnp.zeros((SIDE * SIDE, 3 * CHANNELS), bf16)

    @pl.when(core == 1)
    def _():
        put_columns(mixed_ref[0:1], 2 * ROWS)

    inner = jnp.logical_not(first_chip()) & (core == 0)

    @pl.when(inner)
    def _():
        frames_ref[0:FRAMES] = mixed_ref[...]

    @pl.when(jnp.logical_not(inner))
    def _():
        frames_ref[0] = frames_ref[FRAMES]
        frames_ref[1] = frames_ref[FRAMES]


def blank_edges(pad_ref):
    blank = jnp.zeros((pad_ref.shape[0], 1, SIDE, CHANNELS), bf16)
    pad_ref[:, 0:1] = blank
    pad_ref[:, SIDE + 1 : SIDE + 2] = blank


def taps_kernel(
    frames_ref, wide_ref, stats_ref, gain_ref, bias_ref, out_ref, norm_ref, act_ref
):
    core = lax.axis_index("core")
    means = group_mean(jnp.sum(stats_ref[...], axis=0))
    average = means[0:1]
    spread = means[1:2] - average * average
    inverse_std = lax.rsqrt(spread + EPSILON)
    norm_ref[...] = jnp.concatenate([average, inverse_std, jnp.zeros((6, CHANNELS), f32)], axis=0)

    blank_edges(act_ref)
    for at in range(0, 3 * FRAMES, FRAMES):
        values = frames_ref[at : at + FRAMES].reshape(ROWS, CHANNELS).astype(f32)
        shifted = (values - average) * inverse_std * gain_ref[...] + bias_ref[...]
        act = (shifted / (1.0 + jnp.exp(-shifted))).astype(bf16)
        act_ref[at : at + FRAMES, 1 : SIDE + 1] = act.reshape(FRAMES, SIDE, SIDE, CHANNELS)

    act_ref[3 * FRAMES] = jnp.zeros((SIDE + 2, SIDE, CHANNELS), bf16)

    @pl.when(jnp.logical_not(first_chip()) & (core == 1))
    def _():
        act_ref[0:FRAMES, 1 : SIDE + 1] = jnp.zeros((FRAMES, SIDE, SIDE, CHANNELS), bf16)

    for j in range(5):
        q = 4 * core + j
        a, b = q // 3, q % 3
        x = act_ref[pl.ds(a, 5), pl.ds(b, SIDE)].reshape(5 * SIDE * SIDE, CHANNELS)
        y = lax.dot_general(
            x, wide_ref[...], (((0,), (0,)), ((), ())), preferred_element_type=f32
        ).astype(bf16)
        for c in range(3):
            value = y[:, c * CHANNELS : (c + 1) * CHANNELS]
            at = j * 3 + c

            def put(value=value, at=at):
                rows = pl.ds(pl.multiple_of((at - 2 * core) * CHANNELS, CHANNELS), CHANNELS)
                out_ref[rows] = value

            if at < 2:
                pl.when(core == 0)(put)
            elif at >= TAPS:
                pl.when(core == 1)(put)
            else:
                put()

    @pl.when(core == 1)
    def _():
        out_ref[OWNED - CHANNELS :] = jnp.zeros((CHANNELS, CHANNELS), bf16)


def data_grad_kernel(
    both_ref, partner_ref, mixed_ref, norm_ref, gain_ref, bias_ref, weight_hbm,
    pre_ref, small_ref, pad_ref, wide_ref, weight_ref, sem,
):
    load = pltpu.make_async_copy(weight_hbm, weight_ref, sem)
    load.start()
    core = lax.axis_index("core")
    inside = slice(1, SIDE + 1)
    blank_edges(pad_ref)
    pad_ref[0:FRAMES, inside] = both_ref[FRAMES:]

    @pl.when(core == 0)
    def _():
        pad_ref[FRAMES:, inside] = partner_ref[FRAMES:]

    @pl.when(core == 1)
    def _():
        pad_ref[FRAMES:, inside] = mixed_ref[...]

    def slab(frame, count):
        return jnp.concatenate(
            [
                pad_ref[frame : frame + count, 2 - b : 2 - b + SIDE].reshape(-1, CHANNELS)
                for b in range(3)
            ],
            axis=1,
        )

    def taps(a):
        return jnp.concatenate(
            [weight_ref[a, b].reshape(3 * CHANNELS, CHANNELS) for b in range(3)], axis=1
        )

    def product(x, w):
        return lax.dot_general(x, w, (((1,), (1,)), ((), ())), preferred_element_type=f32)

    load.wait()
    wide_ref[...] = (
        product(slab(2, FRAMES), taps(0))
        + product(slab(1, FRAMES), taps(1))
        + product(slab(0, FRAMES), taps(2))
    )

    @pl.when(first_chip() & (core == 0))
    def _():
        plane = SIDE * SIDE
        wide_ref[0:plane] = wide_ref[0:plane] + (
            product(slab(0, 1), taps(0))
            + (product(slab(1, 1), taps(0)) + product(slab(0, 1), taps(1)))
        )

    act_grad = (
        next_column(wide_ref[:, 0:CHANNELS])
        + wide_ref[:, CHANNELS : 2 * CHANNELS]
        + last_column(wide_ref[:, 2 * CHANNELS :])
    )
    values = both_ref[0:FRAMES].reshape(ROWS, CHANNELS).astype(f32)
    normed = (values - norm_ref[0:1]) * norm_ref[1:2]
    shifted = normed * gain_ref[...] + bias_ref[...]
    sig = 1.0 / (1.0 + jnp.exp(-shifted))
    pre = act_grad * sig * (1.0 + shifted * (1.0 - sig))
    pre_ref[...] = pre
    small_ref[...] = jnp.concatenate(
        [
            jnp.sum(pre * normed, axis=0, keepdims=True),
            jnp.sum(pre, axis=0, keepdims=True),
            jnp.zeros((6, CHANNELS), f32),
        ],
        axis=0,
    )


def sum_kernel(parts_ref, small_ref, other_ref, out_ref):
    total = parts_ref[0].astype(f32)
    for i in range(1, PARTS):
        total = total + parts_ref[i].astype(f32)
    total = jnp.concatenate([total, small_ref[...] + other_ref[...]], axis=0)
    out_ref[...] = jnp.broadcast_to(total[None], out_ref.shape)


def spread_kernel(parts_ref, out_ref, clip_ref):
    total = jnp.sum(parts_ref[...], axis=0)
    clip_ref[...] = jnp.sum(parts_ref[pl.ds(4 * lax.axis_index("y_hi"), 4), CHUNK:], axis=0)
    small = total[CHUNK : CHUNK + 2]
    high = small.astype(bf16).astype(f32)
    mine = jnp.concatenate(
        [total[0:CHUNK], high, small - high, jnp.zeros((4, CHANNELS), f32)], axis=0
    ).astype(bf16)
    out_ref[...] = jnp.broadcast_to(mine[None], out_ref.shape)


def input_grad_kernel(both_ref, pre_ref, norm_ref, clip_ref, other_ref, gain_ref, out_ref):
    clip = jnp.where(lax.axis_index("core") == 0, clip_ref[...], other_ref[...])
    means = group_mean(clip * gain_ref[...])
    values = both_ref[0:FRAMES].reshape(ROWS, CHANNELS).astype(f32)
    normed = (values - norm_ref[0:1]) * norm_ref[1:2]
    grad = norm_ref[1:2] * (pre_ref[...] * gain_ref[...] - means[1:2] - normed * means[0:1])
    out_ref[...] = grad.astype(bf16).reshape(out_ref.shape)


def write_half(core, total_ref, weight_hbm, half_ref, sem):
    half_ref[...] = total_ref[:, 0:CHUNK].astype(f32).reshape(OWNED, CHANNELS) * SCALE
    rest = 27 * CHANNELS - OWNED

    @pl.when(core == 0)
    def _():
        copy = pltpu.make_async_copy(half_ref, weight_hbm.at[0:OWNED], sem)
        copy.start()
        copy.wait()

    @pl.when(core == 1)
    def _():
        copy = pltpu.make_async_copy(half_ref.at[0:rest], weight_hbm.at[OWNED:], sem)
        copy.start()
        copy.wait()


def final_own_kernel(own_ref, weight_hbm, half_ref, sem):
    write_half(lax.axis_index("core"), own_ref, weight_hbm, half_ref, sem)


def final_other_kernel(
    own_ref, other_ref, started_hbm, weight_hbm, gain_ref, bias_ref, half_ref, sem
):
    core = lax.axis_index("core")

    def put_small(ref):
        small = ref[0, CHUNK:].astype(f32)
        for m in range(1, PARTS):
            small = small + ref[m, CHUNK:].astype(f32)
        gain_ref[...] = (small[0:1] + small[2:3]) * SCALE
        bias_ref[...] = (small[1:2] + small[3:4]) * SCALE

    @pl.when(core == 0)
    def _():
        put_small(own_ref)

    @pl.when(core == 1)
    def _():
        put_small(other_ref)

    write_half(1 - core, other_ref, weight_hbm, half_ref, sem)


def exchange(x, groups):
    return lax.all_to_all(x, ALL, 0, 0, axis_index_groups=groups, tiled=True)


def body(inputs, cotangent, conv_weight, norm_gain, norm_bias):
    x, cot = inputs[0], cotangent[0]
    swap = [(0, 1), (1, 0)]
    frames = (FRAMES, SIDE, SIDE, CHANNELS)
    one_row = ((1, CHANNELS), f32)

    both, mixed, stats = call(
        load_kernel,
        [1, 1],
        [((2 * FRAMES, SIDE, SIDE, CHANNELS), bf16), (frames, bf16), ((8, 8, CHANNELS), f32)],
        [pltpu.SemaphoreType.DMA((2,))],
        bytes_accessed=1 << 18,
        vmem=60,
    )(x, cot)
    stats = lax.all_to_all(stats, CTX, 0, 0, tiled=True)
    partner = lax.ppermute(both, "core", swap)
    mixed = lax.ppermute(
        mixed, CTX, [(1, 2), (3, 4), (5, 6), (2, 1), (4, 3), (6, 5)]
    )
    six, wide, gain, bias = call(
        gather_kernel,
        [0] * 5,
        [((3 * FRAMES, SIDE, SIDE, CHANNELS), bf16), ((5 * SIDE * SIDE, 3 * CHANNELS), bf16),
         one_row, one_row],
        bytes_accessed=2 << 20,
    )(both, partner, mixed, norm_gain[None], norm_bias[None])
    buffer, norm = call(
        taps_kernel,
        [0] * 5,
        [((OWNED, CHANNELS), bf16), ((8, CHANNELS), f32)],
        [pltpu.VMEM((3 * FRAMES + 1, SIDE + 2, SIDE, CHANNELS), bf16)],
        flops=4 * ROWS * 15 * CHANNELS * CHANNELS,
        bytes_accessed=1 << 20,
    )(six, wide, stats, gain, bias)
    parts = exchange(buffer.reshape(PARTS, CHUNK, CHANNELS), EXCHANGE)
    pre, small = call(
        data_grad_kernel,
        [0] * 6 + [1],
        [((ROWS, CHANNELS), f32), ((8, CHANNELS), f32)],
        [
            pltpu.VMEM((2 * FRAMES, SIDE + 2, SIDE, CHANNELS), bf16),
            pltpu.VMEM((ROWS, 3 * CHANNELS), f32),
            pltpu.VMEM((3, 3, 3, CHANNELS, CHANNELS), bf16),
            pltpu.SemaphoreType.DMA,
        ],
        flops=2 * ROWS * 27 * CHANNELS * CHANNELS,
        bytes_accessed=2 << 20,
    )(both, partner, mixed, norm, gain, bias, conv_weight)
    other_small = lax.ppermute(small, "core", swap)
    (one,) = call(sum_kernel, [0] * 3, [((8, CHUNK + 8, CHANNELS), f32)], bytes_accessed=1 << 19)(
        parts, small, other_small
    )
    spread, clip = call(
        spread_kernel,
        [0],
        [((PARTS, CHUNK + 8, CHANNELS), bf16), ((8, CHANNELS), f32)],
        bytes_accessed=1 << 19,
    )(exchange(one, COLUMN))
    own_total = exchange(spread, EXCHANGE)
    other_clip = lax.ppermute(clip, "core", [(0, 1)])
    (input_grad,) = call(input_grad_kernel, [0] * 6, [(frames, bf16)], bytes_accessed=1 << 19)(
        both, pre, norm, clip, other_clip, gain
    )
    own_total, input_grad = lax.optimization_barrier((own_total, input_grad))
    other_total = lax.ppermute(own_total, "core", swap)
    scratch = [pltpu.VMEM((OWNED, CHANNELS), f32), pltpu.SemaphoreType.DMA]
    (started,) = call(
        final_own_kernel,
        [0],
        [((27 * CHANNELS, CHANNELS), f32)],
        scratch,
        bytes_accessed=2 << 20,
        far_outs=(0,),
    )(own_total)
    weight_grad, gain_grad, bias_grad = call(
        final_other_kernel,
        [0, 0, 1],
        [((27 * CHANNELS, CHANNELS), f32), one_row, one_row],
        scratch,
        bytes_accessed=2 << 20,
        far_outs=(0,),
        aliases={2: 0},
    )(own_total, other_total, started)
    return (
        input_grad[None],
        weight_grad.reshape(3, 3, 3, CHANNELS, CHANNELS),
        gain_grad[0],
        bias_grad[0],
    )


def solution(mesh):
    fine = jax.sharding.Mesh(
        mesh.devices.reshape(8, 2, 4, 4, 2), ("z", "y_hi", "x", "y_lo", "core")
    )
    whole = P(DP, CTX, None, None, None)
    return jax.shard_map(
        body,
        mesh=fine,
        in_specs=(whole, whole, P(), P(), P()),
        out_specs=(whole, P(), P(), P()),
        check_vma=False,
    )
```

```python
import functools

import jax
import jax.numpy as jnp
from jax import lax
from jax.experimental import pallas as pl
from jax.experimental.pallas import tpu as pltpu
from jax.sharding import PartitionSpec as P

GROUPS = 32
CHANNELS = 128
SIDE = 16
FRAMES = 2
ROWS = FRAMES * SIDE * SIDE
EPSILON = 1e-06
TAPS = 14
OWNED = TAPS * CHANNELS
PARTS = 32
CHUNK = OWNED // PARTS

ALL = ("z", "y_hi", "x", "y_lo", "core")
DP = ("z", "y_hi", "x")
CTX = ("y_lo", "core")
CELLS = 64 * 8 * ROWS
MEMBERS = 8 * ROWS * (CHANNELS // GROUPS)
SCALE = CELLS**-0.5

f32 = jnp.float32
bf16 = jnp.bfloat16


def index(z, y, x, core):
    return ((z * 2 + y // 4) * 4 + x) * 8 + (y % 4) * 2 + core


EXCHANGE = [[index(z, y, x, 0) for z in range(8) for x in range(4)] for y in range(8)] + [
    [index(z, y, x, 1) for y in range(8) for x in range(4)] for z in range(8)
]


COLUMN = [[index(z, y, x, 0) for y in range(8)] for z in range(8) for x in range(4)] + [
    [index(z, y, x, 1) for z in range(8)] for y in range(8) for x in range(4)
]


def call(
    kernel, ins, outs, scratch=(), flops=0, bytes_accessed=0, vmem=32, far_outs=(), aliases=None
):
    return pl.pallas_call(
        kernel,
        out_shape=[jax.ShapeDtypeStruct(s, d) for s, d in outs],
        in_specs=[pl.BlockSpec(memory_space=pltpu.HBM if i else pltpu.VMEM) for i in ins],
        out_specs=[
            pl.BlockSpec(memory_space=pltpu.HBM if i in far_outs else pltpu.VMEM)
            for i in range(len(outs))
        ],
        input_output_aliases=aliases or {},
        scratch_shapes=list(scratch),
        compiler_params=pltpu.CompilerParams(vmem_limit_bytes=vmem << 20),
        cost_estimate=pl.CostEstimate(
            flops=flops, bytes_accessed=bytes_accessed, transcendentals=0
        ),
    )


def column(rows):
    return lax.broadcasted_iota(jnp.int32, (rows, CHANNELS), 0) % SIDE


def next_column(x):
    return jnp.where(column(x.shape[0]) == SIDE - 1, 0.0, pltpu.roll(x, x.shape[0] - 1, 0))


def last_column(x):
    return jnp.where(column(x.shape[0]) == 0, 0.0, pltpu.roll(x, 1, 0))


def group_mean(x):
    place = lax.broadcasted_iota(jnp.int32, x.shape, 1) % (CHANNELS // GROUPS)
    total = x
    for d in range(1, CHANNELS // GROUPS):
        total = total + jnp.where(place >= d, pltpu.roll(x, d, 1), 0.0)
        total = total + jnp.where(
            place < CHANNELS // GROUPS - d, pltpu.roll(x, CHANNELS - d, 1), 0.0
        )
    return total / MEMBERS


def first_chip():
    return lax.axis_index("y_lo") == 0


def load_kernel(
    x_hbm, cot_hbm, gain_hbm, bias_hbm, both_ref, mixed_ref, stats_ref, gain_ref, bias_ref, sems
):
    copies = [
        pltpu.make_async_copy(src, dst, sems.at[i])
        for i, (src, dst) in enumerate(
            [
                (x_hbm, both_ref.at[0:FRAMES]),
                (cot_hbm, both_ref.at[FRAMES:]),
                (gain_hbm, gain_ref),
                (bias_hbm, bias_ref),
            ]
        )
    ]
    for copy in copies:
        copy.start()
    copies[0].wait()
    values = both_ref[0:FRAMES].reshape(ROWS, CHANNELS).astype(f32)
    sums = [
        jnp.sum(values, axis=0, keepdims=True),
        jnp.sum(values * values, axis=0, keepdims=True),
    ]
    for copy in copies[1:]:
        copy.wait()
    sums = jnp.concatenate(
        sums + [gain_ref[...], bias_ref[...], jnp.zeros((4, CHANNELS), f32)], axis=0
    )
    stats_ref[...] = jnp.broadcast_to(sums[None], stats_ref.shape)
    core = lax.axis_index("core")

    @pl.when(core == 0)
    def _():
        mixed_ref[...] = both_ref[FRAMES:]

    @pl.when(core == 1)
    def _():
        mixed_ref[...] = both_ref[0:FRAMES]


def norm_kernel(stats_ref, norm_ref):
    means = group_mean(jnp.sum(stats_ref[...], axis=0))
    average = means[0:1]
    spread = means[1:2] - average * average
    norm_ref[...] = jnp.concatenate(
        [average, lax.rsqrt(spread + EPSILON), stats_ref[0, 2:4], jnp.zeros((4, CHANNELS), f32)],
        axis=0,
    )


def blank_edges(pad_ref):
    blank = jnp.zeros((pad_ref.shape[0], 1, SIDE, CHANNELS), bf16)
    pad_ref[:, 0:1] = blank
    pad_ref[:, SIDE + 1 : SIDE + 2] = blank


def taps_kernel(both_ref, partner_ref, mixed_ref, norm_ref, out_ref, act_ref, wide_ref):
    core = lax.axis_index("core")
    inside = slice(1, SIDE + 1)

    def activation(x):
        values = x.reshape(-1, CHANNELS).astype(f32)
        shifted = (values - norm_ref[0:1]) * norm_ref[1:2] * norm_ref[2:3] + norm_ref[3:4]
        return (shifted / (1.0 + jnp.exp(-shifted))).astype(bf16).reshape(x.shape)

    def put_columns(cot, start):
        cot = cot.reshape(-1, CHANNELS)
        rows = pl.ds(pl.multiple_of(start, SIDE * SIDE), cot.shape[0])
        cot32 = cot.astype(f32)
        wide_ref[rows, 0:CHANNELS] = next_column(cot32).astype(bf16)
        wide_ref[rows, CHANNELS : 2 * CHANNELS] = cot
        wide_ref[rows, 2 * CHANNELS :] = last_column(cot32).astype(bf16)

    blank_edges(act_ref)
    act_ref[3 * FRAMES] = jnp.zeros((SIDE + 2, SIDE, CHANNELS), bf16)
    for source, at in ((both_ref, core), (partner_ref, 1 - core)):
        act_ref[pl.ds(FRAMES + FRAMES * at, FRAMES), inside] = activation(source[0:FRAMES])
        put_columns(source[FRAMES:], at * ROWS)

    @pl.when(core == 0)
    def _():
        wide_ref[2 * ROWS :] = jnp.zeros((SIDE * SIDE, 3 * CHANNELS), bf16)

    @pl.when(core == 1)
    def _():
        put_columns(mixed_ref[0:1], 2 * ROWS)

    later = jnp.logical_not(first_chip())

    @pl.when(first_chip())
    def _():
        act_ref[0:1, inside] = act_ref[FRAMES : FRAMES + 1, inside]
        act_ref[1:2, inside] = act_ref[FRAMES : FRAMES + 1, inside]

    @pl.when(later & (core == 0))
    def _():
        act_ref[0:FRAMES, inside] = activation(mixed_ref[...])

    @pl.when(later & (core == 1))
    def _():
        act_ref[0:FRAMES, inside] = jnp.zeros((FRAMES, SIDE, SIDE, CHANNELS), bf16)

    for j in range(5):
        q = 4 * core + j
        a, b = q // 3, q % 3
        x = act_ref[pl.ds(a, 5), pl.ds(b, SIDE)].reshape(5 * SIDE * SIDE, CHANNELS)
        y = lax.dot_general(
            x, wide_ref[...], (((0,), (0,)), ((), ())), preferred_element_type=f32
        ).astype(bf16)
        for c in range(3):
            value = y[:, c * CHANNELS : (c + 1) * CHANNELS]
            at = j * 3 + c

            def put(value=value, at=at):
                rows = pl.ds(pl.multiple_of((at - 2 * core) * CHANNELS, CHANNELS), CHANNELS)
                out_ref[rows] = value

            if at < 2:
                pl.when(core == 0)(put)
            elif at >= TAPS:
                pl.when(core == 1)(put)
            else:
                put()

    @pl.when(core == 1)
    def _():
        out_ref[OWNED - CHANNELS :] = jnp.zeros((CHANNELS, CHANNELS), bf16)


def data_grad_kernel(
    both_ref, partner_ref, mixed_ref, norm_ref, weight_hbm,
    pre_ref, small_ref, pad_ref, wide_ref, weight_ref, sem,
):
    load = pltpu.make_async_copy(weight_hbm, weight_ref, sem)
    load.start()
    core = lax.axis_index("core")
    inside = slice(1, SIDE + 1)
    blank_edges(pad_ref)
    pad_ref[0:FRAMES, inside] = both_ref[FRAMES:]

    @pl.when(core == 0)
    def _():
        pad_ref[FRAMES:, inside] = partner_ref[FRAMES:]

    @pl.when(core == 1)
    def _():
        pad_ref[FRAMES:, inside] = mixed_ref[...]

    def slab(frame, count):
        return jnp.concatenate(
            [
                pad_ref[frame : frame + count, 2 - b : 2 - b + SIDE].reshape(-1, CHANNELS)
                for b in range(3)
            ],
            axis=1,
        )

    def taps(a):
        return jnp.concatenate(
            [weight_ref[a, b].reshape(3 * CHANNELS, CHANNELS) for b in range(3)], axis=1
        )

    def product(x, w):
        return lax.dot_general(x, w, (((1,), (1,)), ((), ())), preferred_element_type=f32)

    load.wait()
    wide_ref[...] = (
        product(slab(2, FRAMES), taps(0))
        + product(slab(1, FRAMES), taps(1))
        + product(slab(0, FRAMES), taps(2))
    )

    @pl.when(first_chip() & (core == 0))
    def _():
        plane = SIDE * SIDE
        wide_ref[0:plane] = wide_ref[0:plane] + (
            product(slab(0, 1), taps(0))
            + (product(slab(1, 1), taps(0)) + product(slab(0, 1), taps(1)))
        )

    act_grad = (
        next_column(wide_ref[:, 0:CHANNELS])
        + wide_ref[:, CHANNELS : 2 * CHANNELS]
        + last_column(wide_ref[:, 2 * CHANNELS :])
    )
    values = both_ref[0:FRAMES].reshape(ROWS, CHANNELS).astype(f32)
    normed = (values - norm_ref[0:1]) * norm_ref[1:2]
    shifted = normed * norm_ref[2:3] + norm_ref[3:4]
    sig = 1.0 / (1.0 + jnp.exp(-shifted))
    pre = act_grad * sig * (1.0 + shifted * (1.0 - sig))
    pre_ref[...] = pre
    small_ref[...] = jnp.concatenate(
        [
            jnp.sum(pre * normed, axis=0, keepdims=True),
            jnp.sum(pre, axis=0, keepdims=True),
            jnp.zeros((6, CHANNELS), f32),
        ],
        axis=0,
    )


def sum_kernel(parts_ref, small_ref, other_ref, out_ref):
    total = parts_ref[0].astype(f32)
    for i in range(1, PARTS):
        total = total + parts_ref[i].astype(f32)
    total = jnp.concatenate([total, small_ref[...] + other_ref[...]], axis=0)
    out_ref[...] = jnp.broadcast_to(total[None], out_ref.shape)


def spread_kernel(parts_ref, out_ref, clip_ref):
    total = jnp.sum(parts_ref[...], axis=0)
    clip_ref[...] = jnp.sum(parts_ref[pl.ds(4 * lax.axis_index("y_hi"), 4), CHUNK:], axis=0)
    small = total[CHUNK : CHUNK + 2]
    high = small.astype(bf16).astype(f32)
    mine = jnp.concatenate(
        [total[0:CHUNK], high, small - high, jnp.zeros((4, CHANNELS), f32)], axis=0
    ).astype(bf16)
    out_ref[...] = jnp.broadcast_to(mine[None], out_ref.shape)


def input_grad_kernel(both_ref, pre_ref, norm_ref, clip_ref, other_ref, out_ref):
    clip = jnp.where(lax.axis_index("core") == 0, clip_ref[...], other_ref[...])
    means = group_mean(clip * norm_ref[2:3])
    values = both_ref[0:FRAMES].reshape(ROWS, CHANNELS).astype(f32)
    normed = (values - norm_ref[0:1]) * norm_ref[1:2]
    grad = norm_ref[1:2] * (pre_ref[...] * norm_ref[2:3] - means[1:2] - normed * means[0:1])
    out_ref[...] = grad.astype(bf16).reshape(out_ref.shape)


PIECES = 4


def write_half(core, total_ref, weight_hbm, half_ref, sems, meanwhile=None):
    chunks = PARTS // PIECES
    rows = chunks * CHUNK
    end = 27 * CHANNELS - OWNED
    for i in range(PIECES):
        at = i * rows
        half_ref[at : at + rows] = (
            total_ref[i * chunks : (i + 1) * chunks, 0:CHUNK].astype(f32).reshape(rows, CHANNELS)
            * SCALE
        )
        last = min(rows, end - at)

        @pl.when(core == 0)
        def _(i=i, at=at):
            pltpu.make_async_copy(
                half_ref.at[at : at + rows], weight_hbm.at[at : at + rows], sems.at[i]
            ).start()

        @pl.when(core == 1)
        def _(i=i, at=at, last=last):
            pltpu.make_async_copy(
                half_ref.at[at : at + last],
                weight_hbm.at[OWNED + at : OWNED + at + last],
                sems.at[i],
            ).start()

    if meanwhile is not None:
        meanwhile()
    for i in range(PIECES):
        at = i * rows
        last = min(rows, end - at)

        @pl.when(core == 0)
        def _(i=i, at=at):
            pltpu.make_async_copy(
                half_ref.at[at : at + rows], weight_hbm.at[at : at + rows], sems.at[i]
            ).wait()

        @pl.when(core == 1)
        def _(i=i, at=at, last=last):
            pltpu.make_async_copy(
                half_ref.at[at : at + last],
                weight_hbm.at[OWNED + at : OWNED + at + last],
                sems.at[i],
            ).wait()


def final_own_kernel(own_ref, weight_hbm, half_ref, sems):
    write_half(lax.axis_index("core"), own_ref, weight_hbm, half_ref, sems)


def final_other_kernel(
    own_ref, other_ref, started_hbm, weight_hbm, gain_ref, bias_ref, half_ref, sems
):
    core = lax.axis_index("core")

    def put_small(ref):
        small = ref[0, CHUNK:].astype(f32)
        for m in range(1, PARTS):
            small = small + ref[m, CHUNK:].astype(f32)
        gain_ref[...] = (small[0:1] + small[2:3]) * SCALE
        bias_ref[...] = (small[1:2] + small[3:4]) * SCALE

    def smalls():
        pl.when(core == 0)(lambda: put_small(own_ref))
        pl.when(core == 1)(lambda: put_small(other_ref))

    write_half(1 - core, other_ref, weight_hbm, half_ref, sems, smalls)


def exchange(x, groups):
    return lax.all_to_all(x, ALL, 0, 0, axis_index_groups=groups, tiled=True)


def body(inputs, cotangent, conv_weight, norm_gain, norm_bias):
    x, cot = inputs[0], cotangent[0]
    swap = [(0, 1), (1, 0)]
    frames = (FRAMES, SIDE, SIDE, CHANNELS)
    one_row = ((1, CHANNELS), f32)

    both, mixed, stats, _, _ = call(
        load_kernel,
        [1, 1, 1, 1],
        [((2 * FRAMES, SIDE, SIDE, CHANNELS), bf16), (frames, bf16), ((8, 8, CHANNELS), f32),
         one_row, one_row],
        [pltpu.SemaphoreType.DMA((4,))],
        bytes_accessed=1 << 18,
        vmem=60,
    )(x, cot, norm_gain[None], norm_bias[None])
    stats = lax.all_to_all(stats, CTX, 0, 0, tiled=True)
    partner = lax.ppermute(both, "core", swap)
    mixed = lax.ppermute(
        mixed, CTX, [(1, 2), (3, 4), (5, 6), (2, 1), (4, 3), (6, 5)]
    )
    (norm,) = call(
        norm_kernel, [0], [((8, CHANNELS), f32)], bytes_accessed=1 << 19, flops=1 << 34
    )(stats)
    (buffer,) = call(
        taps_kernel,
        [0] * 4,
        [((OWNED, CHANNELS), bf16)],
        [
            pltpu.VMEM((3 * FRAMES + 1, SIDE + 2, SIDE, CHANNELS), bf16),
            pltpu.VMEM((5 * SIDE * SIDE, 3 * CHANNELS), bf16),
        ],
        flops=4 * ROWS * 15 * CHANNELS * CHANNELS,
        bytes_accessed=1 << 20,
    )(both, partner, mixed, norm)
    parts = exchange(buffer.reshape(PARTS, CHUNK, CHANNELS), EXCHANGE)
    pre, small = call(
        data_grad_kernel,
        [0] * 4 + [1],
        [((ROWS, CHANNELS), f32), ((8, CHANNELS), f32)],
        [
            pltpu.VMEM((2 * FRAMES, SIDE + 2, SIDE, CHANNELS), bf16),
            pltpu.VMEM((ROWS, 3 * CHANNELS), f32),
            pltpu.VMEM((3, 3, 3, CHANNELS, CHANNELS), bf16),
            pltpu.SemaphoreType.DMA,
        ],
        flops=2 * ROWS * 27 * CHANNELS * CHANNELS,
        bytes_accessed=2 << 20,
    )(both, partner, mixed, norm, conv_weight)
    other_small = lax.ppermute(small, "core", swap)
    (one,) = call(sum_kernel, [0] * 3, [((8, CHUNK + 8, CHANNELS), f32)], bytes_accessed=1 << 19)(
        parts, small, other_small
    )
    spread, clip = call(
        spread_kernel,
        [0],
        [((PARTS, CHUNK + 8, CHANNELS), bf16), ((8, CHANNELS), f32)],
        bytes_accessed=1 << 19,
    )(exchange(one, COLUMN))
    own_total = exchange(spread, EXCHANGE)
    other_clip = lax.ppermute(clip, "core", [(0, 1)])
    (input_grad,) = call(input_grad_kernel, [0] * 5, [(frames, bf16)], bytes_accessed=1 << 19)(
        both, pre, norm, clip, other_clip
    )
    own_total, input_grad = lax.optimization_barrier((own_total, input_grad))
    other_total = lax.ppermute(own_total, "core", swap)
    scratch = [pltpu.VMEM((OWNED, CHANNELS), f32), pltpu.SemaphoreType.DMA((PIECES,))]
    (started,) = call(
        final_own_kernel,
        [0],
        [((27 * CHANNELS, CHANNELS), f32)],
        scratch,
        bytes_accessed=2 << 20,
        far_outs=(0,),
    )(own_total)
    weight_grad, gain_grad, bias_grad = call(
        final_other_kernel,
        [0, 0, 1],
        [((27 * CHANNELS, CHANNELS), f32), one_row, one_row],
        scratch,
        bytes_accessed=2 << 20,
        far_outs=(0,),
        aliases={2: 0},
    )(own_total, other_total, started)
    return (
        input_grad[None],
        weight_grad.reshape(3, 3, 3, CHANNELS, CHANNELS),
        gain_grad[0],
        bias_grad[0],
    )


def solution(mesh):
    fine = jax.sharding.Mesh(
        mesh.devices.reshape(8, 2, 4, 4, 2), ("z", "y_hi", "x", "y_lo", "core")
    )
    whole = P(DP, CTX, None, None, None)
    return jax.shard_map(
        body,
        mesh=fine,
        in_specs=(whole, whole, P(), P(), P()),
        out_specs=(whole, P(), P(), P()),
        check_vma=False,
    )
```

```python
import functools

import jax
import jax.numpy as jnp
from jax import lax
from jax.experimental import pallas as pl
from jax.experimental.pallas import tpu as pltpu
from jax.sharding import PartitionSpec as P

GROUPS = 32
CHANNELS = 128
SIDE = 16
FRAMES = 2
ROWS = FRAMES * SIDE * SIDE
EPSILON = 1e-06
TAPS = 14
OWNED = TAPS * CHANNELS
PARTS = 32
CHUNK = OWNED // PARTS

ALL = ("z", "y_hi", "x", "y_lo", "core")
DP = ("z", "y_hi", "x")
CTX = ("y_lo", "core")
CELLS = 64 * 8 * ROWS
MEMBERS = 8 * ROWS * (CHANNELS // GROUPS)
SCALE = CELLS**-0.5

f32 = jnp.float32
bf16 = jnp.bfloat16


def index(z, y, x, core):
    return ((z * 2 + y // 4) * 4 + x) * 8 + (y % 4) * 2 + core


EXCHANGE = [[index(z, y, x, 0) for z in range(8) for x in range(4)] for y in range(8)] + [
    [index(z, y, x, 1) for y in range(8) for x in range(4)] for z in range(8)
]


COLUMN = [[index(z, y, x, 0) for y in range(8)] for z in range(8) for x in range(4)] + [
    [index(z, y, x, 1) for z in range(8)] for y in range(8) for x in range(4)
]


def call(
    kernel, ins, outs, scratch=(), flops=0, bytes_accessed=0, vmem=32, far_outs=(), aliases=None
):
    return pl.pallas_call(
        kernel,
        out_shape=[jax.ShapeDtypeStruct(s, d) for s, d in outs],
        in_specs=[pl.BlockSpec(memory_space=pltpu.HBM if i else pltpu.VMEM) for i in ins],
        out_specs=[
            pl.BlockSpec(memory_space=pltpu.HBM if i in far_outs else pltpu.VMEM)
            for i in range(len(outs))
        ],
        input_output_aliases=aliases or {},
        scratch_shapes=list(scratch),
        compiler_params=pltpu.CompilerParams(vmem_limit_bytes=vmem << 20),
        cost_estimate=pl.CostEstimate(
            flops=flops, bytes_accessed=bytes_accessed, transcendentals=0
        ),
    )


def column(rows):
    return lax.broadcasted_iota(jnp.int32, (rows, CHANNELS), 0) % SIDE


def next_column(x):
    return jnp.where(column(x.shape[0]) == SIDE - 1, 0.0, pltpu.roll(x, x.shape[0] - 1, 0))


def last_column(x):
    return jnp.where(column(x.shape[0]) == 0, 0.0, pltpu.roll(x, 1, 0))


def group_mean(x):
    place = lax.broadcasted_iota(jnp.int32, x.shape, 1) % (CHANNELS // GROUPS)
    total = x
    for d in range(1, CHANNELS // GROUPS):
        total = total + jnp.where(place >= d, pltpu.roll(x, d, 1), 0.0)
        total = total + jnp.where(
            place < CHANNELS // GROUPS - d, pltpu.roll(x, CHANNELS - d, 1), 0.0
        )
    return total / MEMBERS


def first_chip():
    return lax.axis_index("y_lo") == 0


def load_kernel(
    x_hbm, cot_hbm, gain_hbm, bias_hbm, both_hbm, mixed_hbm, stats_ref, x_ref, gain_ref, bias_ref, sems
):
    core = lax.axis_index("core")
    loads = [
        pltpu.make_async_copy(src, dst, sems.at[i])
        for i, (src, dst) in enumerate(
            [(x_hbm, x_ref), (gain_hbm, gain_ref), (bias_hbm, bias_ref)]
        )
    ]
    moves = [
        pltpu.make_async_copy(x_hbm, both_hbm.at[0:FRAMES], sems.at[3]),
        pltpu.make_async_copy(cot_hbm, both_hbm.at[FRAMES:], sems.at[4]),
    ]
    for copy in loads + moves:
        copy.start()
    pl.when(core == 0)(lambda: pltpu.make_async_copy(cot_hbm, mixed_hbm, sems.at[5]).start())
    pl.when(core == 1)(lambda: pltpu.make_async_copy(x_hbm, mixed_hbm, sems.at[5]).start())
    for copy in loads:
        copy.wait()
    values = x_ref[...].reshape(ROWS, CHANNELS).astype(f32)
    sums = jnp.concatenate(
        [
            jnp.sum(values, axis=0, keepdims=True),
            jnp.sum(values * values, axis=0, keepdims=True),
            gain_ref[...],
            bias_ref[...],
            jnp.zeros((4, CHANNELS), f32),
        ],
        axis=0,
    )
    stats_ref[...] = jnp.broadcast_to(sums[None], stats_ref.shape)
    for copy in moves:
        copy.wait()
    pl.when(core == 0)(lambda: pltpu.make_async_copy(cot_hbm, mixed_hbm, sems.at[5]).wait())
    pl.when(core == 1)(lambda: pltpu.make_async_copy(x_hbm, mixed_hbm, sems.at[5]).wait())


def norm_kernel(stats_ref, norm_ref):
    means = group_mean(jnp.sum(stats_ref[...], axis=0))
    average = means[0:1]
    spread = means[1:2] - average * average
    norm_ref[...] = jnp.concatenate(
        [average, lax.rsqrt(spread + EPSILON), stats_ref[0, 2:4], jnp.zeros((4, CHANNELS), f32)],
        axis=0,
    )


def blank_edges(pad_ref):
    blank = jnp.zeros((pad_ref.shape[0], 1, SIDE, CHANNELS), bf16)
    pad_ref[:, 0:1] = blank
    pad_ref[:, SIDE + 1 : SIDE + 2] = blank


def taps_kernel(
    both_ref, partner_ref, mixed_ref, norm_ref, out_hbm, out_ref, act_ref, wide_ref, sems
):
    core = lax.axis_index("core")
    inside = slice(1, SIDE + 1)

    def activation(x):
        values = x.reshape(-1, CHANNELS).astype(f32)
        shifted = (values - norm_ref[0:1]) * norm_ref[1:2] * norm_ref[2:3] + norm_ref[3:4]
        return (shifted / (1.0 + jnp.exp(-shifted))).astype(bf16).reshape(x.shape)

    def put_columns(cot, start):
        cot = cot.reshape(-1, CHANNELS)
        rows = pl.ds(pl.multiple_of(start, SIDE * SIDE), cot.shape[0])
        cot32 = cot.astype(f32)
        wide_ref[rows, 0:CHANNELS] = next_column(cot32).astype(bf16)
        wide_ref[rows, CHANNELS : 2 * CHANNELS] = cot
        wide_ref[rows, 2 * CHANNELS :] = last_column(cot32).astype(bf16)

    blank_edges(act_ref)
    act_ref[3 * FRAMES] = jnp.zeros((SIDE + 2, SIDE, CHANNELS), bf16)
    for source, at in ((both_ref, core), (partner_ref, 1 - core)):
        act_ref[pl.ds(FRAMES + FRAMES * at, FRAMES), inside] = activation(source[0:FRAMES])
        put_columns(source[FRAMES:], at * ROWS)

    @pl.when(core == 0)
    def _():
        wide_ref[2 * ROWS :] = jnp.zeros((SIDE * SIDE, 3 * CHANNELS), bf16)

    @pl.when(core == 1)
    def _():
        put_columns(mixed_ref[0:1], 2 * ROWS)

    later = jnp.logical_not(first_chip())

    @pl.when(first_chip())
    def _():
        act_ref[0:1, inside] = act_ref[FRAMES : FRAMES + 1, inside]
        act_ref[1:2, inside] = act_ref[FRAMES : FRAMES + 1, inside]

    @pl.when(later & (core == 0))
    def _():
        act_ref[0:FRAMES, inside] = activation(mixed_ref[...])

    @pl.when(later & (core == 1))
    def _():
        act_ref[0:FRAMES, inside] = jnp.zeros((FRAMES, SIDE, SIDE, CHANNELS), bf16)

    def send(j, begin):
        for own, start, stop in ((0, 3 * j, min(3 * j + 3, TAPS)), (1, max(3 * j - 2, 0), 3 * j + 1)):

            @pl.when(core == own)
            def _(start=start, stop=stop):
                rows = slice(start * CHANNELS, stop * CHANNELS)
                copy = pltpu.make_async_copy(out_ref.at[rows], out_hbm.at[rows], sems.at[j])
                copy.start() if begin else copy.wait()

    def send_blank(begin):
        @pl.when(core == 1)
        def _():
            rows = slice(OWNED - CHANNELS, OWNED)
            copy = pltpu.make_async_copy(out_ref.at[rows], out_hbm.at[rows], sems.at[5])
            copy.start() if begin else copy.wait()

    @pl.when(core == 1)
    def _():
        out_ref[OWNED - CHANNELS :] = jnp.zeros((CHANNELS, CHANNELS), bf16)

    send_blank(True)
    for j in range(5):
        q = 4 * core + j
        a, b = q // 3, q % 3
        x = act_ref[pl.ds(a, 5), pl.ds(b, SIDE)].reshape(5 * SIDE * SIDE, CHANNELS)
        y = lax.dot_general(
            x, wide_ref[...], (((0,), (0,)), ((), ())), preferred_element_type=f32
        ).astype(bf16)
        for c in range(3):
            value = y[:, c * CHANNELS : (c + 1) * CHANNELS]
            at = j * 3 + c

            def put(value=value, at=at):
                rows = pl.ds(pl.multiple_of((at - 2 * core) * CHANNELS, CHANNELS), CHANNELS)
                out_ref[rows] = value

            if at < 2:
                pl.when(core == 0)(put)
            elif at >= TAPS:
                pl.when(core == 1)(put)
            else:
                put()
        send(j, True)
    send_blank(False)
    for j in range(5):
        send(j, False)


def data_grad_kernel(
    both_ref, partner_ref, mixed_ref, norm_ref, weight_hbm,
    pre_ref, small_ref, pad_ref, wide_ref, weight_ref, sem,
):
    load = pltpu.make_async_copy(weight_hbm, weight_ref, sem)
    load.start()
    core = lax.axis_index("core")
    inside = slice(1, SIDE + 1)
    blank_edges(pad_ref)
    pad_ref[0:FRAMES, inside] = both_ref[FRAMES:]

    @pl.when(core == 0)
    def _():
        pad_ref[FRAMES:, inside] = partner_ref[FRAMES:]

    @pl.when(core == 1)
    def _():
        pad_ref[FRAMES:, inside] = mixed_ref[...]

    def slab(frame, count):
        return jnp.concatenate(
            [
                pad_ref[frame : frame + count, 2 - b : 2 - b + SIDE].reshape(-1, CHANNELS)
                for b in range(3)
            ],
            axis=1,
        )

    def taps(a):
        return jnp.concatenate(
            [weight_ref[a, b].reshape(3 * CHANNELS, CHANNELS) for b in range(3)], axis=1
        )

    def product(x, w):
        return lax.dot_general(x, w, (((1,), (1,)), ((), ())), preferred_element_type=f32)

    load.wait()
    wide_ref[...] = (
        product(slab(2, FRAMES), taps(0))
        + product(slab(1, FRAMES), taps(1))
        + product(slab(0, FRAMES), taps(2))
    )

    @pl.when(first_chip() & (core == 0))
    def _():
        plane = SIDE * SIDE
        wide_ref[0:plane] = wide_ref[0:plane] + (
            product(slab(0, 1), taps(0))
            + (product(slab(1, 1), taps(0)) + product(slab(0, 1), taps(1)))
        )

    act_grad = (
        next_column(wide_ref[:, 0:CHANNELS])
        + wide_ref[:, CHANNELS : 2 * CHANNELS]
        + last_column(wide_ref[:, 2 * CHANNELS :])
    )
    values = both_ref[0:FRAMES].reshape(ROWS, CHANNELS).astype(f32)
    normed = (values - norm_ref[0:1]) * norm_ref[1:2]
    shifted = normed * norm_ref[2:3] + norm_ref[3:4]
    sig = 1.0 / (1.0 + jnp.exp(-shifted))
    pre = act_grad * sig * (1.0 + shifted * (1.0 - sig))
    pre_ref[...] = pre
    small_ref[...] = jnp.concatenate(
        [
            jnp.sum(pre * normed, axis=0, keepdims=True),
            jnp.sum(pre, axis=0, keepdims=True),
            jnp.zeros((6, CHANNELS), f32),
        ],
        axis=0,
    )


def sum_kernel(parts_ref, small_ref, other_ref, out_ref):
    total = parts_ref[0].astype(f32)
    for i in range(1, PARTS):
        total = total + parts_ref[i].astype(f32)
    total = jnp.concatenate([total, small_ref[...] + other_ref[...]], axis=0)
    out_ref[...] = jnp.broadcast_to(total[None], out_ref.shape)


def spread_kernel(parts_ref, out_hbm, clip_ref, some_ref, sems):
    total = jnp.sum(parts_ref[...], axis=0)
    clip_ref[...] = jnp.sum(parts_ref[pl.ds(4 * lax.axis_index("y_hi"), 4), CHUNK:], axis=0)
    small = total[CHUNK : CHUNK + 2]
    high = small.astype(bf16).astype(f32)
    mine = jnp.concatenate(
        [total[0:CHUNK], high, small - high, jnp.zeros((4, CHANNELS), f32)], axis=0
    ).astype(bf16)
    some_ref[...] = jnp.broadcast_to(mine[None], some_ref.shape)
    copies = [
        pltpu.make_async_copy(some_ref, out_hbm.at[4 * i : 4 * i + 4], sems.at[i])
        for i in range(PARTS // 4)
    ]
    for copy in copies:
        copy.start()
    for copy in copies:
        copy.wait()


def input_grad_kernel(both_ref, pre_ref, norm_ref, clip_ref, other_ref, out_ref):
    clip = jnp.where(lax.axis_index("core") == 0, clip_ref[...], other_ref[...])
    means = group_mean(clip * norm_ref[2:3])
    values = both_ref[0:FRAMES].reshape(ROWS, CHANNELS).astype(f32)
    normed = (values - norm_ref[0:1]) * norm_ref[1:2]
    grad = norm_ref[1:2] * (pre_ref[...] * norm_ref[2:3] - means[1:2] - normed * means[0:1])
    out_ref[...] = grad.astype(bf16).reshape(out_ref.shape)


PIECES = 4


def write_half(core, total_ref, weight_hbm, half_ref, sems):
    chunks = PARTS // PIECES
    rows = chunks * CHUNK
    end = 27 * CHANNELS - OWNED
    for i in range(PIECES):
        at = i * rows
        half_ref[at : at + rows] = (
            total_ref[i * chunks : (i + 1) * chunks, 0:CHUNK].astype(f32).reshape(rows, CHANNELS)
            * SCALE
        )
        last = min(rows, end - at)

        @pl.when(core == 0)
        def _(i=i, at=at):
            pltpu.make_async_copy(
                half_ref.at[at : at + rows], weight_hbm.at[at : at + rows], sems.at[i]
            ).start()

        @pl.when(core == 1)
        def _(i=i, at=at, last=last):
            pltpu.make_async_copy(
                half_ref.at[at : at + last],
                weight_hbm.at[OWNED + at : OWNED + at + last],
                sems.at[i],
            ).start()

    for i in range(PIECES):
        at = i * rows
        last = min(rows, end - at)

        @pl.when(core == 0)
        def _(i=i, at=at):
            pltpu.make_async_copy(
                half_ref.at[at : at + rows], weight_hbm.at[at : at + rows], sems.at[i]
            ).wait()

        @pl.when(core == 1)
        def _(i=i, at=at, last=last):
            pltpu.make_async_copy(
                half_ref.at[at : at + last],
                weight_hbm.at[OWNED + at : OWNED + at + last],
                sems.at[i],
            ).wait()


def final_own_kernel(own_ref, weight_hbm, half_ref, sems):
    write_half(lax.axis_index("core"), own_ref, weight_hbm, half_ref, sems)


def final_other_kernel(
    own_ref, other_ref, started_hbm, weight_hbm, gain_hbm, bias_hbm,
    half_ref, sems, gain_ref, bias_ref, small_sems,
):
    core = lax.axis_index("core")

    def put_small(ref):
        small = ref[0, CHUNK:].astype(f32)
        for m in range(1, PARTS):
            small = small + ref[m, CHUNK:].astype(f32)
        gain_ref[...] = (small[0:1] + small[2:3]) * SCALE
        bias_ref[...] = (small[1:2] + small[3:4]) * SCALE

    pl.when(core == 0)(lambda: put_small(own_ref))
    pl.when(core == 1)(lambda: put_small(other_ref))
    copies = [
        pltpu.make_async_copy(gain_ref, gain_hbm, small_sems.at[0]),
        pltpu.make_async_copy(bias_ref, bias_hbm, small_sems.at[1]),
    ]
    for copy in copies:
        copy.start()
    write_half(1 - core, other_ref, weight_hbm, half_ref, sems)
    for copy in copies:
        copy.wait()


def exchange(x, groups):
    return lax.all_to_all(x, ALL, 0, 0, axis_index_groups=groups, tiled=True)


def body(inputs, cotangent, conv_weight, norm_gain, norm_bias):
    x, cot = inputs[0], cotangent[0]
    swap = [(0, 1), (1, 0)]
    frames = (FRAMES, SIDE, SIDE, CHANNELS)
    one_row = ((1, CHANNELS), f32)

    both, mixed, stats = call(
        load_kernel,
        [1, 1, 1, 1],
        [((2 * FRAMES, SIDE, SIDE, CHANNELS), bf16), (frames, bf16), ((8, 8, CHANNELS), f32)],
        [
            pltpu.VMEM(frames, bf16),
            pltpu.VMEM((1, CHANNELS), f32),
            pltpu.VMEM((1, CHANNELS), f32),
            pltpu.SemaphoreType.DMA((6,)),
        ],
        bytes_accessed=1 << 18,
        vmem=60,
        far_outs=(0, 1),
    )(x, cot, norm_gain[None], norm_bias[None])
    stats = lax.all_to_all(stats, CTX, 0, 0, tiled=True)
    mixed = lax.ppermute(
        mixed, CTX, [(1, 2), (3, 4), (5, 6), (2, 1), (4, 3), (6, 5)]
    )
    partner = lax.ppermute(both, "core", swap)
    (norm,) = call(
        norm_kernel, [0], [((8, CHANNELS), f32)], bytes_accessed=1 << 19, flops=1 << 34
    )(stats)
    (buffer,) = call(
        taps_kernel,
        [0] * 4,
        [((OWNED, CHANNELS), bf16)],
        [
            pltpu.VMEM((OWNED, CHANNELS), bf16),
            pltpu.VMEM((3 * FRAMES + 1, SIDE + 2, SIDE, CHANNELS), bf16),
            pltpu.VMEM((5 * SIDE * SIDE, 3 * CHANNELS), bf16),
            pltpu.SemaphoreType.DMA((6,)),
        ],
        far_outs=(0,),
        flops=4 * ROWS * 15 * CHANNELS * CHANNELS,
        bytes_accessed=1 << 20,
    )(both, partner, mixed, norm)
    parts = exchange(buffer.reshape(PARTS, CHUNK, CHANNELS), EXCHANGE)
    pre, small = call(
        data_grad_kernel,
        [0] * 4 + [1],
        [((ROWS, CHANNELS), f32), ((8, CHANNELS), f32)],
        [
            pltpu.VMEM((2 * FRAMES, SIDE + 2, SIDE, CHANNELS), bf16),
            pltpu.VMEM((ROWS, 3 * CHANNELS), f32),
            pltpu.VMEM((3, 3, 3, CHANNELS, CHANNELS), bf16),
            pltpu.SemaphoreType.DMA,
        ],
        flops=2 * ROWS * 27 * CHANNELS * CHANNELS,
        bytes_accessed=2 << 20,
    )(both, partner, mixed, norm, conv_weight)
    other_small = lax.ppermute(small, "core", swap)
    (one,) = call(sum_kernel, [0] * 3, [((8, CHUNK + 8, CHANNELS), f32)], bytes_accessed=1 << 19)(
        parts, small, other_small
    )
    spread, clip = call(
        spread_kernel,
        [0],
        [((PARTS, CHUNK + 8, CHANNELS), bf16), ((8, CHANNELS), f32)],
        [pltpu.VMEM((4, CHUNK + 8, CHANNELS), bf16), pltpu.SemaphoreType.DMA((PARTS // 4,))],
        far_outs=(0,),
        bytes_accessed=1 << 19,
    )(exchange(one, COLUMN))
    own_total = exchange(spread, EXCHANGE)
    other_clip = lax.ppermute(clip, "core", [(0, 1)])
    (input_grad,) = call(input_grad_kernel, [0] * 5, [(frames, bf16)], bytes_accessed=1 << 19)(
        both, pre, norm, clip, other_clip
    )
    own_total, input_grad = lax.optimization_barrier((own_total, input_grad))
    other_total = lax.ppermute(own_total, "core", swap)
    scratch = [pltpu.VMEM((OWNED, CHANNELS), f32), pltpu.SemaphoreType.DMA((PIECES,))]
    (started,) = call(
        final_own_kernel,
        [0],
        [((27 * CHANNELS, CHANNELS), f32)],
        scratch,
        bytes_accessed=2 << 20,
        far_outs=(0,),
    )(own_total)
    weight_grad, gain_grad, bias_grad = call(
        final_other_kernel,
        [0, 0, 1],
        [((27 * CHANNELS, CHANNELS), f32), one_row, one_row],
        scratch
        + [
            pltpu.VMEM((1, CHANNELS), f32),
            pltpu.VMEM((1, CHANNELS), f32),
            pltpu.SemaphoreType.DMA((2,)),
        ],
        bytes_accessed=2 << 20,
        far_outs=(0, 1, 2),
        aliases={2: 0},
    )(own_total, other_total, started)
    return (
        input_grad[None],
        weight_grad.reshape(3, 3, 3, CHANNELS, CHANNELS),
        gain_grad[0],
        bias_grad[0],
    )


def solution(mesh):
    fine = jax.sharding.Mesh(
        mesh.devices.reshape(8, 2, 4, 4, 2), ("z", "y_hi", "x", "y_lo", "core")
    )
    whole = P(DP, CTX, None, None, None)
    return jax.shard_map(
        body,
        mesh=fine,
        in_specs=(whole, whole, P(), P(), P()),
        out_specs=(whole, P(), P(), P()),
        check_vma=False,
    )
```

```python
import functools

import jax
import jax.numpy as jnp
from jax import lax
from jax.experimental import pallas as pl
from jax.experimental.pallas import tpu as pltpu
from jax.sharding import PartitionSpec as P

GROUPS = 32
CHANNELS = 128
SIDE = 16
FRAMES = 2
ROWS = FRAMES * SIDE * SIDE
EPSILON = 1e-06
TAPS = 14
OWNED = TAPS * CHANNELS
PARTS = 32
CHUNK = OWNED // PARTS

ALL = ("z", "y_hi", "x", "y_lo", "core")
DP = ("z", "y_hi", "x")
CTX = ("y_lo", "core")
CELLS = 64 * 8 * ROWS
MEMBERS = 8 * ROWS * (CHANNELS // GROUPS)
SCALE = CELLS**-0.5

f32 = jnp.float32
bf16 = jnp.bfloat16


def index(z, y, x, core):
    return ((z * 2 + y // 4) * 4 + x) * 8 + (y % 4) * 2 + core


EXCHANGE = [[index(z, y, x, 0) for z in range(8) for x in range(4)] for y in range(8)] + [
    [index(z, y, x, 1) for y in range(8) for x in range(4)] for z in range(8)
]


COLUMN = [[index(z, y, x, 0) for y in range(8)] for z in range(8) for x in range(4)] + [
    [index(z, y, x, 1) for z in range(8)] for y in range(8) for x in range(4)
]


def call(
    kernel, ins, outs, scratch=(), flops=0, bytes_accessed=0, vmem=32, far_outs=(), aliases=None
):
    return pl.pallas_call(
        kernel,
        out_shape=[jax.ShapeDtypeStruct(s, d) for s, d in outs],
        in_specs=[pl.BlockSpec(memory_space=pltpu.HBM if i else pltpu.VMEM) for i in ins],
        out_specs=[
            pl.BlockSpec(memory_space=pltpu.HBM if i in far_outs else pltpu.VMEM)
            for i in range(len(outs))
        ],
        input_output_aliases=aliases or {},
        scratch_shapes=list(scratch),
        compiler_params=pltpu.CompilerParams(vmem_limit_bytes=vmem << 20),
        cost_estimate=pl.CostEstimate(
            flops=flops, bytes_accessed=bytes_accessed, transcendentals=0
        ),
    )


def column(rows):
    return lax.broadcasted_iota(jnp.int32, (rows, CHANNELS), 0) % SIDE


def next_column(x):
    return jnp.where(column(x.shape[0]) == SIDE - 1, 0.0, pltpu.roll(x, x.shape[0] - 1, 0))


def last_column(x):
    return jnp.where(column(x.shape[0]) == 0, 0.0, pltpu.roll(x, 1, 0))


def group_mean(x):
    place = lax.broadcasted_iota(jnp.int32, x.shape, 1) % (CHANNELS // GROUPS)
    total = x
    for d in range(1, CHANNELS // GROUPS):
        total = total + jnp.where(place >= d, pltpu.roll(x, d, 1), 0.0)
        total = total + jnp.where(
            place < CHANNELS // GROUPS - d, pltpu.roll(x, CHANNELS - d, 1), 0.0
        )
    return total / MEMBERS


def first_chip():
    return lax.axis_index("y_lo") == 0


def load_kernel(
    x_hbm, cot_hbm, gain_hbm, bias_hbm, both_hbm, mixed_hbm, stats_ref,
    x_ref, cot_ref, gain_ref, bias_ref, sems,
):
    core = lax.axis_index("core")
    loads = [
        pltpu.make_async_copy(src, dst, sems.at[i])
        for i, (src, dst) in enumerate(
            [(x_hbm, x_ref), (cot_hbm, cot_ref), (gain_hbm, gain_ref), (bias_hbm, bias_ref)]
        )
    ]
    keep_x = pltpu.make_async_copy(x_ref, both_hbm.at[0:FRAMES], sems.at[4])
    keep_cot = pltpu.make_async_copy(cot_ref, both_hbm.at[FRAMES:], sems.at[5])
    mix_x = pltpu.make_async_copy(x_ref, mixed_hbm, sems.at[6])
    mix_cot = pltpu.make_async_copy(cot_ref, mixed_hbm, sems.at[6])
    for copy in loads:
        copy.start()
    loads[0].wait()
    keep_x.start()
    pl.when(core == 1)(lambda: mix_x.start())
    loads[1].wait()
    keep_cot.start()
    pl.when(core == 0)(lambda: mix_cot.start())
    values = x_ref[...].reshape(ROWS, CHANNELS).astype(f32)
    sums = [
        jnp.sum(values, axis=0, keepdims=True),
        jnp.sum(values * values, axis=0, keepdims=True),
    ]
    loads[2].wait()
    loads[3].wait()
    sums = jnp.concatenate(
        sums + [gain_ref[...], bias_ref[...], jnp.zeros((4, CHANNELS), f32)], axis=0
    )
    stats_ref[...] = jnp.broadcast_to(sums[None], stats_ref.shape)
    keep_x.wait()
    keep_cot.wait()
    pl.when(core == 1)(lambda: mix_x.wait())
    pl.when(core == 0)(lambda: mix_cot.wait())


def norm_kernel(stats_ref, norm_ref):
    means = group_mean(jnp.sum(stats_ref[...], axis=0))
    average = means[0:1]
    spread = means[1:2] - average * average
    norm_ref[...] = jnp.concatenate(
        [average, lax.rsqrt(spread + EPSILON), stats_ref[0, 2:4], jnp.zeros((4, CHANNELS), f32)],
        axis=0,
    )


def blank_edges(pad_ref):
    blank = jnp.zeros((pad_ref.shape[0], 1, SIDE, CHANNELS), bf16)
    pad_ref[:, 0:1] = blank
    pad_ref[:, SIDE + 1 : SIDE + 2] = blank


def taps_kernel(
    both_ref, partner_ref, mixed_ref, norm_ref, out_hbm, out_ref, act_ref, wide_ref, sems
):
    core = lax.axis_index("core")
    inside = slice(1, SIDE + 1)

    def activation(x):
        values = x.reshape(-1, CHANNELS).astype(f32)
        shifted = (values - norm_ref[0:1]) * norm_ref[1:2] * norm_ref[2:3] + norm_ref[3:4]
        return (shifted / (1.0 + jnp.exp(-shifted))).astype(bf16).reshape(x.shape)

    def put_columns(cot, start):
        cot = cot.reshape(-1, CHANNELS)
        rows = pl.ds(pl.multiple_of(start, SIDE * SIDE), cot.shape[0])
        cot32 = cot.astype(f32)
        wide_ref[rows, 0:CHANNELS] = next_column(cot32).astype(bf16)
        wide_ref[rows, CHANNELS : 2 * CHANNELS] = cot
        wide_ref[rows, 2 * CHANNELS :] = last_column(cot32).astype(bf16)

    blank_edges(act_ref)
    act_ref[3 * FRAMES] = jnp.zeros((SIDE + 2, SIDE, CHANNELS), bf16)
    for source, at in ((both_ref, core), (partner_ref, 1 - core)):
        act_ref[pl.ds(FRAMES + FRAMES * at, FRAMES), inside] = activation(source[0:FRAMES])
        put_columns(source[FRAMES:], at * ROWS)

    @pl.when(core == 0)
    def _():
        wide_ref[2 * ROWS :] = jnp.zeros((SIDE * SIDE, 3 * CHANNELS), bf16)

    @pl.when(core == 1)
    def _():
        put_columns(mixed_ref[0:1], 2 * ROWS)

    later = jnp.logical_not(first_chip())

    @pl.when(first_chip())
    def _():
        act_ref[0:1, inside] = act_ref[FRAMES : FRAMES + 1, inside]
        act_ref[1:2, inside] = act_ref[FRAMES : FRAMES + 1, inside]

    @pl.when(later & (core == 0))
    def _():
        act_ref[0:FRAMES, inside] = activation(mixed_ref[...])

    @pl.when(later & (core == 1))
    def _():
        act_ref[0:FRAMES, inside] = jnp.zeros((FRAMES, SIDE, SIDE, CHANNELS), bf16)

    def send(j, begin):
        for own, start, stop in ((0, 3 * j, min(3 * j + 3, TAPS)), (1, max(3 * j - 2, 0), 3 * j + 1)):

            @pl.when(core == own)
            def _(start=start, stop=stop):
                rows = slice(start * CHANNELS, stop * CHANNELS)
                copy = pltpu.make_async_copy(out_ref.at[rows], out_hbm.at[rows], sems.at[j])
                copy.start() if begin else copy.wait()

    def send_blank(begin):
        @pl.when(core == 1)
        def _():
            rows = slice(OWNED - CHANNELS, OWNED)
            copy = pltpu.make_async_copy(out_ref.at[rows], out_hbm.at[rows], sems.at[5])
            copy.start() if begin else copy.wait()

    @pl.when(core == 1)
    def _():
        out_ref[OWNED - CHANNELS :] = jnp.zeros((CHANNELS, CHANNELS), bf16)

    send_blank(True)
    for j in range(5):
        q = 4 * core + j
        a, b = q // 3, q % 3
        x = act_ref[pl.ds(a, 5), pl.ds(b, SIDE)].reshape(5 * SIDE * SIDE, CHANNELS)
        y = lax.dot_general(
            x, wide_ref[...], (((0,), (0,)), ((), ())), preferred_element_type=f32
        ).astype(bf16)
        for c in range(3):
            value = y[:, c * CHANNELS : (c + 1) * CHANNELS]
            at = j * 3 + c

            def put(value=value, at=at):
                rows = pl.ds(pl.multiple_of((at - 2 * core) * CHANNELS, CHANNELS), CHANNELS)
                out_ref[rows] = value

            if at < 2:
                pl.when(core == 0)(put)
            elif at >= TAPS:
                pl.when(core == 1)(put)
            else:
                put()
        send(j, True)
    send_blank(False)
    for j in range(5):
        send(j, False)


def data_grad_kernel(
    both_ref, partner_ref, mixed_ref, norm_ref, weight_hbm,
    pre_ref, small_ref, pad_ref, wide_ref, weight_ref, sem,
):
    load = pltpu.make_async_copy(weight_hbm, weight_ref, sem)
    load.start()
    core = lax.axis_index("core")
    inside = slice(1, SIDE + 1)
    blank_edges(pad_ref)
    pad_ref[0:FRAMES, inside] = both_ref[FRAMES:]

    @pl.when(core == 0)
    def _():
        pad_ref[FRAMES:, inside] = partner_ref[FRAMES:]

    @pl.when(core == 1)
    def _():
        pad_ref[FRAMES:, inside] = mixed_ref[...]

    def slab(frame, count):
        return jnp.concatenate(
            [
                pad_ref[frame : frame + count, 2 - b : 2 - b + SIDE].reshape(-1, CHANNELS)
                for b in range(3)
            ],
            axis=1,
        )

    def taps(a):
        return jnp.concatenate(
            [weight_ref[a, b].reshape(3 * CHANNELS, CHANNELS) for b in range(3)], axis=1
        )

    def product(x, w):
        return lax.dot_general(x, w, (((1,), (1,)), ((), ())), preferred_element_type=f32)

    load.wait()
    wide_ref[...] = (
        product(slab(2, FRAMES), taps(0))
        + product(slab(1, FRAMES), taps(1))
        + product(slab(0, FRAMES), taps(2))
    )

    @pl.when(first_chip() & (core == 0))
    def _():
        plane = SIDE * SIDE
        wide_ref[0:plane] = wide_ref[0:plane] + (
            product(slab(0, 1), taps(0))
            + (product(slab(1, 1), taps(0)) + product(slab(0, 1), taps(1)))
        )

    act_grad = (
        next_column(wide_ref[:, 0:CHANNELS])
        + wide_ref[:, CHANNELS : 2 * CHANNELS]
        + last_column(wide_ref[:, 2 * CHANNELS :])
    )
    values = both_ref[0:FRAMES].reshape(ROWS, CHANNELS).astype(f32)
    normed = (values - norm_ref[0:1]) * norm_ref[1:2]
    shifted = normed * norm_ref[2:3] + norm_ref[3:4]
    sig = 1.0 / (1.0 + jnp.exp(-shifted))
    pre = act_grad * sig * (1.0 + shifted * (1.0 - sig))
    pre_ref[...] = pre
    small_ref[...] = jnp.concatenate(
        [
            jnp.sum(pre * normed, axis=0, keepdims=True),
            jnp.sum(pre, axis=0, keepdims=True),
            jnp.zeros((6, CHANNELS), f32),
        ],
        axis=0,
    )


def sum_kernel(parts_ref, small_ref, other_ref, out_ref):
    total = parts_ref[0].astype(f32)
    for i in range(1, PARTS):
        total = total + parts_ref[i].astype(f32)
    total = jnp.concatenate([total, small_ref[...] + other_ref[...]], axis=0)
    out_ref[...] = jnp.broadcast_to(total[None], out_ref.shape)


def spread_kernel(parts_ref, out_hbm, clip_ref, some_ref, sems):
    total = jnp.sum(parts_ref[...], axis=0)
    clip_ref[...] = jnp.sum(parts_ref[pl.ds(4 * lax.axis_index("y_hi"), 4), CHUNK:], axis=0)
    small = total[CHUNK : CHUNK + 2]
    high = small.astype(bf16).astype(f32)
    mine = jnp.concatenate(
        [total[0:CHUNK], high, small - high, jnp.zeros((4, CHANNELS), f32)], axis=0
    ).astype(bf16)
    some_ref[...] = jnp.broadcast_to(mine[None], some_ref.shape)
    copies = [
        pltpu.make_async_copy(some_ref, out_hbm.at[4 * i : 4 * i + 4], sems.at[i])
        for i in range(PARTS // 4)
    ]
    for copy in copies:
        copy.start()
    for copy in copies:
        copy.wait()


def input_grad_kernel(both_ref, pre_ref, norm_ref, clip_ref, other_ref, out_ref):
    clip = jnp.where(lax.axis_index("core") == 0, clip_ref[...], other_ref[...])
    means = group_mean(clip * norm_ref[2:3])
    values = both_ref[0:FRAMES].reshape(ROWS, CHANNELS).astype(f32)
    normed = (values - norm_ref[0:1]) * norm_ref[1:2]
    grad = norm_ref[1:2] * (pre_ref[...] * norm_ref[2:3] - means[1:2] - normed * means[0:1])
    out_ref[...] = grad.astype(bf16).reshape(out_ref.shape)


PIECES = 4


def write_half(core, total_ref, weight_hbm, half_ref, sems):
    chunks = PARTS // PIECES
    rows = chunks * CHUNK
    end = 27 * CHANNELS - OWNED
    for i in range(PIECES):
        at = i * rows
        half_ref[at : at + rows] = (
            total_ref[i * chunks : (i + 1) * chunks, 0:CHUNK].astype(f32).reshape(rows, CHANNELS)
            * SCALE
        )
        last = min(rows, end - at)

        @pl.when(core == 0)
        def _(i=i, at=at):
            pltpu.make_async_copy(
                half_ref.at[at : at + rows], weight_hbm.at[at : at + rows], sems.at[i]
            ).start()

        @pl.when(core == 1)
        def _(i=i, at=at, last=last):
            pltpu.make_async_copy(
                half_ref.at[at : at + last],
                weight_hbm.at[OWNED + at : OWNED + at + last],
                sems.at[i],
            ).start()

    for i in range(PIECES):
        at = i * rows
        last = min(rows, end - at)

        @pl.when(core == 0)
        def _(i=i, at=at):
            pltpu.make_async_copy(
                half_ref.at[at : at + rows], weight_hbm.at[at : at + rows], sems.at[i]
            ).wait()

        @pl.when(core == 1)
        def _(i=i, at=at, last=last):
            pltpu.make_async_copy(
                half_ref.at[at : at + last],
                weight_hbm.at[OWNED + at : OWNED + at + last],
                sems.at[i],
            ).wait()


def final_own_kernel(own_ref, weight_hbm, half_ref, sems):
    write_half(lax.axis_index("core"), own_ref, weight_hbm, half_ref, sems)


def final_other_kernel(
    own_ref, other_ref, started_hbm, weight_hbm, gain_hbm, bias_hbm,
    half_ref, sems, gain_ref, bias_ref, small_sems,
):
    core = lax.axis_index("core")

    def put_small(ref):
        small = ref[0, CHUNK:].astype(f32)
        for m in range(1, PARTS):
            small = small + ref[m, CHUNK:].astype(f32)
        gain_ref[...] = (small[0:1] + small[2:3]) * SCALE
        bias_ref[...] = (small[1:2] + small[3:4]) * SCALE

    pl.when(core == 0)(lambda: put_small(own_ref))
    pl.when(core == 1)(lambda: put_small(other_ref))
    copies = [
        pltpu.make_async_copy(gain_ref, gain_hbm, small_sems.at[0]),
        pltpu.make_async_copy(bias_ref, bias_hbm, small_sems.at[1]),
    ]
    for copy in copies:
        copy.start()
    write_half(1 - core, other_ref, weight_hbm, half_ref, sems)
    for copy in copies:
        copy.wait()


def exchange(x, groups):
    return lax.all_to_all(x, ALL, 0, 0, axis_index_groups=groups, tiled=True)


def body(inputs, cotangent, conv_weight, norm_gain, norm_bias):
    x, cot = inputs[0], cotangent[0]
    swap = [(0, 1), (1, 0)]
    frames = (FRAMES, SIDE, SIDE, CHANNELS)
    one_row = ((1, CHANNELS), f32)

    both, mixed, stats = call(
        load_kernel,
        [1, 1, 1, 1],
        [((2 * FRAMES, SIDE, SIDE, CHANNELS), bf16), (frames, bf16), ((8, 8, CHANNELS), f32)],
        [
            pltpu.VMEM(frames, bf16),
            pltpu.VMEM(frames, bf16),
            pltpu.VMEM((1, CHANNELS), f32),
            pltpu.VMEM((1, CHANNELS), f32),
            pltpu.SemaphoreType.DMA((7,)),
        ],
        bytes_accessed=1 << 18,
        vmem=60,
        far_outs=(0, 1),
    )(x, cot, norm_gain[None], norm_bias[None])
    stats = lax.all_to_all(stats, CTX, 0, 0, tiled=True)
    mixed = lax.ppermute(
        mixed, CTX, [(1, 2), (3, 4), (5, 6), (2, 1), (4, 3), (6, 5)]
    )
    partner = lax.ppermute(both, "core", swap)
    (norm,) = call(
        norm_kernel, [0], [((8, CHANNELS), f32)], bytes_accessed=1 << 19, flops=1 << 34
    )(stats)
    (buffer,) = call(
        taps_kernel,
        [0] * 4,
        [((OWNED, CHANNELS), bf16)],
        [
            pltpu.VMEM((OWNED, CHANNELS), bf16),
            pltpu.VMEM((3 * FRAMES + 1, SIDE + 2, SIDE, CHANNELS), bf16),
            pltpu.VMEM((5 * SIDE * SIDE, 3 * CHANNELS), bf16),
            pltpu.SemaphoreType.DMA((6,)),
        ],
        far_outs=(0,),
        flops=4 * ROWS * 15 * CHANNELS * CHANNELS,
        bytes_accessed=1 << 20,
    )(both, partner, mixed, norm)
    parts = exchange(buffer.reshape(PARTS, CHUNK, CHANNELS), EXCHANGE)
    pre, small = call(
        data_grad_kernel,
        [0] * 4 + [1],
        [((ROWS, CHANNELS), f32), ((8, CHANNELS), f32)],
        [
            pltpu.VMEM((2 * FRAMES, SIDE + 2, SIDE, CHANNELS), bf16),
            pltpu.VMEM((ROWS, 3 * CHANNELS), f32),
            pltpu.VMEM((3, 3, 3, CHANNELS, CHANNELS), bf16),
            pltpu.SemaphoreType.DMA,
        ],
        flops=2 * ROWS * 27 * CHANNELS * CHANNELS,
        bytes_accessed=2 << 20,
    )(both, partner, mixed, norm, conv_weight)
    other_small = lax.ppermute(small, "core", swap)
    (one,) = call(sum_kernel, [0] * 3, [((8, CHUNK + 8, CHANNELS), f32)], bytes_accessed=1 << 19)(
        parts, small, other_small
    )
    spread, clip = call(
        spread_kernel,
        [0],
        [((PARTS, CHUNK + 8, CHANNELS), bf16), ((8, CHANNELS), f32)],
        [pltpu.VMEM((4, CHUNK + 8, CHANNELS), bf16), pltpu.SemaphoreType.DMA((PARTS // 4,))],
        far_outs=(0,),
        bytes_accessed=1 << 19,
    )(exchange(one, COLUMN))
    own_total = exchange(spread, EXCHANGE)
    other_clip = lax.ppermute(clip, "core", [(0, 1)])
    (input_grad,) = call(input_grad_kernel, [0] * 5, [(frames, bf16)], bytes_accessed=1 << 19)(
        both, pre, norm, clip, other_clip
    )
    own_total, input_grad = lax.optimization_barrier((own_total, input_grad))
    other_total = lax.ppermute(own_total, "core", swap)
    scratch = [pltpu.VMEM((OWNED, CHANNELS), f32), pltpu.SemaphoreType.DMA((PIECES,))]
    (started,) = call(
        final_own_kernel,
        [0],
        [((27 * CHANNELS, CHANNELS), f32)],
        scratch,
        bytes_accessed=2 << 20,
        far_outs=(0,),
    )(own_total)
    weight_grad, gain_grad, bias_grad = call(
        final_other_kernel,
        [0, 0, 1],
        [((27 * CHANNELS, CHANNELS), f32), one_row, one_row],
        scratch
        + [
            pltpu.VMEM((1, CHANNELS), f32),
            pltpu.VMEM((1, CHANNELS), f32),
            pltpu.SemaphoreType.DMA((2,)),
        ],
        bytes_accessed=2 << 20,
        far_outs=(0, 1, 2),
        aliases={2: 0},
    )(own_total, other_total, started)
    return (
        input_grad[None],
        weight_grad.reshape(3, 3, 3, CHANNELS, CHANNELS),
        gain_grad[0],
        bias_grad[0],
    )


def solution(mesh):
    fine = jax.sharding.Mesh(
        mesh.devices.reshape(8, 2, 4, 4, 2), ("z", "y_hi", "x", "y_lo", "core")
    )
    whole = P(DP, CTX, None, None, None)
    return jax.shard_map(
        body,
        mesh=fine,
        in_specs=(whole, whole, P(), P(), P()),
        out_specs=(whole, P(), P(), P()),
        check_vma=False,
    )
```

```python
import functools

import jax
import jax.numpy as jnp
from jax import lax
from jax.experimental import pallas as pl
from jax.experimental.pallas import tpu as pltpu
from jax.sharding import PartitionSpec as P

GROUPS = 32
CHANNELS = 128
SIDE = 16
FRAMES = 2
ROWS = FRAMES * SIDE * SIDE
EPSILON = 1e-06
TAPS = 14
OWNED = TAPS * CHANNELS
PARTS = 32
CHUNK = OWNED // PARTS

ALL = ("z", "y_hi", "x", "y_lo", "core")
DP = ("z", "y_hi", "x")
CTX = ("y_lo", "core")
CELLS = 64 * 8 * ROWS
MEMBERS = 8 * ROWS * (CHANNELS // GROUPS)
SCALE = CELLS**-0.5

f32 = jnp.float32
bf16 = jnp.bfloat16


def index(z, y, x, core):
    return ((z * 2 + y // 4) * 4 + x) * 8 + (y % 4) * 2 + core


EXCHANGE = [[index(z, y, x, 0) for z in range(8) for x in range(4)] for y in range(8)] + [
    [index(z, y, x, 1) for y in range(8) for x in range(4)] for z in range(8)
]


COLUMN = [[index(z, y, x, 0) for y in range(8)] for z in range(8) for x in range(4)] + [
    [index(z, y, x, 1) for z in range(8)] for y in range(8) for x in range(4)
]


def call(
    kernel, ins, outs, scratch=(), flops=0, bytes_accessed=0, vmem=32, far_outs=(), aliases=None
):
    return pl.pallas_call(
        kernel,
        out_shape=[jax.ShapeDtypeStruct(s, d) for s, d in outs],
        in_specs=[pl.BlockSpec(memory_space=pltpu.HBM if i else pltpu.VMEM) for i in ins],
        out_specs=[
            pl.BlockSpec(memory_space=pltpu.HBM if i in far_outs else pltpu.VMEM)
            for i in range(len(outs))
        ],
        input_output_aliases=aliases or {},
        scratch_shapes=list(scratch),
        compiler_params=pltpu.CompilerParams(vmem_limit_bytes=vmem << 20),
        cost_estimate=pl.CostEstimate(
            flops=flops, bytes_accessed=bytes_accessed, transcendentals=0
        ),
    )


def column(rows):
    return lax.broadcasted_iota(jnp.int32, (rows, CHANNELS), 0) % SIDE


def next_column(x):
    return jnp.where(column(x.shape[0]) == SIDE - 1, 0.0, pltpu.roll(x, x.shape[0] - 1, 0))


def last_column(x):
    return jnp.where(column(x.shape[0]) == 0, 0.0, pltpu.roll(x, 1, 0))


def group_mean(x):
    place = lax.broadcasted_iota(jnp.int32, x.shape, 1) % (CHANNELS // GROUPS)
    total = x
    for d in range(1, CHANNELS // GROUPS):
        total = total + jnp.where(place >= d, pltpu.roll(x, d, 1), 0.0)
        total = total + jnp.where(
            place < CHANNELS // GROUPS - d, pltpu.roll(x, CHANNELS - d, 1), 0.0
        )
    return total / MEMBERS


def first_chip():
    return lax.axis_index("y_lo") == 0


def load_kernel(
    x_hbm, cot_hbm, gain_hbm, bias_hbm, both_ref, mixed_ref, stats_ref, gain_ref, bias_ref, sems
):
    copies = [
        pltpu.make_async_copy(src, dst, sems.at[i])
        for i, (src, dst) in enumerate(
            [
                (x_hbm, both_ref.at[0:FRAMES]),
                (cot_hbm, both_ref.at[FRAMES:]),
                (gain_hbm, gain_ref),
                (bias_hbm, bias_ref),
            ]
        )
    ]
    for copy in copies:
        copy.start()
    copies[0].wait()
    values = both_ref[0:FRAMES].reshape(ROWS, CHANNELS).astype(f32)
    sums = [
        jnp.sum(values, axis=0, keepdims=True),
        jnp.sum(values * values, axis=0, keepdims=True),
    ]
    for copy in copies[1:]:
        copy.wait()
    sums = jnp.concatenate(
        sums + [gain_ref[...], bias_ref[...], jnp.zeros((4, CHANNELS), f32)], axis=0
    )
    stats_ref[...] = jnp.broadcast_to(sums[None], stats_ref.shape)
    core = lax.axis_index("core")

    @pl.when(core == 0)
    def _():
        mixed_ref[...] = both_ref[FRAMES:]

    @pl.when(core == 1)
    def _():
        mixed_ref[...] = both_ref[0:FRAMES]


def norm_kernel(stats_ref, norm_ref):
    means = group_mean(jnp.sum(stats_ref[...], axis=0))
    average = means[0:1]
    spread = means[1:2] - average * average
    norm_ref[...] = jnp.concatenate(
        [average, lax.rsqrt(spread + EPSILON), stats_ref[0, 2:4], jnp.zeros((4, CHANNELS), f32)],
        axis=0,
    )


def blank_edges(pad_ref):
    blank = jnp.zeros((pad_ref.shape[0], 1, SIDE, CHANNELS), bf16)
    pad_ref[:, 0:1] = blank
    pad_ref[:, SIDE + 1 : SIDE + 2] = blank


def taps_kernel(
    both_ref, partner_ref, mixed_ref, norm_ref, out_hbm, out_ref, act_ref, wide_ref, sems
):
    core = lax.axis_index("core")
    inside = slice(1, SIDE + 1)

    def activation(x):
        values = x.reshape(-1, CHANNELS).astype(f32)
        shifted = (values - norm_ref[0:1]) * norm_ref[1:2] * norm_ref[2:3] + norm_ref[3:4]
        return (shifted / (1.0 + jnp.exp(-shifted))).astype(bf16).reshape(x.shape)

    def put_columns(cot, start):
        cot = cot.reshape(-1, CHANNELS)
        rows = pl.ds(pl.multiple_of(start, SIDE * SIDE), cot.shape[0])
        cot32 = cot.astype(f32)
        wide_ref[rows, 0:CHANNELS] = next_column(cot32).astype(bf16)
        wide_ref[rows, CHANNELS : 2 * CHANNELS] = cot
        wide_ref[rows, 2 * CHANNELS :] = last_column(cot32).astype(bf16)

    blank_edges(act_ref)
    for source, at in ((both_ref, core), (partner_ref, 1 - core)):
        act_ref[pl.ds(FRAMES + FRAMES * at, FRAMES), inside] = activation(source[0:FRAMES])
        put_columns(source[FRAMES:], at * ROWS)

    @pl.when(core == 1)
    def _():
        put_columns(mixed_ref[0:1], 2 * ROWS)

    later = jnp.logical_not(first_chip())

    @pl.when(first_chip())
    def _():
        act_ref[0:1, inside] = act_ref[FRAMES : FRAMES + 1, inside]
        act_ref[1:2, inside] = act_ref[FRAMES : FRAMES + 1, inside]

    @pl.when(later & (core == 0))
    def _():
        act_ref[0:FRAMES, inside] = activation(mixed_ref[...])

    @pl.when(later & (core == 1))
    def _():
        act_ref[0:FRAMES, inside] = jnp.zeros((FRAMES, SIDE, SIDE, CHANNELS), bf16)

    def send(j, begin):
        for own, start, stop in ((0, 3 * j, min(3 * j + 3, TAPS)), (1, max(3 * j - 2, 0), 3 * j + 1)):

            @pl.when(core == own)
            def _(start=start, stop=stop):
                rows = slice(start * CHANNELS, stop * CHANNELS)
                copy = pltpu.make_async_copy(out_ref.at[rows], out_hbm.at[rows], sems.at[j])
                copy.start() if begin else copy.wait()

    def send_blank(begin):
        @pl.when(core == 1)
        def _():
            rows = slice(OWNED - CHANNELS, OWNED)
            copy = pltpu.make_async_copy(out_ref.at[rows], out_hbm.at[rows], sems.at[5])
            copy.start() if begin else copy.wait()

    @pl.when(core == 1)
    def _():
        out_ref[OWNED - CHANNELS :] = jnp.zeros((CHANNELS, CHANNELS), bf16)

    send_blank(True)
    def product(q, frames):
        a, b = q // 3, q % 3
        x = act_ref[pl.ds(a, frames), pl.ds(b, SIDE)].reshape(frames * SIDE * SIDE, CHANNELS)
        return lax.dot_general(
            x,
            wide_ref[0 : frames * SIDE * SIDE],
            (((0,), (0,)), ((), ())),
            preferred_element_type=f32,
        ).astype(bf16)

    def put(y, slot, c):
        out_ref[pl.ds(pl.multiple_of(slot * CHANNELS, CHANNELS), CHANNELS)] = y[
            :, c * CHANNELS : (c + 1) * CHANNELS
        ]

    for j in range(5):
        if j < 2:

            @pl.when(core == 0)
            def _(j=j):
                y = product(j, 2 * FRAMES)
                for c in range(3):
                    put(y, 3 * j + c, c)

            @pl.when(core == 1)
            def _(j=j):
                y = product(4 + j, 2 * FRAMES + 1)
                for c in range(3):
                    if 3 * j + c >= 2:
                        put(y, 3 * j + c - 2, c)

        else:
            y = product(4 * core + j, 2 * FRAMES)
            for c in range(3):
                if 3 * j + c < TAPS:
                    put(y, 3 * j + c - 2 * core, c)
                else:
                    pl.when(core == 1)(lambda y=y, slot=3 * j + c - 2, c=c: put(y, slot, c))
        send(j, True)
    send_blank(False)
    for j in range(5):
        send(j, False)


def data_grad_kernel(
    both_ref, partner_ref, mixed_ref, norm_ref, weight_hbm,
    pre_ref, small_ref, pad_ref, wide_ref, weight_ref, sem,
):
    load = pltpu.make_async_copy(weight_hbm, weight_ref, sem)
    load.start()
    core = lax.axis_index("core")
    inside = slice(1, SIDE + 1)
    blank_edges(pad_ref)
    pad_ref[0:FRAMES, inside] = both_ref[FRAMES:]

    @pl.when(core == 0)
    def _():
        pad_ref[FRAMES:, inside] = partner_ref[FRAMES:]

    @pl.when(core == 1)
    def _():
        pad_ref[FRAMES:, inside] = mixed_ref[...]

    def slab(frame, count):
        return jnp.concatenate(
            [
                pad_ref[frame : frame + count, 2 - b : 2 - b + SIDE].reshape(-1, CHANNELS)
                for b in range(3)
            ],
            axis=1,
        )

    def taps(a):
        return jnp.concatenate(
            [weight_ref[a, b].reshape(3 * CHANNELS, CHANNELS) for b in range(3)], axis=1
        )

    def product(x, w):
        return lax.dot_general(x, w, (((1,), (1,)), ((), ())), preferred_element_type=f32)

    load.wait()
    wide_ref[...] = (
        product(slab(2, FRAMES), taps(0))
        + product(slab(1, FRAMES), taps(1))
        + product(slab(0, FRAMES), taps(2))
    )

    @pl.when(first_chip() & (core == 0))
    def _():
        plane = SIDE * SIDE
        wide_ref[0:plane] = wide_ref[0:plane] + (
            product(slab(0, 1), taps(0))
            + (product(slab(1, 1), taps(0)) + product(slab(0, 1), taps(1)))
        )

    act_grad = (
        next_column(wide_ref[:, 0:CHANNELS])
        + wide_ref[:, CHANNELS : 2 * CHANNELS]
        + last_column(wide_ref[:, 2 * CHANNELS :])
    )
    values = both_ref[0:FRAMES].reshape(ROWS, CHANNELS).astype(f32)
    normed = (values - norm_ref[0:1]) * norm_ref[1:2]
    shifted = normed * norm_ref[2:3] + norm_ref[3:4]
    sig = 1.0 / (1.0 + jnp.exp(-shifted))
    pre = act_grad * sig * (1.0 + shifted * (1.0 - sig))
    pre_ref[...] = pre
    small_ref[...] = jnp.concatenate(
        [
            jnp.sum(pre * normed, axis=0, keepdims=True),
            jnp.sum(pre, axis=0, keepdims=True),
            jnp.zeros((6, CHANNELS), f32),
        ],
        axis=0,
    )


def sum_kernel(parts_ref, small_ref, other_ref, out_ref):
    total = parts_ref[0].astype(f32)
    for i in range(1, PARTS):
        total = total + parts_ref[i].astype(f32)
    total = jnp.concatenate([total, small_ref[...] + other_ref[...]], axis=0)
    out_ref[...] = jnp.broadcast_to(total[None], out_ref.shape)


def spread_kernel(parts_ref, out_hbm, clip_ref, some_ref, sems):
    total = jnp.sum(parts_ref[...], axis=0)
    clip_ref[...] = jnp.sum(parts_ref[pl.ds(4 * lax.axis_index("y_hi"), 4), CHUNK:], axis=0)
    small = total[CHUNK : CHUNK + 2]
    high = small.astype(bf16).astype(f32)
    mine = jnp.concatenate(
        [total[0:CHUNK], high, small - high, jnp.zeros((4, CHANNELS), f32)], axis=0
    ).astype(bf16)
    some_ref[...] = jnp.broadcast_to(mine[None], some_ref.shape)
    copies = [
        pltpu.make_async_copy(some_ref, out_hbm.at[4 * i : 4 * i + 4], sems.at[i])
        for i in range(PARTS // 4)
    ]
    for copy in copies:
        copy.start()
    for copy in copies:
        copy.wait()


def input_grad_kernel(both_ref, pre_ref, norm_ref, clip_ref, other_ref, out_ref):
    clip = jnp.where(lax.axis_index("core") == 0, clip_ref[...], other_ref[...])
    means = group_mean(clip * norm_ref[2:3])
    values = both_ref[0:FRAMES].reshape(ROWS, CHANNELS).astype(f32)
    normed = (values - norm_ref[0:1]) * norm_ref[1:2]
    grad = norm_ref[1:2] * (pre_ref[...] * norm_ref[2:3] - means[1:2] - normed * means[0:1])
    out_ref[...] = grad.astype(bf16).reshape(out_ref.shape)


PIECES = 4


def write_half(core, total_ref, weight_hbm, half_ref, sems):
    chunks = PARTS // PIECES
    rows = chunks * CHUNK
    end = 27 * CHANNELS - OWNED
    for i in range(PIECES):
        at = i * rows
        half_ref[at : at + rows] = (
            total_ref[i * chunks : (i + 1) * chunks, 0:CHUNK].astype(f32).reshape(rows, CHANNELS)
            * SCALE
        )
        last = min(rows, end - at)

        @pl.when(core == 0)
        def _(i=i, at=at):
            pltpu.make_async_copy(
                half_ref.at[at : at + rows], weight_hbm.at[at : at + rows], sems.at[i]
            ).start()

        @pl.when(core == 1)
        def _(i=i, at=at, last=last):
            pltpu.make_async_copy(
                half_ref.at[at : at + last],
                weight_hbm.at[OWNED + at : OWNED + at + last],
                sems.at[i],
            ).start()

    for i in range(PIECES):
        at = i * rows
        last = min(rows, end - at)

        @pl.when(core == 0)
        def _(i=i, at=at):
            pltpu.make_async_copy(
                half_ref.at[at : at + rows], weight_hbm.at[at : at + rows], sems.at[i]
            ).wait()

        @pl.when(core == 1)
        def _(i=i, at=at, last=last):
            pltpu.make_async_copy(
                half_ref.at[at : at + last],
                weight_hbm.at[OWNED + at : OWNED + at + last],
                sems.at[i],
            ).wait()


def final_own_kernel(own_ref, weight_hbm, half_ref, sems):
    write_half(lax.axis_index("core"), own_ref, weight_hbm, half_ref, sems)


def final_other_kernel(
    own_ref, other_ref, started_hbm, weight_hbm, gain_hbm, bias_hbm,
    half_ref, sems, gain_ref, bias_ref, small_sems,
):
    core = lax.axis_index("core")

    def put_small(ref):
        small = ref[0, CHUNK:].astype(f32)
        for m in range(1, PARTS):
            small = small + ref[m, CHUNK:].astype(f32)
        gain_ref[...] = (small[0:1] + small[2:3]) * SCALE
        bias_ref[...] = (small[1:2] + small[3:4]) * SCALE

    pl.when(core == 0)(lambda: put_small(own_ref))
    pl.when(core == 1)(lambda: put_small(other_ref))
    copies = [
        pltpu.make_async_copy(gain_ref, gain_hbm, small_sems.at[0]),
        pltpu.make_async_copy(bias_ref, bias_hbm, small_sems.at[1]),
    ]
    for copy in copies:
        copy.start()
    write_half(1 - core, other_ref, weight_hbm, half_ref, sems)
    for copy in copies:
        copy.wait()


def exchange(x, groups):
    return lax.all_to_all(x, ALL, 0, 0, axis_index_groups=groups, tiled=True)


def body(inputs, cotangent, conv_weight, norm_gain, norm_bias):
    x, cot = inputs[0], cotangent[0]
    swap = [(0, 1), (1, 0)]
    frames = (FRAMES, SIDE, SIDE, CHANNELS)
    one_row = ((1, CHANNELS), f32)

    both, mixed, stats, _, _ = call(
        load_kernel,
        [1, 1, 1, 1],
        [((2 * FRAMES, SIDE, SIDE, CHANNELS), bf16), (frames, bf16), ((8, 8, CHANNELS), f32),
         one_row, one_row],
        [pltpu.SemaphoreType.DMA((4,))],
        bytes_accessed=1 << 18,
        vmem=60,
    )(x, cot, norm_gain[None], norm_bias[None])
    stats = lax.all_to_all(stats, CTX, 0, 0, tiled=True)
    partner = lax.ppermute(both, "core", swap)
    mixed = lax.ppermute(
        mixed, CTX, [(1, 2), (3, 4), (5, 6), (2, 1), (4, 3), (6, 5)]
    )
    (norm,) = call(
        norm_kernel, [0], [((8, CHANNELS), f32)], bytes_accessed=1 << 19, flops=1 << 34
    )(stats)
    (buffer,) = call(
        taps_kernel,
        [0] * 4,
        [((OWNED, CHANNELS), bf16)],
        [
            pltpu.VMEM((OWNED, CHANNELS), bf16),
            pltpu.VMEM((3 * FRAMES, SIDE + 2, SIDE, CHANNELS), bf16),
            pltpu.VMEM((5 * SIDE * SIDE, 3 * CHANNELS), bf16),
            pltpu.SemaphoreType.DMA((6,)),
        ],
        far_outs=(0,),
        flops=4 * ROWS * 15 * CHANNELS * CHANNELS,
        bytes_accessed=1 << 20,
    )(both, partner, mixed, norm)
    parts = exchange(buffer.reshape(PARTS, CHUNK, CHANNELS), EXCHANGE)
    pre, small = call(
        data_grad_kernel,
        [0] * 4 + [1],
        [((ROWS, CHANNELS), f32), ((8, CHANNELS), f32)],
        [
            pltpu.VMEM((2 * FRAMES, SIDE + 2, SIDE, CHANNELS), bf16),
            pltpu.VMEM((ROWS, 3 * CHANNELS), f32),
            pltpu.VMEM((3, 3, 3, CHANNELS, CHANNELS), bf16),
            pltpu.SemaphoreType.DMA,
        ],
        flops=2 * ROWS * 27 * CHANNELS * CHANNELS,
        bytes_accessed=2 << 20,
    )(both, partner, mixed, norm, conv_weight)
    other_small = lax.ppermute(small, "core", swap)
    (one,) = call(sum_kernel, [0] * 3, [((8, CHUNK + 8, CHANNELS), f32)], bytes_accessed=1 << 19)(
        parts, small, other_small
    )
    spread, clip = call(
        spread_kernel,
        [0],
        [((PARTS, CHUNK + 8, CHANNELS), bf16), ((8, CHANNELS), f32)],
        [pltpu.VMEM((4, CHUNK + 8, CHANNELS), bf16), pltpu.SemaphoreType.DMA((PARTS // 4,))],
        far_outs=(0,),
        bytes_accessed=1 << 19,
    )(exchange(one, COLUMN))
    own_total = exchange(spread, EXCHANGE)
    other_clip = lax.ppermute(clip, "core", [(0, 1)])
    (input_grad,) = call(input_grad_kernel, [0] * 5, [(frames, bf16)], bytes_accessed=1 << 19)(
        both, pre, norm, clip, other_clip
    )
    own_total, input_grad = lax.optimization_barrier((own_total, input_grad))
    other_total = lax.ppermute(own_total, "core", swap)
    scratch = [pltpu.VMEM((OWNED, CHANNELS), f32), pltpu.SemaphoreType.DMA((PIECES,))]
    (started,) = call(
        final_own_kernel,
        [0],
        [((27 * CHANNELS, CHANNELS), f32)],
        scratch,
        bytes_accessed=2 << 20,
        far_outs=(0,),
    )(own_total)
    weight_grad, gain_grad, bias_grad = call(
        final_other_kernel,
        [0, 0, 1],
        [((27 * CHANNELS, CHANNELS), f32), one_row, one_row],
        scratch
        + [
            pltpu.VMEM((1, CHANNELS), f32),
            pltpu.VMEM((1, CHANNELS), f32),
            pltpu.SemaphoreType.DMA((2,)),
        ],
        bytes_accessed=2 << 20,
        far_outs=(0, 1, 2),
        aliases={2: 0},
    )(own_total, other_total, started)
    return (
        input_grad[None],
        weight_grad.reshape(3, 3, 3, CHANNELS, CHANNELS),
        gain_grad[0],
        bias_grad[0],
    )


def solution(mesh):
    fine = jax.sharding.Mesh(
        mesh.devices.reshape(8, 2, 4, 4, 2), ("z", "y_hi", "x", "y_lo", "core")
    )
    whole = P(DP, CTX, None, None, None)
    return jax.shard_map(
        body,
        mesh=fine,
        in_specs=(whole, whole, P(), P(), P()),
        out_specs=(whole, P(), P(), P()),
        check_vma=False,
    )
```

```python
import functools

import jax
import jax.numpy as jnp
from jax import lax
from jax.experimental import pallas as pl
from jax.experimental.pallas import tpu as pltpu
from jax.sharding import PartitionSpec as P

GROUPS = 32
CHANNELS = 128
SIDE = 16
FRAMES = 2
ROWS = FRAMES * SIDE * SIDE
EPSILON = 1e-06
TAPS = 14
OWNED = TAPS * CHANNELS
PARTS = 32
CHUNK = OWNED // PARTS

ALL = ("z", "y_hi", "x", "y_lo", "core")
DP = ("z", "y_hi", "x")
CTX = ("y_lo", "core")
CELLS = 64 * 8 * ROWS
MEMBERS = 8 * ROWS * (CHANNELS // GROUPS)
SCALE = CELLS**-0.5

f32 = jnp.float32
bf16 = jnp.bfloat16


def index(z, y, x, core):
    return ((z * 2 + y // 4) * 4 + x) * 8 + (y % 4) * 2 + core


CLIP = [[8 * d + c for c in reversed(range(8))] for d in range(64)]

EXCHANGE = [
    [index(z, y, x, 0) for z in reversed(range(8)) for x in range(4)] for y in range(8)
] + [[index(z, y, x, 1) for y in reversed(range(8)) for x in range(4)] for z in range(8)]


COLUMN = [[index(z, y, x, 0) for y in reversed(range(8))] for z in range(8) for x in range(4)] + [
    [index(z, y, x, 1) for z in reversed(range(8))] for y in range(8) for x in range(4)
]


def call(
    kernel, ins, outs, scratch=(), flops=0, bytes_accessed=0, vmem=32, far_outs=(), aliases=None
):
    return pl.pallas_call(
        kernel,
        out_shape=[jax.ShapeDtypeStruct(s, d) for s, d in outs],
        in_specs=[pl.BlockSpec(memory_space=pltpu.HBM if i else pltpu.VMEM) for i in ins],
        out_specs=[
            pl.BlockSpec(memory_space=pltpu.HBM if i in far_outs else pltpu.VMEM)
            for i in range(len(outs))
        ],
        input_output_aliases=aliases or {},
        scratch_shapes=list(scratch),
        compiler_params=pltpu.CompilerParams(vmem_limit_bytes=vmem << 20),
        cost_estimate=pl.CostEstimate(
            flops=flops, bytes_accessed=bytes_accessed, transcendentals=0
        ),
    )


def column(rows):
    return lax.broadcasted_iota(jnp.int32, (rows, CHANNELS), 0) % SIDE


def next_column(x):
    return jnp.where(column(x.shape[0]) == SIDE - 1, 0.0, pltpu.roll(x, x.shape[0] - 1, 0))


def last_column(x):
    return jnp.where(column(x.shape[0]) == 0, 0.0, pltpu.roll(x, 1, 0))


def group_mean(x):
    place = lax.broadcasted_iota(jnp.int32, x.shape, 1) % (CHANNELS // GROUPS)
    total = x
    for d in range(1, CHANNELS // GROUPS):
        total = total + jnp.where(place >= d, pltpu.roll(x, d, 1), 0.0)
        total = total + jnp.where(
            place < CHANNELS // GROUPS - d, pltpu.roll(x, CHANNELS - d, 1), 0.0
        )
    return total / MEMBERS


def first_chip():
    return lax.axis_index("y_lo") == 0


def load_kernel(
    x_hbm, cot_hbm, gain_hbm, bias_hbm, both_ref, mixed_ref, stats_ref, gain_ref, bias_ref, sems
):
    copies = [
        pltpu.make_async_copy(src, dst, sems.at[i])
        for i, (src, dst) in enumerate(
            [
                (x_hbm, both_ref.at[0:FRAMES]),
                (cot_hbm, both_ref.at[FRAMES:]),
                (gain_hbm, gain_ref),
                (bias_hbm, bias_ref),
            ]
        )
    ]
    for copy in copies:
        copy.start()
    copies[0].wait()
    values = both_ref[0:FRAMES].reshape(ROWS, CHANNELS).astype(f32)
    sums = [
        jnp.sum(values, axis=0, keepdims=True),
        jnp.sum(values * values, axis=0, keepdims=True),
    ]
    for copy in copies[1:]:
        copy.wait()
    sums = jnp.concatenate(
        sums + [gain_ref[...], bias_ref[...], jnp.zeros((4, CHANNELS), f32)], axis=0
    )
    stats_ref[...] = jnp.broadcast_to(sums[None], stats_ref.shape)
    core = lax.axis_index("core")

    @pl.when(core == 0)
    def _():
        mixed_ref[...] = both_ref[FRAMES:]

    @pl.when(core == 1)
    def _():
        mixed_ref[...] = both_ref[0:FRAMES]


def norm_kernel(stats_ref, norm_ref):
    means = group_mean(jnp.sum(stats_ref[...], axis=0))
    average = means[0:1]
    spread = means[1:2] - average * average
    norm_ref[...] = jnp.concatenate(
        [average, lax.rsqrt(spread + EPSILON), stats_ref[0, 2:4], jnp.zeros((4, CHANNELS), f32)],
        axis=0,
    )


def blank_edges(pad_ref):
    blank = jnp.zeros((pad_ref.shape[0], 1, SIDE, CHANNELS), bf16)
    pad_ref[:, 0:1] = blank
    pad_ref[:, SIDE + 1 : SIDE + 2] = blank


def taps_kernel(
    both_ref, partner_ref, mixed_ref, norm_ref, out_hbm, out_ref, act_ref, wide_ref, sems
):
    core = lax.axis_index("core")
    inside = slice(1, SIDE + 1)

    def activation(x):
        values = x.reshape(-1, CHANNELS).astype(f32)
        shifted = (values - norm_ref[0:1]) * norm_ref[1:2] * norm_ref[2:3] + norm_ref[3:4]
        return (shifted / (1.0 + jnp.exp(-shifted))).astype(bf16).reshape(x.shape)

    def put_columns(cot, start):
        cot = cot.reshape(-1, CHANNELS)
        rows = pl.ds(pl.multiple_of(start, SIDE * SIDE), cot.shape[0])
        cot32 = cot.astype(f32)
        wide_ref[rows, 0:CHANNELS] = next_column(cot32).astype(bf16)
        wide_ref[rows, CHANNELS : 2 * CHANNELS] = cot
        wide_ref[rows, 2 * CHANNELS :] = last_column(cot32).astype(bf16)

    blank_edges(act_ref)
    for source, at in ((both_ref, core), (partner_ref, 1 - core)):
        act_ref[pl.ds(FRAMES + FRAMES * at, FRAMES), inside] = activation(source[0:FRAMES])
        put_columns(source[FRAMES:], at * ROWS)

    @pl.when(core == 1)
    def _():
        put_columns(mixed_ref[0:1], 2 * ROWS)

    later = jnp.logical_not(first_chip())

    @pl.when(first_chip())
    def _():
        act_ref[0:1, inside] = act_ref[FRAMES : FRAMES + 1, inside]
        act_ref[1:2, inside] = act_ref[FRAMES : FRAMES + 1, inside]

    @pl.when(later & (core == 0))
    def _():
        act_ref[0:FRAMES, inside] = activation(mixed_ref[...])

    @pl.when(later & (core == 1))
    def _():
        act_ref[0:FRAMES, inside] = jnp.zeros((FRAMES, SIDE, SIDE, CHANNELS), bf16)

    def send(j, begin):
        for own, start, stop in ((0, 3 * j, min(3 * j + 3, TAPS)), (1, max(3 * j - 2, 0), 3 * j + 1)):

            @pl.when(core == own)
            def _(start=start, stop=stop):
                rows = slice(start * CHANNELS, stop * CHANNELS)
                copy = pltpu.make_async_copy(out_ref.at[rows], out_hbm.at[rows], sems.at[j])
                copy.start() if begin else copy.wait()

    def send_blank(begin):
        @pl.when(core == 1)
        def _():
            rows = slice(OWNED - CHANNELS, OWNED)
            copy = pltpu.make_async_copy(out_ref.at[rows], out_hbm.at[rows], sems.at[5])
            copy.start() if begin else copy.wait()

    @pl.when(core == 1)
    def _():
        out_ref[OWNED - CHANNELS :] = jnp.zeros((CHANNELS, CHANNELS), bf16)

    send_blank(True)
    def product(q, frames):
        a, b = q // 3, q % 3
        x = act_ref[pl.ds(a, frames), pl.ds(b, SIDE)].reshape(frames * SIDE * SIDE, CHANNELS)
        return lax.dot_general(
            x,
            wide_ref[0 : frames * SIDE * SIDE],
            (((0,), (0,)), ((), ())),
            preferred_element_type=f32,
        ).astype(bf16)

    def put(y, slot, c):
        out_ref[pl.ds(pl.multiple_of(slot * CHANNELS, CHANNELS), CHANNELS)] = y[
            :, c * CHANNELS : (c + 1) * CHANNELS
        ]

    for j in range(5):
        if j < 2:

            @pl.when(core == 0)
            def _(j=j):
                y = product(j, 2 * FRAMES)
                for c in range(3):
                    put(y, 3 * j + c, c)

            @pl.when(core == 1)
            def _(j=j):
                y = product(4 + j, 2 * FRAMES + 1)
                for c in range(3):
                    if 3 * j + c >= 2:
                        put(y, 3 * j + c - 2, c)

        else:
            y = product(4 * core + j, 2 * FRAMES)
            for c in range(3):
                if 3 * j + c < TAPS:
                    put(y, 3 * j + c - 2 * core, c)
                else:
                    pl.when(core == 1)(lambda y=y, slot=3 * j + c - 2, c=c: put(y, slot, c))
        send(j, True)
    send_blank(False)
    for j in range(5):
        send(j, False)


def data_grad_kernel(
    both_ref, partner_ref, mixed_ref, norm_ref, weight_hbm,
    pre_ref, small_ref, pad_ref, wide_ref, weight_ref, sem,
):
    load = pltpu.make_async_copy(weight_hbm, weight_ref, sem)
    load.start()
    core = lax.axis_index("core")
    inside = slice(1, SIDE + 1)
    blank_edges(pad_ref)
    pad_ref[0:FRAMES, inside] = both_ref[FRAMES:]

    @pl.when(core == 0)
    def _():
        pad_ref[FRAMES:, inside] = partner_ref[FRAMES:]

    @pl.when(core == 1)
    def _():
        pad_ref[FRAMES:, inside] = mixed_ref[...]

    def slab(frame, count):
        return jnp.concatenate(
            [
                pad_ref[frame : frame + count, 2 - b : 2 - b + SIDE].reshape(-1, CHANNELS)
                for b in range(3)
            ],
            axis=1,
        )

    def taps(a):
        return jnp.concatenate(
            [weight_ref[a, b].reshape(3 * CHANNELS, CHANNELS) for b in range(3)], axis=1
        )

    def product(x, w):
        return lax.dot_general(x, w, (((1,), (1,)), ((), ())), preferred_element_type=f32)

    load.wait()
    wide_ref[...] = (
        product(slab(2, FRAMES), taps(0))
        + product(slab(1, FRAMES), taps(1))
        + product(slab(0, FRAMES), taps(2))
    )

    @pl.when(first_chip() & (core == 0))
    def _():
        plane = SIDE * SIDE
        wide_ref[0:plane] = wide_ref[0:plane] + (
            product(slab(0, 1), taps(0))
            + (product(slab(1, 1), taps(0)) + product(slab(0, 1), taps(1)))
        )

    act_grad = (
        next_column(wide_ref[:, 0:CHANNELS])
        + wide_ref[:, CHANNELS : 2 * CHANNELS]
        + last_column(wide_ref[:, 2 * CHANNELS :])
    )
    values = both_ref[0:FRAMES].reshape(ROWS, CHANNELS).astype(f32)
    normed = (values - norm_ref[0:1]) * norm_ref[1:2]
    shifted = normed * norm_ref[2:3] + norm_ref[3:4]
    sig = 1.0 / (1.0 + jnp.exp(-shifted))
    pre = act_grad * sig * (1.0 + shifted * (1.0 - sig))
    pre_ref[...] = pre
    small_ref[...] = jnp.concatenate(
        [
            jnp.sum(pre * normed, axis=0, keepdims=True),
            jnp.sum(pre, axis=0, keepdims=True),
            jnp.zeros((6, CHANNELS), f32),
        ],
        axis=0,
    )


def sum_kernel(parts_ref, small_ref, other_ref, out_ref):
    total = parts_ref[0].astype(f32)
    for i in range(1, PARTS):
        total = total + parts_ref[i].astype(f32)
    total = jnp.concatenate([total, small_ref[...] + other_ref[...]], axis=0)
    out_ref[...] = jnp.broadcast_to(total[None], out_ref.shape)


def spread_kernel(parts_ref, out_hbm, clip_ref, some_ref, sems):
    total = jnp.sum(parts_ref[...], axis=0)
    clip_ref[...] = jnp.sum(parts_ref[pl.ds(4 * (1 - lax.axis_index("y_hi")), 4), CHUNK:], axis=0)
    small = total[CHUNK : CHUNK + 2]
    high = small.astype(bf16).astype(f32)
    mine = jnp.concatenate(
        [total[0:CHUNK], high, small - high, jnp.zeros((4, CHANNELS), f32)], axis=0
    ).astype(bf16)
    some_ref[...] = jnp.broadcast_to(mine[None], some_ref.shape)
    copies = [
        pltpu.make_async_copy(some_ref, out_hbm.at[4 * i : 4 * i + 4], sems.at[i])
        for i in range(PARTS // 4)
    ]
    for copy in copies:
        copy.start()
    for copy in copies:
        copy.wait()


def input_grad_kernel(both_ref, pre_ref, norm_ref, clip_ref, other_ref, out_ref):
    clip = jnp.where(lax.axis_index("core") == 0, clip_ref[...], other_ref[...])
    means = group_mean(clip * norm_ref[2:3])
    values = both_ref[0:FRAMES].reshape(ROWS, CHANNELS).astype(f32)
    normed = (values - norm_ref[0:1]) * norm_ref[1:2]
    grad = norm_ref[1:2] * (pre_ref[...] * norm_ref[2:3] - means[1:2] - normed * means[0:1])
    out_ref[...] = grad.astype(bf16).reshape(out_ref.shape)


PIECES = 4


def write_half(core, total_ref, weight_hbm, half_ref, sems):
    chunks = PARTS // PIECES
    rows = chunks * CHUNK
    end = 27 * CHANNELS - OWNED
    for i in range(PIECES):
        at = i * rows
        half_ref[at : at + rows] = (
            total_ref[i * chunks : (i + 1) * chunks, 0:CHUNK].astype(f32).reshape(rows, CHANNELS)
            * SCALE
        )
        last = min(rows, end - at)

        @pl.when(core == 0)
        def _(i=i, at=at):
            pltpu.make_async_copy(
                half_ref.at[at : at + rows], weight_hbm.at[at : at + rows], sems.at[i]
            ).start()

        @pl.when(core == 1)
        def _(i=i, at=at, last=last):
            pltpu.make_async_copy(
                half_ref.at[at : at + last],
                weight_hbm.at[OWNED + at : OWNED + at + last],
                sems.at[i],
            ).start()

    for i in range(PIECES):
        at = i * rows
        last = min(rows, end - at)

        @pl.when(core == 0)
        def _(i=i, at=at):
            pltpu.make_async_copy(
                half_ref.at[at : at + rows], weight_hbm.at[at : at + rows], sems.at[i]
            ).wait()

        @pl.when(core == 1)
        def _(i=i, at=at, last=last):
            pltpu.make_async_copy(
                half_ref.at[at : at + last],
                weight_hbm.at[OWNED + at : OWNED + at + last],
                sems.at[i],
            ).wait()


def final_own_kernel(own_ref, weight_hbm, half_ref, sems):
    write_half(lax.axis_index("core"), own_ref, weight_hbm, half_ref, sems)


def final_other_kernel(
    own_ref, other_ref, started_hbm, weight_hbm, gain_hbm, bias_hbm,
    half_ref, sems, gain_ref, bias_ref, small_sems,
):
    core = lax.axis_index("core")

    def put_small(ref):
        small = ref[0, CHUNK:].astype(f32)
        for m in range(1, PARTS):
            small = small + ref[m, CHUNK:].astype(f32)
        gain_ref[...] = (small[0:1] + small[2:3]) * SCALE
        bias_ref[...] = (small[1:2] + small[3:4]) * SCALE

    pl.when(core == 0)(lambda: put_small(own_ref))
    pl.when(core == 1)(lambda: put_small(other_ref))
    copies = [
        pltpu.make_async_copy(gain_ref, gain_hbm, small_sems.at[0]),
        pltpu.make_async_copy(bias_ref, bias_hbm, small_sems.at[1]),
    ]
    for copy in copies:
        copy.start()
    write_half(1 - core, other_ref, weight_hbm, half_ref, sems)
    for copy in copies:
        copy.wait()


def exchange(x, groups):
    return lax.all_to_all(x, ALL, 0, 0, axis_index_groups=groups, tiled=True)


def body(inputs, cotangent, conv_weight, norm_gain, norm_bias):
    x, cot = inputs[0], cotangent[0]
    swap = [(0, 1), (1, 0)]
    frames = (FRAMES, SIDE, SIDE, CHANNELS)
    one_row = ((1, CHANNELS), f32)

    both, mixed, stats, _, _ = call(
        load_kernel,
        [1, 1, 1, 1],
        [((2 * FRAMES, SIDE, SIDE, CHANNELS), bf16), (frames, bf16), ((8, 8, CHANNELS), f32),
         one_row, one_row],
        [pltpu.SemaphoreType.DMA((4,))],
        bytes_accessed=1 << 18,
        vmem=60,
    )(x, cot, norm_gain[None], norm_bias[None])
    stats = exchange(stats, CLIP)
    partner = lax.ppermute(both, "core", swap)
    mixed = lax.ppermute(
        mixed, CTX, [(1, 2), (3, 4), (5, 6), (2, 1), (4, 3), (6, 5)]
    )
    (norm,) = call(
        norm_kernel, [0], [((8, CHANNELS), f32)], bytes_accessed=1 << 19, flops=1 << 34
    )(stats)
    (buffer,) = call(
        taps_kernel,
        [0] * 4,
        [((OWNED, CHANNELS), bf16)],
        [
            pltpu.VMEM((OWNED, CHANNELS), bf16),
            pltpu.VMEM((3 * FRAMES, SIDE + 2, SIDE, CHANNELS), bf16),
            pltpu.VMEM((5 * SIDE * SIDE, 3 * CHANNELS), bf16),
            pltpu.SemaphoreType.DMA((6,)),
        ],
        far_outs=(0,),
        flops=4 * ROWS * 15 * CHANNELS * CHANNELS,
        bytes_accessed=1 << 20,
    )(both, partner, mixed, norm)
    parts = exchange(buffer.reshape(PARTS, CHUNK, CHANNELS), EXCHANGE)
    pre, small = call(
        data_grad_kernel,
        [0] * 4 + [1],
        [((ROWS, CHANNELS), f32), ((8, CHANNELS), f32)],
        [
            pltpu.VMEM((2 * FRAMES, SIDE + 2, SIDE, CHANNELS), bf16),
            pltpu.VMEM((ROWS, 3 * CHANNELS), f32),
            pltpu.VMEM((3, 3, 3, CHANNELS, CHANNELS), bf16),
            pltpu.SemaphoreType.DMA,
        ],
        flops=2 * ROWS * 27 * CHANNELS * CHANNELS,
        bytes_accessed=2 << 20,
    )(both, partner, mixed, norm, conv_weight)
    other_small = lax.ppermute(small, "core", swap)
    (one,) = call(sum_kernel, [0] * 3, [((8, CHUNK + 8, CHANNELS), f32)], bytes_accessed=1 << 19)(
        parts, small, other_small
    )
    spread, clip = call(
        spread_kernel,
        [0],
        [((PARTS, CHUNK + 8, CHANNELS), bf16), ((8, CHANNELS), f32)],
        [pltpu.VMEM((4, CHUNK + 8, CHANNELS), bf16), pltpu.SemaphoreType.DMA((PARTS // 4,))],
        far_outs=(0,),
        bytes_accessed=1 << 19,
    )(exchange(one, COLUMN))
    own_total = exchange(spread, EXCHANGE)
    other_clip = lax.ppermute(clip, "core", [(0, 1)])
    (input_grad,) = call(input_grad_kernel, [0] * 5, [(frames, bf16)], bytes_accessed=1 << 19)(
        both, pre, norm, clip, other_clip
    )
    own_total, input_grad = lax.optimization_barrier((own_total, input_grad))
    other_total = lax.ppermute(own_total, "core", swap)
    scratch = [pltpu.VMEM((OWNED, CHANNELS), f32), pltpu.SemaphoreType.DMA((PIECES,))]
    (started,) = call(
        final_own_kernel,
        [0],
        [((27 * CHANNELS, CHANNELS), f32)],
        scratch,
        bytes_accessed=2 << 20,
        far_outs=(0,),
    )(own_total)
    weight_grad, gain_grad, bias_grad = call(
        final_other_kernel,
        [0, 0, 1],
        [((27 * CHANNELS, CHANNELS), f32), one_row, one_row],
        scratch
        + [
            pltpu.VMEM((1, CHANNELS), f32),
            pltpu.VMEM((1, CHANNELS), f32),
            pltpu.SemaphoreType.DMA((2,)),
        ],
        bytes_accessed=2 << 20,
        far_outs=(0, 1, 2),
        aliases={2: 0},
    )(own_total, other_total, started)
    return (
        input_grad[None],
        weight_grad.reshape(3, 3, 3, CHANNELS, CHANNELS),
        gain_grad[0],
        bias_grad[0],
    )


def solution(mesh):
    fine = jax.sharding.Mesh(
        mesh.devices.reshape(8, 2, 4, 4, 2), ("z", "y_hi", "x", "y_lo", "core")
    )
    whole = P(DP, CTX, None, None, None)
    return jax.shard_map(
        body,
        mesh=fine,
        in_specs=(whole, whole, P(), P(), P()),
        out_specs=(whole, P(), P(), P()),
        check_vma=False,
    )
```

```python
import functools

import jax
import jax.numpy as jnp
from jax import lax
from jax.experimental import pallas as pl
from jax.experimental.pallas import tpu as pltpu
from jax.sharding import PartitionSpec as P

GROUPS = 32
CHANNELS = 128
SIDE = 16
FRAMES = 2
ROWS = FRAMES * SIDE * SIDE
EPSILON = 1e-06
TAPS = 14
OWNED = TAPS * CHANNELS
PARTS = 32
CHUNK = OWNED // PARTS

ALL = ("z", "y_hi", "x", "y_lo", "core")
DP = ("z", "y_hi", "x")
CTX = ("y_lo", "core")
CELLS = 64 * 8 * ROWS
MEMBERS = 8 * ROWS * (CHANNELS // GROUPS)
SCALE = CELLS**-0.5

f32 = jnp.float32
bf16 = jnp.bfloat16


def index(z, y, x, core):
    return ((z * 2 + y // 4) * 4 + x) * 8 + (y % 4) * 2 + core


LATE_FIRST = (4, 5, 6, 7, 3, 2, 1, 0)
CLIP = [[8 * d + c for c in reversed(range(8))] for d in range(64)]

EXCHANGE = [
    [index(z, y, x, 0) for z in reversed(range(8)) for x in reversed(range(4))] for y in range(8)
] + [[index(z, y, x, 1) for y in LATE_FIRST for x in reversed(range(4))] for z in range(8)]


COLUMN = [[index(z, y, x, 0) for y in LATE_FIRST] for z in range(8) for x in range(4)] + [
    [index(z, y, x, 1) for z in reversed(range(8))] for y in range(8) for x in range(4)
]


def call(
    kernel, ins, outs, scratch=(), flops=0, bytes_accessed=0, vmem=32, far_outs=(), aliases=None
):
    return pl.pallas_call(
        kernel,
        out_shape=[jax.ShapeDtypeStruct(s, d) for s, d in outs],
        in_specs=[pl.BlockSpec(memory_space=pltpu.HBM if i else pltpu.VMEM) for i in ins],
        out_specs=[
            pl.BlockSpec(memory_space=pltpu.HBM if i in far_outs else pltpu.VMEM)
            for i in range(len(outs))
        ],
        input_output_aliases=aliases or {},
        scratch_shapes=list(scratch),
        compiler_params=pltpu.CompilerParams(vmem_limit_bytes=vmem << 20),
        cost_estimate=pl.CostEstimate(
            flops=flops, bytes_accessed=bytes_accessed, transcendentals=0
        ),
    )


def column(rows):
    return lax.broadcasted_iota(jnp.int32, (rows, CHANNELS), 0) % SIDE


def next_column(x):
    return jnp.where(column(x.shape[0]) == SIDE - 1, 0.0, pltpu.roll(x, x.shape[0] - 1, 0))


def last_column(x):
    return jnp.where(column(x.shape[0]) == 0, 0.0, pltpu.roll(x, 1, 0))


def group_mean(x):
    place = lax.broadcasted_iota(jnp.int32, x.shape, 1) % (CHANNELS // GROUPS)
    total = x
    for d in range(1, CHANNELS // GROUPS):
        total = total + jnp.where(place >= d, pltpu.roll(x, d, 1), 0.0)
        total = total + jnp.where(
            place < CHANNELS // GROUPS - d, pltpu.roll(x, CHANNELS - d, 1), 0.0
        )
    return total / MEMBERS


def first_chip():
    return lax.axis_index("y_lo") == 0


def load_kernel(
    x_hbm, cot_hbm, gain_hbm, bias_hbm, both_ref, mixed_ref, stats_ref, gain_ref, bias_ref, sems
):
    copies = [
        pltpu.make_async_copy(src, dst, sems.at[i])
        for i, (src, dst) in enumerate(
            [
                (x_hbm, both_ref.at[0:FRAMES]),
                (cot_hbm, both_ref.at[FRAMES:]),
                (gain_hbm, gain_ref),
                (bias_hbm, bias_ref),
            ]
        )
    ]
    for copy in copies:
        copy.start()
    copies[0].wait()
    values = both_ref[0:FRAMES].reshape(ROWS, CHANNELS).astype(f32)
    sums = [
        jnp.sum(values, axis=0, keepdims=True),
        jnp.sum(values * values, axis=0, keepdims=True),
    ]
    for copy in copies[1:]:
        copy.wait()
    sums = jnp.concatenate(
        sums + [gain_ref[...], bias_ref[...], jnp.zeros((4, CHANNELS), f32)], axis=0
    )
    stats_ref[...] = jnp.broadcast_to(sums[None], stats_ref.shape)
    core = lax.axis_index("core")

    @pl.when(core == 0)
    def _():
        mixed_ref[...] = both_ref[FRAMES:]

    @pl.when(core == 1)
    def _():
        mixed_ref[...] = both_ref[0:FRAMES]


def norm_kernel(stats_ref, norm_ref):
    means = group_mean(jnp.sum(stats_ref[...], axis=0))
    average = means[0:1]
    spread = means[1:2] - average * average
    norm_ref[...] = jnp.concatenate(
        [average, lax.rsqrt(spread + EPSILON), stats_ref[0, 2:4], jnp.zeros((4, CHANNELS), f32)],
        axis=0,
    )


def blank_edges(pad_ref):
    blank = jnp.zeros((pad_ref.shape[0], 1, SIDE, CHANNELS), bf16)
    pad_ref[:, 0:1] = blank
    pad_ref[:, SIDE + 1 : SIDE + 2] = blank


def taps_kernel(
    both_ref, partner_ref, mixed_ref, norm_ref, out_hbm, out_ref, act_ref, wide_ref, sems
):
    core = lax.axis_index("core")
    inside = slice(1, SIDE + 1)

    def activation(x):
        values = x.reshape(-1, CHANNELS).astype(f32)
        shifted = (values - norm_ref[0:1]) * norm_ref[1:2] * norm_ref[2:3] + norm_ref[3:4]
        return (shifted / (1.0 + jnp.exp(-shifted))).astype(bf16).reshape(x.shape)

    def put_columns(cot, start):
        cot = cot.reshape(-1, CHANNELS)
        rows = pl.ds(pl.multiple_of(start, SIDE * SIDE), cot.shape[0])
        cot32 = cot.astype(f32)
        wide_ref[rows, 0:CHANNELS] = next_column(cot32).astype(bf16)
        wide_ref[rows, CHANNELS : 2 * CHANNELS] = cot
        wide_ref[rows, 2 * CHANNELS :] = last_column(cot32).astype(bf16)

    blank_edges(act_ref)
    for source, at in ((both_ref, core), (partner_ref, 1 - core)):
        act_ref[pl.ds(FRAMES + FRAMES * at, FRAMES), inside] = activation(source[0:FRAMES])
        put_columns(source[FRAMES:], at * ROWS)

    @pl.when(core == 1)
    def _():
        put_columns(mixed_ref[0:1], 2 * ROWS)

    later = jnp.logical_not(first_chip())

    @pl.when(first_chip())
    def _():
        act_ref[0:1, inside] = act_ref[FRAMES : FRAMES + 1, inside]
        act_ref[1:2, inside] = act_ref[FRAMES : FRAMES + 1, inside]

    @pl.when(later & (core == 0))
    def _():
        act_ref[0:FRAMES, inside] = activation(mixed_ref[...])

    @pl.when(later & (core == 1))
    def _():
        act_ref[0:FRAMES, inside] = jnp.zeros((FRAMES, SIDE, SIDE, CHANNELS), bf16)

    def send(j, begin):
        for own, start, stop in ((0, 3 * j, min(3 * j + 3, TAPS)), (1, max(3 * j - 2, 0), 3 * j + 1)):

            @pl.when(core == own)
            def _(start=start, stop=stop):
                rows = slice(start * CHANNELS, stop * CHANNELS)
                copy = pltpu.make_async_copy(out_ref.at[rows], out_hbm.at[rows], sems.at[j])
                copy.start() if begin else copy.wait()

    def send_blank(begin):
        @pl.when(core == 1)
        def _():
            rows = slice(OWNED - CHANNELS, OWNED)
            copy = pltpu.make_async_copy(out_ref.at[rows], out_hbm.at[rows], sems.at[5])
            copy.start() if begin else copy.wait()

    @pl.when(core == 1)
    def _():
        out_ref[OWNED - CHANNELS :] = jnp.zeros((CHANNELS, CHANNELS), bf16)

    send_blank(True)
    def product(q, frames):
        a, b = q // 3, q % 3
        x = act_ref[pl.ds(a, frames), pl.ds(b, SIDE)].reshape(frames * SIDE * SIDE, CHANNELS)
        return lax.dot_general(
            x,
            wide_ref[0 : frames * SIDE * SIDE],
            (((0,), (0,)), ((), ())),
            preferred_element_type=f32,
        ).astype(bf16)

    def put(y, slot, c):
        out_ref[pl.ds(pl.multiple_of(slot * CHANNELS, CHANNELS), CHANNELS)] = y[
            :, c * CHANNELS : (c + 1) * CHANNELS
        ]

    for j in range(5):
        if j < 2:

            @pl.when(core == 0)
            def _(j=j):
                y = product(j, 2 * FRAMES)
                for c in range(3):
                    put(y, 3 * j + c, c)

            @pl.when(core == 1)
            def _(j=j):
                y = product(4 + j, 2 * FRAMES + 1)
                for c in range(3):
                    if 3 * j + c >= 2:
                        put(y, 3 * j + c - 2, c)

        else:
            y = product(4 * core + j, 2 * FRAMES)
            for c in range(3):
                if 3 * j + c < TAPS:
                    put(y, 3 * j + c - 2 * core, c)
                else:
                    pl.when(core == 1)(lambda y=y, slot=3 * j + c - 2, c=c: put(y, slot, c))
        send(j, True)
    send_blank(False)
    for j in range(5):
        send(j, False)


def data_grad_kernel(
    both_ref, partner_ref, mixed_ref, norm_ref, weight_hbm,
    pre_ref, small_ref, pad_ref, wide_ref, weight_ref, sem,
):
    load = pltpu.make_async_copy(weight_hbm, weight_ref, sem)
    load.start()
    core = lax.axis_index("core")
    inside = slice(1, SIDE + 1)
    blank_edges(pad_ref)
    pad_ref[0:FRAMES, inside] = both_ref[FRAMES:]

    @pl.when(core == 0)
    def _():
        pad_ref[FRAMES:, inside] = partner_ref[FRAMES:]

    @pl.when(core == 1)
    def _():
        pad_ref[FRAMES:, inside] = mixed_ref[...]

    def slab(frame, count):
        return jnp.concatenate(
            [
                pad_ref[frame : frame + count, 2 - b : 2 - b + SIDE].reshape(-1, CHANNELS)
                for b in range(3)
            ],
            axis=1,
        )

    def taps(a):
        return jnp.concatenate(
            [weight_ref[a, b].reshape(3 * CHANNELS, CHANNELS) for b in range(3)], axis=1
        )

    def product(x, w):
        return lax.dot_general(x, w, (((1,), (1,)), ((), ())), preferred_element_type=f32)

    load.wait()
    wide_ref[...] = (
        product(slab(2, FRAMES), taps(0))
        + product(slab(1, FRAMES), taps(1))
        + product(slab(0, FRAMES), taps(2))
    )

    @pl.when(first_chip() & (core == 0))
    def _():
        plane = SIDE * SIDE
        wide_ref[0:plane] = wide_ref[0:plane] + (
            product(slab(0, 1), taps(0))
            + (product(slab(1, 1), taps(0)) + product(slab(0, 1), taps(1)))
        )

    act_grad = (
        next_column(wide_ref[:, 0:CHANNELS])
        + wide_ref[:, CHANNELS : 2 * CHANNELS]
        + last_column(wide_ref[:, 2 * CHANNELS :])
    )
    values = both_ref[0:FRAMES].reshape(ROWS, CHANNELS).astype(f32)
    normed = (values - norm_ref[0:1]) * norm_ref[1:2]
    shifted = normed * norm_ref[2:3] + norm_ref[3:4]
    sig = 1.0 / (1.0 + jnp.exp(-shifted))
    pre = act_grad * sig * (1.0 + shifted * (1.0 - sig))
    pre_ref[...] = pre
    small_ref[...] = jnp.concatenate(
        [
            jnp.sum(pre * normed, axis=0, keepdims=True),
            jnp.sum(pre, axis=0, keepdims=True),
            jnp.zeros((6, CHANNELS), f32),
        ],
        axis=0,
    )


def sum_kernel(parts_ref, small_ref, other_ref, out_ref):
    total = parts_ref[0].astype(f32)
    for i in range(1, PARTS):
        total = total + parts_ref[i].astype(f32)
    total = jnp.concatenate([total, small_ref[...] + other_ref[...]], axis=0)
    out_ref[...] = jnp.broadcast_to(total[None], out_ref.shape)


def spread_kernel(parts_ref, out_hbm, clip_ref, some_ref, sems):
    total = jnp.sum(parts_ref[...], axis=0)
    clip_ref[...] = jnp.sum(parts_ref[pl.ds(4 * (1 - lax.axis_index("y_hi")), 4), CHUNK:], axis=0)
    small = total[CHUNK : CHUNK + 2]
    high = small.astype(bf16).astype(f32)
    mine = jnp.concatenate(
        [total[0:CHUNK], high, small - high, jnp.zeros((4, CHANNELS), f32)], axis=0
    ).astype(bf16)
    some_ref[...] = jnp.broadcast_to(mine[None], some_ref.shape)
    copies = [
        pltpu.make_async_copy(some_ref, out_hbm.at[4 * i : 4 * i + 4], sems.at[i])
        for i in range(PARTS // 4)
    ]
    for copy in copies:
        copy.start()
    for copy in copies:
        copy.wait()


def input_grad_kernel(both_ref, pre_ref, norm_ref, clip_ref, other_ref, out_ref):
    clip = jnp.where(lax.axis_index("core") == 0, clip_ref[...], other_ref[...])
    means = group_mean(clip * norm_ref[2:3])
    values = both_ref[0:FRAMES].reshape(ROWS, CHANNELS).astype(f32)
    normed = (values - norm_ref[0:1]) * norm_ref[1:2]
    grad = norm_ref[1:2] * (pre_ref[...] * norm_ref[2:3] - means[1:2] - normed * means[0:1])
    out_ref[...] = grad.astype(bf16).reshape(out_ref.shape)


PIECES = 4


def write_half(core, total_ref, weight_hbm, half_ref, sems):
    chunks = PARTS // PIECES
    rows = chunks * CHUNK
    end = 27 * CHANNELS - OWNED
    for i in range(PIECES):
        at = i * rows
        half_ref[at : at + rows] = (
            total_ref[i * chunks : (i + 1) * chunks, 0:CHUNK].astype(f32).reshape(rows, CHANNELS)
            * SCALE
        )
        last = min(rows, end - at)

        @pl.when(core == 0)
        def _(i=i, at=at):
            pltpu.make_async_copy(
                half_ref.at[at : at + rows], weight_hbm.at[at : at + rows], sems.at[i]
            ).start()

        @pl.when(core == 1)
        def _(i=i, at=at, last=last):
            pltpu.make_async_copy(
                half_ref.at[at : at + last],
                weight_hbm.at[OWNED + at : OWNED + at + last],
                sems.at[i],
            ).start()

    for i in range(PIECES):
        at = i * rows
        last = min(rows, end - at)

        @pl.when(core == 0)
        def _(i=i, at=at):
            pltpu.make_async_copy(
                half_ref.at[at : at + rows], weight_hbm.at[at : at + rows], sems.at[i]
            ).wait()

        @pl.when(core == 1)
        def _(i=i, at=at, last=last):
            pltpu.make_async_copy(
                half_ref.at[at : at + last],
                weight_hbm.at[OWNED + at : OWNED + at + last],
                sems.at[i],
            ).wait()


def final_own_kernel(own_ref, weight_hbm, half_ref, sems):
    write_half(lax.axis_index("core"), own_ref, weight_hbm, half_ref, sems)


def final_other_kernel(
    own_ref, other_ref, started_hbm, weight_hbm, gain_hbm, bias_hbm,
    half_ref, sems, gain_ref, bias_ref, small_sems,
):
    core = lax.axis_index("core")

    def put_small(ref):
        small = ref[0, CHUNK:].astype(f32)
        for m in range(1, PARTS):
            small = small + ref[m, CHUNK:].astype(f32)
        gain_ref[...] = (small[0:1] + small[2:3]) * SCALE
        bias_ref[...] = (small[1:2] + small[3:4]) * SCALE

    pl.when(core == 0)(lambda: put_small(own_ref))
    pl.when(core == 1)(lambda: put_small(other_ref))
    copies = [
        pltpu.make_async_copy(gain_ref, gain_hbm, small_sems.at[0]),
        pltpu.make_async_copy(bias_ref, bias_hbm, small_sems.at[1]),
    ]
    for copy in copies:
        copy.start()
    write_half(1 - core, other_ref, weight_hbm, half_ref, sems)
    for copy in copies:
        copy.wait()


def exchange(x, groups):
    return lax.all_to_all(x, ALL, 0, 0, axis_index_groups=groups, tiled=True)


def body(inputs, cotangent, conv_weight, norm_gain, norm_bias):
    x, cot = inputs[0], cotangent[0]
    swap = [(0, 1), (1, 0)]
    frames = (FRAMES, SIDE, SIDE, CHANNELS)
    one_row = ((1, CHANNELS), f32)

    both, mixed, stats, _, _ = call(
        load_kernel,
        [1, 1, 1, 1],
        [((2 * FRAMES, SIDE, SIDE, CHANNELS), bf16), (frames, bf16), ((8, 8, CHANNELS), f32),
         one_row, one_row],
        [pltpu.SemaphoreType.DMA((4,))],
        bytes_accessed=1 << 18,
        vmem=60,
    )(x, cot, norm_gain[None], norm_bias[None])
    stats = exchange(stats, CLIP)
    partner = lax.ppermute(both, "core", swap)
    mixed = lax.ppermute(
        mixed, CTX, [(1, 2), (3, 4), (5, 6), (2, 1), (4, 3), (6, 5)]
    )
    (norm,) = call(
        norm_kernel, [0], [((8, CHANNELS), f32)], bytes_accessed=1 << 19, flops=1 << 34
    )(stats)
    (buffer,) = call(
        taps_kernel,
        [0] * 4,
        [((OWNED, CHANNELS), bf16)],
        [
            pltpu.VMEM((OWNED, CHANNELS), bf16),
            pltpu.VMEM((3 * FRAMES, SIDE + 2, SIDE, CHANNELS), bf16),
            pltpu.VMEM((5 * SIDE * SIDE, 3 * CHANNELS), bf16),
            pltpu.SemaphoreType.DMA((6,)),
        ],
        far_outs=(0,),
        flops=4 * ROWS * 15 * CHANNELS * CHANNELS,
        bytes_accessed=1 << 20,
    )(both, partner, mixed, norm)
    parts = exchange(buffer.reshape(PARTS, CHUNK, CHANNELS), EXCHANGE)
    pre, small = call(
        data_grad_kernel,
        [0] * 4 + [1],
        [((ROWS, CHANNELS), f32), ((8, CHANNELS), f32)],
        [
            pltpu.VMEM((2 * FRAMES, SIDE + 2, SIDE, CHANNELS), bf16),
            pltpu.VMEM((ROWS, 3 * CHANNELS), f32),
            pltpu.VMEM((3, 3, 3, CHANNELS, CHANNELS), bf16),
            pltpu.SemaphoreType.DMA,
        ],
        flops=2 * ROWS * 27 * CHANNELS * CHANNELS,
        bytes_accessed=2 << 20,
    )(both, partner, mixed, norm, conv_weight)
    other_small = lax.ppermute(small, "core", swap)
    (one,) = call(sum_kernel, [0] * 3, [((8, CHUNK + 8, CHANNELS), f32)], bytes_accessed=1 << 19)(
        parts, small, other_small
    )
    spread, clip = call(
        spread_kernel,
        [0],
        [((PARTS, CHUNK + 8, CHANNELS), bf16), ((8, CHANNELS), f32)],
        [pltpu.VMEM((4, CHUNK + 8, CHANNELS), bf16), pltpu.SemaphoreType.DMA((PARTS // 4,))],
        far_outs=(0,),
        bytes_accessed=1 << 19,
    )(exchange(one, COLUMN))
    own_total = exchange(spread, EXCHANGE)
    other_clip = lax.ppermute(clip, "core", [(0, 1)])
    (input_grad,) = call(input_grad_kernel, [0] * 5, [(frames, bf16)], bytes_accessed=1 << 19)(
        both, pre, norm, clip, other_clip
    )
    own_total, input_grad = lax.optimization_barrier((own_total, input_grad))
    other_total = lax.ppermute(own_total, "core", swap)
    scratch = [pltpu.VMEM((OWNED, CHANNELS), f32), pltpu.SemaphoreType.DMA((PIECES,))]
    (started,) = call(
        final_own_kernel,
        [0],
        [((27 * CHANNELS, CHANNELS), f32)],
        scratch,
        bytes_accessed=2 << 20,
        far_outs=(0,),
    )(own_total)
    weight_grad, gain_grad, bias_grad = call(
        final_other_kernel,
        [0, 0, 1],
        [((27 * CHANNELS, CHANNELS), f32), one_row, one_row],
        scratch
        + [
            pltpu.VMEM((1, CHANNELS), f32),
            pltpu.VMEM((1, CHANNELS), f32),
            pltpu.SemaphoreType.DMA((2,)),
        ],
        bytes_accessed=2 << 20,
        far_outs=(0, 1, 2),
        aliases={2: 0},
    )(own_total, other_total, started)
    return (
        input_grad[None],
        weight_grad.reshape(3, 3, 3, CHANNELS, CHANNELS),
        gain_grad[0],
        bias_grad[0],
    )


def solution(mesh):
    fine = jax.sharding.Mesh(
        mesh.devices.reshape(8, 2, 4, 4, 2), ("z", "y_hi", "x", "y_lo", "core")
    )
    whole = P(DP, CTX, None, None, None)
    return jax.shard_map(
        body,
        mesh=fine,
        in_specs=(whole, whole, P(), P(), P()),
        out_specs=(whole, P(), P(), P()),
        check_vma=False,
    )
```

```python
import functools

import jax
import jax.numpy as jnp
from jax import lax
from jax.experimental import pallas as pl
from jax.experimental.pallas import tpu as pltpu
from jax.sharding import PartitionSpec as P

GROUPS = 32
CHANNELS = 128
SIDE = 16
FRAMES = 2
ROWS = FRAMES * SIDE * SIDE
EPSILON = 1e-06
TAPS = 14
OWNED = TAPS * CHANNELS
PARTS = 32
CHUNK = OWNED // PARTS

ALL = ("z", "y_hi", "x", "y_lo", "core")
DP = ("z", "y_hi", "x")
CTX = ("y_lo", "core")
CELLS = 64 * 8 * ROWS
MEMBERS = 8 * ROWS * (CHANNELS // GROUPS)
SCALE = CELLS**-0.5

f32 = jnp.float32
bf16 = jnp.bfloat16


def index(z, y, x, core):
    return ((z * 2 + y // 4) * 4 + x) * 8 + (y % 4) * 2 + core


LATE_FIRST = (4, 5, 6, 7, 3, 2, 1, 0)
CLIP = [
    [8 * d + 2 * y + core for y in (range(4) if d // 4 % 2 else reversed(range(4))) for core in range(2)]
    for d in range(64)
]

EXCHANGE = [
    [index(z, y, x, 0) for z in reversed(range(8)) for x in reversed(range(4))] for y in range(8)
] + [[index(z, y, x, 1) for y in LATE_FIRST for x in reversed(range(4))] for z in range(8)]


COLUMN = [[index(z, y, x, 0) for y in LATE_FIRST] for z in range(8) for x in range(4)] + [
    [index(z, y, x, 1) for z in reversed(range(8))] for y in range(8) for x in range(4)
]


def call(
    kernel, ins, outs, scratch=(), flops=0, bytes_accessed=0, vmem=32, far_outs=(), aliases=None
):
    return pl.pallas_call(
        kernel,
        out_shape=[jax.ShapeDtypeStruct(s, d) for s, d in outs],
        in_specs=[pl.BlockSpec(memory_space=pltpu.HBM if i else pltpu.VMEM) for i in ins],
        out_specs=[
            pl.BlockSpec(memory_space=pltpu.HBM if i in far_outs else pltpu.VMEM)
            for i in range(len(outs))
        ],
        input_output_aliases=aliases or {},
        scratch_shapes=list(scratch),
        compiler_params=pltpu.CompilerParams(vmem_limit_bytes=vmem << 20),
        cost_estimate=pl.CostEstimate(
            flops=flops, bytes_accessed=bytes_accessed, transcendentals=0
        ),
    )


def column(rows):
    return lax.broadcasted_iota(jnp.int32, (rows, CHANNELS), 0) % SIDE


def next_column(x):
    return jnp.where(column(x.shape[0]) == SIDE - 1, 0.0, pltpu.roll(x, x.shape[0] - 1, 0))


def last_column(x):
    return jnp.where(column(x.shape[0]) == 0, 0.0, pltpu.roll(x, 1, 0))


def group_mean(x):
    place = lax.broadcasted_iota(jnp.int32, x.shape, 1) % (CHANNELS // GROUPS)
    total = x
    for d in range(1, CHANNELS // GROUPS):
        total = total + jnp.where(place >= d, pltpu.roll(x, d, 1), 0.0)
        total = total + jnp.where(
            place < CHANNELS // GROUPS - d, pltpu.roll(x, CHANNELS - d, 1), 0.0
        )
    return total / MEMBERS


def first_chip():
    return lax.axis_index("y_lo") == 0


def load_kernel(
    x_hbm, cot_hbm, gain_hbm, bias_hbm, both_ref, mixed_ref, stats_ref, gain_ref, bias_ref, sems
):
    copies = [
        pltpu.make_async_copy(src, dst, sems.at[i])
        for i, (src, dst) in enumerate(
            [
                (x_hbm, both_ref.at[0:FRAMES]),
                (cot_hbm, both_ref.at[FRAMES:]),
                (gain_hbm, gain_ref),
                (bias_hbm, bias_ref),
            ]
        )
    ]
    for copy in copies:
        copy.start()
    copies[0].wait()
    values = both_ref[0:FRAMES].reshape(ROWS, CHANNELS).astype(f32)
    sums = [
        jnp.sum(values, axis=0, keepdims=True),
        jnp.sum(values * values, axis=0, keepdims=True),
    ]
    for copy in copies[1:]:
        copy.wait()
    sums = jnp.concatenate(
        sums + [gain_ref[...], bias_ref[...], jnp.zeros((4, CHANNELS), f32)], axis=0
    )
    stats_ref[...] = jnp.broadcast_to(sums[None], stats_ref.shape)
    core = lax.axis_index("core")

    @pl.when(core == 0)
    def _():
        mixed_ref[...] = both_ref[FRAMES:]

    @pl.when(core == 1)
    def _():
        mixed_ref[...] = both_ref[0:FRAMES]


def norm_kernel(stats_ref, norm_ref):
    means = group_mean(jnp.sum(stats_ref[...], axis=0))
    average = means[0:1]
    spread = means[1:2] - average * average
    norm_ref[...] = jnp.concatenate(
        [average, lax.rsqrt(spread + EPSILON), stats_ref[0, 2:4], jnp.zeros((4, CHANNELS), f32)],
        axis=0,
    )


def blank_edges(pad_ref):
    blank = jnp.zeros((pad_ref.shape[0], 1, SIDE, CHANNELS), bf16)
    pad_ref[:, 0:1] = blank
    pad_ref[:, SIDE + 1 : SIDE + 2] = blank


def taps_kernel(
    both_ref, partner_ref, mixed_ref, norm_ref, out_hbm, out_ref, act_ref, wide_ref, sems
):
    core = lax.axis_index("core")
    inside = slice(1, SIDE + 1)

    def activation(x):
        values = x.reshape(-1, CHANNELS).astype(f32)
        shifted = (values - norm_ref[0:1]) * norm_ref[1:2] * norm_ref[2:3] + norm_ref[3:4]
        return (shifted / (1.0 + jnp.exp(-shifted))).astype(bf16).reshape(x.shape)

    def put_columns(cot, start):
        cot = cot.reshape(-1, CHANNELS)
        rows = pl.ds(pl.multiple_of(start, SIDE * SIDE), cot.shape[0])
        cot32 = cot.astype(f32)
        wide_ref[rows, 0:CHANNELS] = next_column(cot32).astype(bf16)
        wide_ref[rows, CHANNELS : 2 * CHANNELS] = cot
        wide_ref[rows, 2 * CHANNELS :] = last_column(cot32).astype(bf16)

    blank_edges(act_ref)
    for source, at in ((both_ref, core), (partner_ref, 1 - core)):
        act_ref[pl.ds(FRAMES + FRAMES * at, FRAMES), inside] = activation(source[0:FRAMES])
        put_columns(source[FRAMES:], at * ROWS)

    @pl.when(core == 1)
    def _():
        put_columns(mixed_ref[0:1], 2 * ROWS)

    later = jnp.logical_not(first_chip())

    @pl.when(first_chip())
    def _():
        act_ref[0:1, inside] = act_ref[FRAMES : FRAMES + 1, inside]
        act_ref[1:2, inside] = act_ref[FRAMES : FRAMES + 1, inside]

    @pl.when(later & (core == 0))
    def _():
        act_ref[0:FRAMES, inside] = activation(mixed_ref[...])

    @pl.when(later & (core == 1))
    def _():
        act_ref[0:FRAMES, inside] = jnp.zeros((FRAMES, SIDE, SIDE, CHANNELS), bf16)

    def send(j, begin):
        for own, start, stop in ((0, 3 * j, min(3 * j + 3, TAPS)), (1, max(3 * j - 2, 0), 3 * j + 1)):

            @pl.when(core == own)
            def _(start=start, stop=stop):
                rows = slice(start * CHANNELS, stop * CHANNELS)
                copy = pltpu.make_async_copy(out_ref.at[rows], out_hbm.at[rows], sems.at[j])
                copy.start() if begin else copy.wait()

    def send_blank(begin):
        @pl.when(core == 1)
        def _():
            rows = slice(OWNED - CHANNELS, OWNED)
            copy = pltpu.make_async_copy(out_ref.at[rows], out_hbm.at[rows], sems.at[5])
            copy.start() if begin else copy.wait()

    @pl.when(core == 1)
    def _():
        out_ref[OWNED - CHANNELS :] = jnp.zeros((CHANNELS, CHANNELS), bf16)

    send_blank(True)
    def product(q, frames):
        a, b = q // 3, q % 3
        x = act_ref[pl.ds(a, frames), pl.ds(b, SIDE)].reshape(frames * SIDE * SIDE, CHANNELS)
        return lax.dot_general(
            x,
            wide_ref[0 : frames * SIDE * SIDE],
            (((0,), (0,)), ((), ())),
            preferred_element_type=f32,
        ).astype(bf16)

    def put(y, slot, c):
        out_ref[pl.ds(pl.multiple_of(slot * CHANNELS, CHANNELS), CHANNELS)] = y[
            :, c * CHANNELS : (c + 1) * CHANNELS
        ]

    for j in range(5):
        if j < 2:

            @pl.when(core == 0)
            def _(j=j):
                y = product(j, 2 * FRAMES)
                for c in range(3):
                    put(y, 3 * j + c, c)

            @pl.when(core == 1)
            def _(j=j):
                y = product(4 + j, 2 * FRAMES + 1)
                for c in range(3):
                    if 3 * j + c >= 2:
                        put(y, 3 * j + c - 2, c)

        else:
            y = product(4 * core + j, 2 * FRAMES)
            for c in range(3):
                if 3 * j + c < TAPS:
                    put(y, 3 * j + c - 2 * core, c)
                else:
                    pl.when(core == 1)(lambda y=y, slot=3 * j + c - 2, c=c: put(y, slot, c))
        send(j, True)
    send_blank(False)
    for j in range(5):
        send(j, False)


def data_grad_kernel(
    both_ref, partner_ref, mixed_ref, norm_ref, weight_hbm,
    pre_ref, small_ref, pad_ref, wide_ref, weight_ref, sem,
):
    load = pltpu.make_async_copy(weight_hbm, weight_ref, sem)
    load.start()
    core = lax.axis_index("core")
    inside = slice(1, SIDE + 1)
    blank_edges(pad_ref)
    pad_ref[0:FRAMES, inside] = both_ref[FRAMES:]

    @pl.when(core == 0)
    def _():
        pad_ref[FRAMES:, inside] = partner_ref[FRAMES:]

    @pl.when(core == 1)
    def _():
        pad_ref[FRAMES:, inside] = mixed_ref[...]

    def slab(frame, count):
        return jnp.concatenate(
            [
                pad_ref[frame : frame + count, 2 - b : 2 - b + SIDE].reshape(-1, CHANNELS)
                for b in range(3)
            ],
            axis=1,
        )

    def taps(a):
        return jnp.concatenate(
            [weight_ref[a, b].reshape(3 * CHANNELS, CHANNELS) for b in range(3)], axis=1
        )

    def product(x, w):
        return lax.dot_general(x, w, (((1,), (1,)), ((), ())), preferred_element_type=f32)

    load.wait()
    wide_ref[...] = (
        product(slab(2, FRAMES), taps(0))
        + product(slab(1, FRAMES), taps(1))
        + product(slab(0, FRAMES), taps(2))
    )

    @pl.when(first_chip() & (core == 0))
    def _():
        plane = SIDE * SIDE
        wide_ref[0:plane] = wide_ref[0:plane] + (
            product(slab(0, 1), taps(0))
            + (product(slab(1, 1), taps(0)) + product(slab(0, 1), taps(1)))
        )

    act_grad = (
        next_column(wide_ref[:, 0:CHANNELS])
        + wide_ref[:, CHANNELS : 2 * CHANNELS]
        + last_column(wide_ref[:, 2 * CHANNELS :])
    )
    values = both_ref[0:FRAMES].reshape(ROWS, CHANNELS).astype(f32)
    normed = (values - norm_ref[0:1]) * norm_ref[1:2]
    shifted = normed * norm_ref[2:3] + norm_ref[3:4]
    sig = 1.0 / (1.0 + jnp.exp(-shifted))
    pre = act_grad * sig * (1.0 + shifted * (1.0 - sig))
    pre_ref[...] = pre
    small_ref[...] = jnp.concatenate(
        [
            jnp.sum(pre * normed, axis=0, keepdims=True),
            jnp.sum(pre, axis=0, keepdims=True),
            jnp.zeros((6, CHANNELS), f32),
        ],
        axis=0,
    )


def sum_kernel(parts_ref, small_ref, other_ref, out_ref):
    total = parts_ref[0].astype(f32)
    for i in range(1, PARTS):
        total = total + parts_ref[i].astype(f32)
    total = jnp.concatenate([total, small_ref[...] + other_ref[...]], axis=0)
    out_ref[...] = jnp.broadcast_to(total[None], out_ref.shape)


def spread_kernel(parts_ref, out_hbm, clip_ref, some_ref, sems):
    total = jnp.sum(parts_ref[...], axis=0)
    clip_ref[...] = jnp.sum(parts_ref[pl.ds(4 * (1 - lax.axis_index("y_hi")), 4), CHUNK:], axis=0)
    small = total[CHUNK : CHUNK + 2]
    high = small.astype(bf16).astype(f32)
    mine = jnp.concatenate(
        [total[0:CHUNK], high, small - high, jnp.zeros((4, CHANNELS), f32)], axis=0
    ).astype(bf16)
    some_ref[...] = jnp.broadcast_to(mine[None], some_ref.shape)
    copies = [
        pltpu.make_async_copy(some_ref, out_hbm.at[4 * i : 4 * i + 4], sems.at[i])
        for i in range(PARTS // 4)
    ]
    for copy in copies:
        copy.start()
    for copy in copies:
        copy.wait()


def input_grad_kernel(both_ref, pre_ref, norm_ref, clip_ref, other_ref, out_ref):
    clip = jnp.where(lax.axis_index("core") == 0, clip_ref[...], other_ref[...])
    means = group_mean(clip * norm_ref[2:3])
    values = both_ref[0:FRAMES].reshape(ROWS, CHANNELS).astype(f32)
    normed = (values - norm_ref[0:1]) * norm_ref[1:2]
    grad = norm_ref[1:2] * (pre_ref[...] * norm_ref[2:3] - means[1:2] - normed * means[0:1])
    out_ref[...] = grad.astype(bf16).reshape(out_ref.shape)


PIECES = 4


def write_half(core, total_ref, weight_hbm, half_ref, sems):
    chunks = PARTS // PIECES
    rows = chunks * CHUNK
    end = 27 * CHANNELS - OWNED
    for i in range(PIECES):
        at = i * rows
        half_ref[at : at + rows] = (
            total_ref[i * chunks : (i + 1) * chunks, 0:CHUNK].astype(f32).reshape(rows, CHANNELS)
            * SCALE
        )
        last = min(rows, end - at)

        @pl.when(core == 0)
        def _(i=i, at=at):
            pltpu.make_async_copy(
                half_ref.at[at : at + rows], weight_hbm.at[at : at + rows], sems.at[i]
            ).start()

        @pl.when(core == 1)
        def _(i=i, at=at, last=last):
            pltpu.make_async_copy(
                half_ref.at[at : at + last],
                weight_hbm.at[OWNED + at : OWNED + at + last],
                sems.at[i],
            ).start()

    for i in range(PIECES):
        at = i * rows
        last = min(rows, end - at)

        @pl.when(core == 0)
        def _(i=i, at=at):
            pltpu.make_async_copy(
                half_ref.at[at : at + rows], weight_hbm.at[at : at + rows], sems.at[i]
            ).wait()

        @pl.when(core == 1)
        def _(i=i, at=at, last=last):
            pltpu.make_async_copy(
                half_ref.at[at : at + last],
                weight_hbm.at[OWNED + at : OWNED + at + last],
                sems.at[i],
            ).wait()


def final_own_kernel(own_ref, weight_hbm, half_ref, sems):
    write_half(lax.axis_index("core"), own_ref, weight_hbm, half_ref, sems)


def final_other_kernel(
    own_ref, other_ref, started_hbm, weight_hbm, gain_hbm, bias_hbm,
    half_ref, sems, gain_ref, bias_ref, small_sems,
):
    core = lax.axis_index("core")

    def put_small(ref):
        small = ref[0, CHUNK:].astype(f32)
        for m in range(1, PARTS):
            small = small + ref[m, CHUNK:].astype(f32)
        gain_ref[...] = (small[0:1] + small[2:3]) * SCALE
        bias_ref[...] = (small[1:2] + small[3:4]) * SCALE

    pl.when(core == 0)(lambda: put_small(own_ref))
    pl.when(core == 1)(lambda: put_small(other_ref))
    copies = [
        pltpu.make_async_copy(gain_ref, gain_hbm, small_sems.at[0]),
        pltpu.make_async_copy(bias_ref, bias_hbm, small_sems.at[1]),
    ]
    for copy in copies:
        copy.start()
    write_half(1 - core, other_ref, weight_hbm, half_ref, sems)
    for copy in copies:
        copy.wait()


def exchange(x, groups):
    return lax.all_to_all(x, ALL, 0, 0, axis_index_groups=groups, tiled=True)


def body(inputs, cotangent, conv_weight, norm_gain, norm_bias):
    x, cot = inputs[0], cotangent[0]
    swap = [(0, 1), (1, 0)]
    frames = (FRAMES, SIDE, SIDE, CHANNELS)
    one_row = ((1, CHANNELS), f32)

    both, mixed, stats, _, _ = call(
        load_kernel,
        [1, 1, 1, 1],
        [((2 * FRAMES, SIDE, SIDE, CHANNELS), bf16), (frames, bf16), ((8, 8, CHANNELS), f32),
         one_row, one_row],
        [pltpu.SemaphoreType.DMA((4,))],
        bytes_accessed=1 << 18,
        vmem=60,
    )(x, cot, norm_gain[None], norm_bias[None])
    stats = exchange(stats, CLIP)
    partner = lax.ppermute(both, "core", swap)
    mixed = lax.ppermute(
        mixed, CTX, [(1, 2), (3, 4), (5, 6), (2, 1), (4, 3), (6, 5)]
    )
    (norm,) = call(
        norm_kernel, [0], [((8, CHANNELS), f32)], bytes_accessed=1 << 19, flops=1 << 34
    )(stats)
    (buffer,) = call(
        taps_kernel,
        [0] * 4,
        [((OWNED, CHANNELS), bf16)],
        [
            pltpu.VMEM((OWNED, CHANNELS), bf16),
            pltpu.VMEM((3 * FRAMES, SIDE + 2, SIDE, CHANNELS), bf16),
            pltpu.VMEM((5 * SIDE * SIDE, 3 * CHANNELS), bf16),
            pltpu.SemaphoreType.DMA((6,)),
        ],
        far_outs=(0,),
        flops=4 * ROWS * 15 * CHANNELS * CHANNELS,
        bytes_accessed=1 << 20,
    )(both, partner, mixed, norm)
    parts = exchange(buffer.reshape(PARTS, CHUNK, CHANNELS), EXCHANGE)
    pre, small = call(
        data_grad_kernel,
        [0] * 4 + [1],
        [((ROWS, CHANNELS), f32), ((8, CHANNELS), f32)],
        [
            pltpu.VMEM((2 * FRAMES, SIDE + 2, SIDE, CHANNELS), bf16),
            pltpu.VMEM((ROWS, 3 * CHANNELS), f32),
            pltpu.VMEM((3, 3, 3, CHANNELS, CHANNELS), bf16),
            pltpu.SemaphoreType.DMA,
        ],
        flops=2 * ROWS * 27 * CHANNELS * CHANNELS,
        bytes_accessed=2 << 20,
    )(both, partner, mixed, norm, conv_weight)
    other_small = lax.ppermute(small, "core", swap)
    (one,) = call(sum_kernel, [0] * 3, [((8, CHUNK + 8, CHANNELS), f32)], bytes_accessed=1 << 19)(
        parts, small, other_small
    )
    spread, clip = call(
        spread_kernel,
        [0],
        [((PARTS, CHUNK + 8, CHANNELS), bf16), ((8, CHANNELS), f32)],
        [pltpu.VMEM((4, CHUNK + 8, CHANNELS), bf16), pltpu.SemaphoreType.DMA((PARTS // 4,))],
        far_outs=(0,),
        bytes_accessed=1 << 19,
    )(exchange(one, COLUMN))
    own_total = exchange(spread, EXCHANGE)
    other_clip = lax.ppermute(clip, "core", [(0, 1)])
    (input_grad,) = call(input_grad_kernel, [0] * 5, [(frames, bf16)], bytes_accessed=1 << 19)(
        both, pre, norm, clip, other_clip
    )
    own_total, input_grad = lax.optimization_barrier((own_total, input_grad))
    other_total = lax.ppermute(own_total, "core", swap)
    scratch = [pltpu.VMEM((OWNED, CHANNELS), f32), pltpu.SemaphoreType.DMA((PIECES,))]
    (started,) = call(
        final_own_kernel,
        [0],
        [((27 * CHANNELS, CHANNELS), f32)],
        scratch,
        bytes_accessed=2 << 20,
        far_outs=(0,),
    )(own_total)
    weight_grad, gain_grad, bias_grad = call(
        final_other_kernel,
        [0, 0, 1],
        [((27 * CHANNELS, CHANNELS), f32), one_row, one_row],
        scratch
        + [
            pltpu.VMEM((1, CHANNELS), f32),
            pltpu.VMEM((1, CHANNELS), f32),
            pltpu.SemaphoreType.DMA((2,)),
        ],
        bytes_accessed=2 << 20,
        far_outs=(0, 1, 2),
        aliases={2: 0},
    )(own_total, other_total, started)
    return (
        input_grad[None],
        weight_grad.reshape(3, 3, 3, CHANNELS, CHANNELS),
        gain_grad[0],
        bias_grad[0],
    )


def solution(mesh):
    fine = jax.sharding.Mesh(
        mesh.devices.reshape(8, 2, 4, 4, 2), ("z", "y_hi", "x", "y_lo", "core")
    )
    whole = P(DP, CTX, None, None, None)
    return jax.shard_map(
        body,
        mesh=fine,
        in_specs=(whole, whole, P(), P(), P()),
        out_specs=(whole, P(), P(), P()),
        check_vma=False,
    )
```
